32 devices in a mesh: grp: 4 (over y, x), mem: 8 (over z, core).
Axes of the slice: x: 2, y: 2, z: 4, core: 2. Of those that a mesh axis runs over, the one named last changes fastest.
Arguments:
- factors: bfloat16 [32, 512, 2048], P(('grp', 'mem')), may hold values from -1 to 1
- occ_energy: bfloat16 [32], P(('grp', 'mem')), may hold values from -1.5 to -0.29882812
- vir_energy: bfloat16 [512], replicated, may hold values from 0.3984375 to 3
- pair_code: int32 [4, 8, 3], P('grp'), may hold values from 0 to 2
- pair_count: int32 [4, 8], P('grp'), may hold values from 1 to 3
Outputs:
- aux_density: bfloat16 [32, 512, 2048], P(('grp', 'mem'))
- lagrangian: bfloat16 [32, 512, 2048], P(('grp', 'mem'))
The draws below stay inside these ranges and needn't reach their ends.
Inputs may be any that keep to these rules, and one draw needn't show every extreme that they name: `pair_code`: only the first pair_count entries of a device's list are read; entries may repeat.
All inputs are finite; a program needn't handle non-finite values.
Results may differ from the reference program's by a relative error of at most 0.0056.
Values may be sent and summed in bfloat16 or wider, within the bound.
No kernel may reach another device: no remote copies, remote signals or barrier semaphores. Data moves between devices by JAX's collectives and lax.ppermute only.
A program may use at most 128 MiB of HBM per device.

```python
import jax
import jax.numpy as jnp
from jax import lax

V = 512
A = 2048
OCC_DEV = 1
SLOTS = 3
ROUNDS = 2
OCC = 32
N_GRP = 4
N_MEM = 8


def draw_factors(key, part):
    unit_scale = A ** (-0.25)
    own_part = jax.random.normal(key, (OCC, V, A), jnp.float32)
    values_all = own_part
    return jnp.clip(values_all * unit_scale, -1.0, 1.0).astype(jnp.bfloat16)


def plant(drawn, stream_key, smallest, largest):
    longest = drawn.shape.index(max(drawn.shape))
    spots = []
    for shift in (0, 1):
        where = [jax.random.randint(jax.random.fold_in(stream_key, axis), (), 0, length) for axis, length in enumerate(drawn.shape)]
        where[longest] = (where[longest] + shift) % drawn.shape[longest]
        spots.append(tuple(where))
    return drawn.at[spots[0]].set(smallest).at[spots[1]].set(largest)


def block_levels(rng, shape, cuts, least, top_value):
    def one(dim, shards_of):
        steps = jax.random.uniform(jax.random.fold_in(jax.random.fold_in(rng, 6), dim), (shards_of,), jnp.float32, least / len(cuts), top_value / len(cuts))
        return jnp.repeat(jnp.exp(steps), shape[dim] // shards_of).reshape((-1,) + (1,) * (len(shape) - dim - 1))

    factor_of = one(*cuts[0])
    for cut in cuts[1:]:
        factor_of = factor_of * one(*cut)
    return factor_of


def setup_inputs(seed: int = 0) -> dict:
    key_of = jax.random.split(jax.random.key(seed), 6)
    return {
        "factors": draw_factors(jax.random.fold_in(key_of[5], 71), 0),
        "occ_energy": jnp.clip(-1.5 + 1.2011719 * jax.random.uniform(key_of[1], (OCC,), jnp.float32) ** block_levels(key_of[1], (OCC,), ((0, 32),), -0.2, 0.2), -1.5, -0.29882812).astype(jnp.bfloat16),
        "vir_energy": jnp.clip(jax.random.uniform(key_of[2], (V,), jnp.float32, 0.3984375, 3.0), 0.3984375, 3.0).astype(jnp.bfloat16),
        "pair_code": plant(jax.random.randint(key_of[3], (N_GRP, N_MEM, SLOTS), 0, (ROUNDS + 1) * OCC_DEV * OCC_DEV), jax.random.fold_in(key_of[3], 1), 0, ((ROUNDS + 1) * OCC_DEV * OCC_DEV) - 1).astype(jnp.int32),
        "pair_count": plant(jax.random.randint(key_of[4], (N_GRP, N_MEM), 1, SLOTS + 1), jax.random.fold_in(key_of[4], 1), 1, SLOTS).astype(jnp.int32),
    }


def decode_pair(code):
    round_no = code // (OCC_DEV * OCC_DEV)
    left_orb = (code // OCC_DEV) % OCC_DEV
    right_orb = code % OCC_DEV
    return round_no, left_orb, right_orb


def add_at(target, indices, contribution):
    zero_index = jnp.zeros((), jnp.int32)
    anchor = tuple(indices) + (zero_index,) * contribution.ndim
    extent = (1,) * len(indices) + contribution.shape
    current = lax.dynamic_slice(target, anchor, extent)
    return lax.dynamic_update_slice(target, current + contribution.reshape(extent), anchor)


def reference(factors, occ_energy, vir_energy, pair_code, pair_count):
    virtual = vir_energy.astype(jnp.float32)
    group_span = N_MEM * OCC_DEV

    def group_work(group_no):
        group_factors = lax.dynamic_slice_in_dim(factors, group_no * group_span, group_span, 0).reshape(N_MEM, OCC_DEV, V, A)
        group_energy = lax.dynamic_slice_in_dim(occ_energy, group_no * group_span, group_span, 0).reshape(N_MEM, OCC_DEV).astype(jnp.float32)
        group_codes = lax.dynamic_index_in_dim(pair_code, group_no, 0, keepdims=False)
        group_counts = lax.dynamic_index_in_dim(pair_count, group_no, 0, keepdims=False)

        def device_work(carry_in, member):
            def pair_step(slot_no, carry_pair):
                density, gamma_all = carry_pair
                round_no, left_orb, right_orb = decode_pair(group_codes[member, slot_no])
                shift_bits = jnp.left_shift(jnp.int32(1), jnp.maximum(round_no - 1, 0))
                partner = jnp.where(round_no == 0, member, jnp.bitwise_xor(member, shift_bits)).astype(jnp.int32)
                left_block = group_factors[member, left_orb]
                right_block = group_factors[partner, right_orb]
                integrals = lax.dot_general(left_block, right_block, (((1,), (1,)), ((), ())), preferred_element_type=jnp.float32)
                denominator = virtual[:, None] + virtual[None, :] - group_energy[member, left_orb] - group_energy[partner, right_orb]
                amp_tile = (integrals / denominator).astype(jnp.bfloat16)
                density = density + lax.dot_general(amp_tile, amp_tile, (((1,), (1,)), ((), ())), preferred_element_type=jnp.float32)
                near_term = jnp.dot(amp_tile, right_block, preferred_element_type=jnp.float32)
                far_term = lax.dot_general(amp_tile, left_block, (((0,), (0,)), ((), ())), preferred_element_type=jnp.float32)
                gamma_all = add_at(gamma_all, (member, left_orb), near_term)
                gamma_all = add_at(gamma_all, (partner, right_orb), far_term)
                return density, gamma_all

            return lax.fori_loop(0, group_counts[member], pair_step, carry_in), None

        initial = (jnp.zeros((V, V), jnp.float32), jnp.zeros((N_MEM, OCC_DEV, V, A), jnp.float32))
        (density, gamma_all), _ = lax.scan(device_work, initial, jnp.arange(N_MEM, dtype=jnp.int32))
        return density, gamma_all.astype(jnp.bfloat16).reshape(group_span, V, A)

    densities, gammas = lax.map(group_work, jnp.arange(N_GRP, dtype=jnp.int32))
    density = jnp.sum(densities, axis=0)
    density_tile = (density * (1.0 / (8.0 * N_GRP * N_MEM))).astype(jnp.bfloat16)
    aux_density = gammas.reshape(OCC, V, A)

    def apply_density(block):
        product = lax.dot_general(density_tile, block, (((1,), (1,)), ((), ())), preferred_element_type=jnp.float32)
        return jnp.transpose(product, (1, 0, 2)).astype(jnp.bfloat16)

    lagrangian = lax.map(apply_density, factors.reshape(N_GRP, group_span, V, A)).reshape(OCC, V, A)
    return aux_density, lagrangian
```

```python
import functools

import jax
import jax.numpy as jnp
from jax import lax
from jax.experimental import pallas as pl
from jax.experimental.pallas import tpu as pltpu
from jax.sharding import PartitionSpec as P

CHUNKS = 4
TILE = 128
F32 = jnp.float32
BF16 = jnp.bfloat16

VMEM = pl.BlockSpec(memory_space=pltpu.VMEM)
SMEM = pl.BlockSpec(memory_space=pltpu.SMEM)


def leads(member):
    return (member & 1) == ((member >> 1) & 1)


def first_round(member):
    return jnp.where(leads(member), 2, 1)


def turn(value, back):
    pairs = []
    for member in range(lax.axis_size("mem")):
        target = member ^ (1 if leads(member) else 2)
        pairs.append((target, member) if back else (member, target))
    return lax.ppermute(value, "mem", pairs)


def swap(value, grp_mask, mem_mask):
    groups, members = lax.axis_size("grp"), lax.axis_size("mem")
    pairs = []
    for g in range(groups):
        for m in range(members):
            mask = grp_mask(m) if callable(grp_mask) else grp_mask
            pairs.append((g * members + m, (g ^ mask) * members + (m ^ mem_mask)))
    return lax.ppermute(value, ("grp", "mem"), pairs)


def live(codes, counts, member, round_no):
    total = jnp.int32(0)
    for slot in range(codes.shape[2]):
        hit = (slot < counts[0, member]) & (codes[0, member, slot] == round_no)
        total = total + hit.astype(jnp.int32)
    return total


def weights(codes, counts, round_no):
    me = lax.axis_index("mem")
    other = jnp.where(round_no == 0, me, me ^ round_no)
    own = live(codes, counts, me, round_no)
    far = live(codes, counts, other, round_no)
    return own.astype(F32), far.astype(F32)


def nt(a, b):
    return lax.dot_general(a, b, (((1,), (1,)), ((), ())), preferred_element_type=F32)


def nn(a, b):
    return jnp.dot(a, b, preferred_element_type=F32)


def early_kernel(b_ref, row_ref, e_ref, codes, counts, base_ref, dens_ref, gamma_ref, amp):
    vir = b_ref.shape[0]
    row = row_ref[...]
    col = jnp.broadcast_to(row, (vir, vir)).T
    base_ref[...] = col + row
    own, _ = weights(codes, counts, 0)
    energy = e_ref[0]
    width = vir // CHUNKS
    for c in range(CHUNKS):
        at = pl.ds(c * width, width)
        k = nt(b_ref[...], b_ref[at, :])
        amp[:, at] = (k / (base_ref[:, at] - energy - energy)).astype(BF16)
    a = amp[...]
    dens_ref[...] = own * nn(a, a)
    for c in range(CHUNKS):
        wide = b_ref.shape[1] // CHUNKS
        at = pl.ds(c * wide, wide)
        gamma_ref[:, at] = (2.0 * own) * nn(a, b_ref[:, at])


def amp_part(b_ref, r_ref, base_ref, e_ref, far_ref, at):
    k = nt(b_ref[...], r_ref[...])
    return (k / (base_ref[:, at] - e_ref[0] - far_ref[0])).astype(BF16)


def part_kernel(part, b_ref, r_ref, base_ref, e_ref, far_ref, mt_ref, m_ref):
    width = r_ref.shape[0]
    mt = amp_part(b_ref, r_ref, base_ref, e_ref, far_ref, pl.ds(part * width, width))
    mt_ref[...] = mt
    m_ref[...] = mt.T


def blocks(size):
    count = size // TILE
    return [(i, j) for i in range(count) for j in range(i, count)]


def density_kernel(*refs):
    (b_ref, r_ref, base_ref, e_ref, far_ref, codes, counts, dens_ref), rest = refs[:8], refs[8:]
    old, (mt_ref, m_ref, keep_ref, send_ref, mt_all, m_all, packed) = rest[:-7], rest[-7:]
    width = r_ref.shape[0]
    vir = b_ref.shape[0]
    last = CHUNKS - 1
    at = pl.ds(last * width, width)
    mt = amp_part(b_ref, r_ref, base_ref, e_ref, far_ref, at)
    m = mt.T
    mt_ref[...] = mt
    m_ref[...] = m
    for c in range(last):
        mt_all[:, pl.ds(c * width, width)] = old[2 * c][...]
        m_all[pl.ds(c * width, width), :] = old[2 * c + 1][...]
    mt_all[:, at] = mt
    m_all[at, :] = m
    me = lax.axis_index("mem")
    own, far = weights(codes, counts, first_round(me))
    total = dens_ref[...] + own * nn(mt_all[...], m_all[...]) + far * nn(m_all[...], mt_all[...])
    for n, (i, j) in enumerate(blocks(vir)):
        packed[pl.ds(n * TILE, TILE), :] = total[i * TILE : (i + 1) * TILE, j * TILE : (j + 1) * TILE]
    half = keep_ref.shape[0]
    lead = leads(me).astype(jnp.int32)
    keep_ref[...] = packed[pl.ds(pl.multiple_of((1 - lead) * half, TILE), half), :]
    send_ref[...] = packed[pl.ds(pl.multiple_of(lead * half, TILE), half), :].astype(BF16)


def first_gamma_kernel(*refs):
    codes, counts, gamma_in, rest, gamma_ref = refs[0], refs[1], refs[2], refs[3:-1], refs[-1]
    own, far = weights(codes, counts, first_round(lax.axis_index("mem")))
    weight = own + far
    wide = gamma_ref.shape[1] // CHUNKS
    for p in range(CHUNKS):
        at = pl.ds(p * wide, wide)
        total = nn(rest[0][...], rest[CHUNKS][:, at])
        for c in range(1, CHUNKS):
            total = total + nn(rest[c][...], rest[CHUNKS + c][:, at])
        gamma_ref[:, at] = gamma_in[:, at] + weight * total


def second_gamma_kernel(part, codes, counts, b_ref, r_ref, base_ref, e_ref, far_ref, gamma_in, gamma_ref):
    me = lax.axis_index("mem")
    own, far = weights(codes, counts, 3 - first_round(me))
    weight = own + far
    width = r_ref.shape[0]
    mt = amp_part(b_ref, r_ref, base_ref, e_ref, far_ref, pl.ds(part * width, width))
    wide = gamma_ref.shape[1] // CHUNKS
    for p in range(CHUNKS):
        at = pl.ds(p * wide, wide)
        total = gamma_in[:, at] + weight * nn(mt, r_ref[:, at])
        gamma_ref[:, at] = total.astype(gamma_ref.dtype)


def apply_kernel(mine_ref, other_ref, b_ref, out_ref, tile):
    vir = tile.shape[0]

    @pl.when(pl.program_id(0) == 0)
    def _():
        lead = leads(lax.axis_index("mem"))
        names = blocks(vir)
        half = len(names) // 2
        for n, (i, j) in enumerate(names):
            at = pl.ds((n % half) * TILE, TILE)
            low, high = (mine_ref, other_ref) if n < half else (other_ref, mine_ref)
            block = jnp.where(lead, low[at, :].astype(F32), high[at, :].astype(F32))
            tile[pl.ds(i * TILE, TILE), pl.ds(j * TILE, TILE)] = block.astype(BF16)
            if i != j:
                tile[pl.ds(j * TILE, TILE), pl.ds(i * TILE, TILE)] = block.T.astype(BF16)

    out_ref[...] = nn(tile[...], b_ref[...]).astype(BF16)


def call(kernel, outs, scratch=(), smem=(), count=0, flops=0, name=None):
    return pl.pallas_call(
        kernel,
        out_shape=outs,
        in_specs=[SMEM if i in smem else VMEM for i in range(count)],
        out_specs=jax.tree.map(lambda _: VMEM, outs),
        scratch_shapes=scratch,
        compiler_params=pltpu.CompilerParams(vmem_limit_bytes=40 << 20),
        cost_estimate=pl.CostEstimate(flops=flops, bytes_accessed=1 << 20, transcendentals=0),
        name=name,
    )


def per_device(factors, occ_energy, vir_energy, pair_code, pair_count):
    block = factors[0]
    vir, aux = block.shape
    width = vir // CHUNKS
    members, groups = lax.axis_size("mem"), lax.axis_size("grp")
    parts = [block[c * width : (c + 1) * width] for c in range(CHUNKS)]
    energy = occ_energy.astype(F32)
    row = vir_energy.astype(F32).reshape(1, vir)

    first = [turn(p, False) for p in parts]
    first_energy = turn(energy, False)

    shape = jax.ShapeDtypeStruct
    square = shape((vir, vir), F32)
    wide = shape((vir, aux), F32)
    dot = 2 * vir * vir * aux
    base, dens, gamma = call(
        early_kernel, (square, square, wide), [pltpu.VMEM((vir, vir), BF16)], (2, 3, 4), 5, 2 * dot, "early"
    )(block, row, energy, pair_code, pair_count)

    mts, ms = [], []
    for c in range(CHUNKS - 1):
        mt, m = call(
            functools.partial(part_kernel, c),
            (shape((vir, width), BF16), shape((width, vir), BF16)),
            (), (3, 4), 5, dot // CHUNKS, "part%d" % c,
        )(block, first[c], base, energy, first_energy)
        mts.append(mt)
        ms.append(m)
    old = [x for pair in zip(mts, ms) for x in pair]
    packed = len(blocks(vir)) * TILE
    half = packed // 2
    mt, _, keep, send = call(
        density_kernel,
        (shape((vir, width), BF16), shape((width, vir), BF16), shape((half, TILE), F32), shape((half, TILE), BF16)),
        [pltpu.VMEM((vir, vir), BF16), pltpu.VMEM((vir, vir), BF16), pltpu.VMEM((packed, TILE), F32)],
        (3, 4, 5, 6), 8 + len(old), dot // CHUNKS, "density",
    )(block, first[-1], base, energy, first_energy, pair_code, pair_count, dens, *old)
    mts.append(mt)

    total = keep + swap(send, 0, 1).astype(F32)
    total = total + swap(total.astype(BF16), 0, 3).astype(F32)
    bits = [1 << k for k in range(groups.bit_length() - 1)]
    for k, bit in enumerate(bits):
        twin = bits[k ^ 1] if (k ^ 1) < len(bits) else bit
        mask = functools.partial(lambda a, b, m: a if leads(m) else b, bit, twin)
        total = total + swap(total.astype(BF16), mask, 0).astype(F32)
    for k in range(2, members.bit_length() - 1):
        total = total + swap(total.astype(BF16), 0, (1 << k) | 3).astype(F32)
    mine = (total * (1.0 / (8.0 * groups * members))).astype(BF16)
    other = swap(mine, 0, 1)

    second = [turn(p, True) for p in parts]
    second_energy = turn(energy, True)
    gamma = call(first_gamma_kernel, wide, (), (0, 1), 3 + 2 * CHUNKS, dot, "gamma1")(
        pair_code, pair_count, gamma, *mts, *first
    )
    for c in range(CHUNKS):
        gamma = call(
            functools.partial(second_gamma_kernel, c),
            shape((vir, aux), F32 if c < CHUNKS - 1 else BF16),
            (), (0, 1, 5, 6), 8, 2 * dot // CHUNKS, "gamma2%d" % c,
        )(pair_code, pair_count, block, second[c], base, energy, second_energy, gamma)

    step = aux // CHUNKS
    lagrangian = pl.pallas_call(
        apply_kernel,
        out_shape=shape((vir, aux), BF16),
        grid=(CHUNKS,),
        in_specs=[
            pl.BlockSpec((half, TILE), lambda i: (0, 0)),
            pl.BlockSpec((half, TILE), lambda i: (0, 0)),
            pl.BlockSpec((vir, step), lambda i: (0, i)),
        ],
        out_specs=pl.BlockSpec((vir, step), lambda i: (0, i)),
        scratch_shapes=[pltpu.VMEM((vir, vir), BF16)],
        compiler_params=pltpu.CompilerParams(vmem_limit_bytes=24 << 20),
        cost_estimate=pl.CostEstimate(flops=dot, bytes_accessed=4 * vir * aux, transcendentals=0),
        name="apply",
    )(mine, other, block)
    return (gamma[None], lagrangian[None])


def solution(mesh):
    in_specs = (
        P(("grp", "mem"), None, None),
        P(("grp", "mem")),
        P(),
        P("grp", None, None),
        P("grp", None),
    )
    out_specs = (P(("grp", "mem"), None, None), P(("grp", "mem"), None, None))
    return jax.shard_map(
        per_device, mesh=mesh, in_specs=in_specs, out_specs=out_specs, check_vma=False
    )
```

```python
import jax
import jax.numpy as jnp
from jax import lax
from jax.experimental import pallas as pl
from jax.experimental.pallas import tpu as pltpu
from jax.sharding import PartitionSpec as P


STRIPS = 4
TILE = 128
F32 = jnp.float32
BF16 = jnp.bfloat16

VMEM = pl.BlockSpec(memory_space=pltpu.VMEM)
SMEM = pl.BlockSpec(memory_space=pltpu.SMEM)


def leads(member):
    return (member & 1) == ((member >> 1) & 1)


def first_round(member):
    return jnp.where(leads(member), 2, 1)


def turn(value, back):
    pairs = []
    for member in range(lax.axis_size("mem")):
        target = member ^ (1 if leads(member) else 2)
        pairs.append((target, member) if back else (member, target))
    return lax.ppermute(value, "mem", pairs)


def swap(value, masks):
    groups, members = lax.axis_size("grp"), lax.axis_size("mem")
    pairs = []
    for g in range(groups):
        for m in range(members):
            grp_mask, mem_mask = masks[0] if leads(m) else masks[1]
            pairs.append((g * members + m, (g ^ grp_mask) * members + (m ^ mem_mask)))
    return lax.ppermute(value, ("grp", "mem"), pairs)


def live(codes, counts, member, round_no):
    total = jnp.int32(0)
    for slot in range(codes.shape[2]):
        hit = (slot < counts[0, member]) & (codes[0, member, slot] == round_no)
        total = total + hit.astype(jnp.int32)
    return total


def weights(codes, counts, round_no):
    me = lax.axis_index("mem")
    other = jnp.where(round_no == 0, me, me ^ round_no)
    own = live(codes, counts, me, round_no)
    far = live(codes, counts, other, round_no)
    return own.astype(F32), far.astype(F32)


def nt(a, b):
    return lax.dot_general(a, b, (((1,), (1,)), ((), ())), preferred_element_type=F32)


def nn(a, b):
    return jnp.dot(a, b, preferred_element_type=F32)


def early_kernel(b_ref, row_ref, e_ref, codes, counts, base_ref, dens_ref, gamma_ref, amp):
    vir, aux = b_ref.shape
    row = row_ref[...]
    col = jnp.broadcast_to(row, (vir, vir)).T
    base_ref[...] = col + row
    own, _ = weights(codes, counts, 0)
    energy = e_ref[0]
    half = vir // 2
    for at in (slice(0, half), slice(half, vir)):
        k = nt(b_ref[...], b_ref[at, :])
        amp[:, at] = (k / (base_ref[:, at] - energy - energy)).astype(BF16)
    a = amp[...]
    dens_ref[...] = own * nn(a, a)
    for p in range(STRIPS):
        at = pl.ds(p * (aux // STRIPS), aux // STRIPS)
        gamma_ref[:, at] = (2.0 * own) * nn(a, b_ref[:, at])


def amp_part(at, b_ref, r_ref, base_ref, e_ref, far_ref):
    k = nt(b_ref[...], r_ref[...])
    return (k / (base_ref[:, at] - e_ref[0] - far_ref[0])).astype(BF16)


def blocks(size):
    count = size // TILE
    return [(i, j) for i in range(count) for j in range(i, count)]


def density_kernel(b_ref, r_ref, base_ref, e_ref, far_ref, codes, counts, dens_in, mt_ref, keep_ref, send_ref, m_ref):
    vir = b_ref.shape[0]
    half = vir // 2
    me = lax.axis_index("mem")
    own, far = weights(codes, counts, first_round(me))
    for at in (slice(0, half), slice(half, vir)):
        mt = amp_part(at, b_ref, r_ref.at[at, :], base_ref, e_ref, far_ref)
        mt_ref[:, at] = mt
        m_ref[at, :] = mt.T
    high, low = slice(0, half), slice(half, vir)

    def sums(rows, columns):
        one = nn(mt_ref[rows, :], m_ref[:, columns])
        two = nn(m_ref[rows, :], mt_ref[:, columns])
        return dens_in[rows, columns] + own * one + far * two

    top, rest = sums(high, slice(0, vir)), sums(low, low)
    pieces = []
    for i, j in blocks(vir):
        if i * TILE < half:
            pieces.append(top[i * TILE : (i + 1) * TILE, j * TILE : (j + 1) * TILE])
        else:
            a, b = i * TILE - half, j * TILE - half
            pieces.append(rest[a : a + TILE, b : b + TILE])
    lead = leads(me)
    count = len(pieces) // 2
    for n in range(count):
        at = pl.ds(n * TILE, TILE)
        keep_ref[at, :] = jnp.where(lead, pieces[n], pieces[n + count])
        send_ref[at, :] = jnp.where(lead, pieces[n + count], pieces[n]).astype(BF16)


def first_gamma_kernel(codes, counts, gamma_in, mt_ref, r_ref, gamma_ref):
    own, far = weights(codes, counts, first_round(lax.axis_index("mem")))
    aux = gamma_ref.shape[1]
    for p in range(STRIPS):
        at = pl.ds(p * (aux // STRIPS), aux // STRIPS)
        gamma_ref[:, at] = gamma_in[:, at] + (own + far) * nn(mt_ref[...], r_ref[:, at])


def strips_out(out_ref, held, sems, compute):
    step = held.shape[1] // STRIPS
    copies = []
    for p in range(STRIPS):
        at = pl.ds(p * step, step)
        held[:, at] = compute(at).astype(held.dtype)
        copies.append(pltpu.make_async_copy(held.at[:, at], out_ref.at[:, at], sems.at[p]))
        copies[-1].start()
    for copy in copies:
        copy.wait()


def last_gamma_kernel(
    codes, counts, b_ref, ra_ref, rb_ref, base_ref, e_ref, far_ref, gamma_in, out_ref, held, mt_ref, sems
):
    own, far = weights(codes, counts, 3 - first_round(lax.axis_index("mem")))
    vir, cut = b_ref.shape[0], ra_ref.shape[0]
    for at, r_ref in ((slice(0, cut), ra_ref), (slice(cut, vir), rb_ref)):
        mt_ref[:, at] = amp_part(at, b_ref, r_ref, base_ref, e_ref, far_ref)

    def strip(at):
        total = nn(mt_ref[:, :cut], ra_ref[:, at]) + nn(mt_ref[:, cut:], rb_ref[:, at])
        return gamma_in[:, at] + (own + far) * total

    strips_out(out_ref, held, sems, strip)


def apply_kernel(mine_ref, other_ref, b_ref, out_ref, tile, held, sems):
    lead = leads(lax.axis_index("mem"))
    names = blocks(tile.shape[0])
    half = len(names) // 2
    for n, (i, j) in enumerate(names):
        at = pl.ds((n % half) * TILE, TILE)
        low, high = (mine_ref, other_ref) if n < half else (other_ref, mine_ref)
        block = jnp.where(lead, low[at, :].astype(F32), high[at, :].astype(F32)).astype(BF16)
        tile[pl.ds(i * TILE, TILE), pl.ds(j * TILE, TILE)] = block
        if i != j:
            tile[pl.ds(j * TILE, TILE), pl.ds(i * TILE, TILE)] = block.T
    strips_out(out_ref, held, sems, lambda at: nn(tile[...], b_ref[:, at]))


def call(kernel, outs, scratch=(), smem=(), count=0, flops=0, out_spec=VMEM):
    return lambda *args: kernel_call(kernel, outs, scratch, smem, count, flops, out_spec)(*args)


def kernel_call(kernel, outs, scratch, smem, count, flops, out_spec):
    return pl.pallas_call(
        kernel,
        out_shape=outs,
        in_specs=[SMEM if i in smem else VMEM for i in range(count)],
        out_specs=jax.tree.map(lambda _: out_spec, outs),
        scratch_shapes=scratch,
        compiler_params=pltpu.CompilerParams(vmem_limit_bytes=32 << 20),
        cost_estimate=pl.CostEstimate(flops=flops, bytes_accessed=1 << 20, transcendentals=0),
    )


def per_device(factors, occ_energy, vir_energy, pair_code, pair_count):
    return body(factors[0], occ_energy, vir_energy, pair_code, pair_count)


def body(block, occ_energy, vir_energy, pair_code, pair_count):
    vir, aux = block.shape
    members, groups = lax.axis_size("mem"), lax.axis_size("grp")
    shape = jax.ShapeDtypeStruct
    square = shape((vir, vir), F32)
    wide = shape((vir, aux), F32)
    dot = 2 * vir * vir * aux
    out_scratch = [pltpu.VMEM((vir, aux), BF16), pltpu.SemaphoreType.DMA((STRIPS,))]
    any_space = pl.BlockSpec(memory_space=pl.ANY)

    first_energy = turn(occ_energy, False).astype(F32)
    first = turn(block, False)

    energy = occ_energy.astype(F32)
    row = vir_energy.astype(F32).reshape(1, vir)
    base, dens, gamma = call(
        early_kernel, (square, square, wide), [pltpu.VMEM((vir, vir), BF16)], (2, 3, 4), 5, 2 * dot
    )(block, row, energy, pair_code, pair_count)

    half = len(blocks(vir)) * TILE // 2
    mt, keep, send = call(
        density_kernel,
        (shape((vir, vir), BF16), shape((half, TILE), F32), shape((half, TILE), BF16)),
        [pltpu.VMEM((vir, vir), BF16)], (3, 4, 5, 6), 8, dot,
    )(block, first, base, energy, first_energy, pair_code, pair_count, dens)

    total = keep + swap(send, [(0, 1), (0, 1)]).astype(F32)
    near = [(0, 3)]
    along = [(0, (1 << k) | 3) for k in range(2, members.bit_length() - 1)]
    across = [(1 << k, 0) for k in range(groups.bit_length() - 1)]
    for masks in zip(near + across + along, near + along + across):
        got = swap(total.astype(BF16), masks)
        total = total + got.astype(F32)
    mine = (total * (1.0 / (8.0 * groups * members))).astype(BF16)
    other = swap(mine, [(0, 1), (0, 1)])

    second_energy = turn(occ_energy, True).astype(F32)
    cut = vir // 4
    parta, partb = block[:cut], block[cut:]
    seconda = turn(parta, True)
    secondb = turn(partb, True)
    gamma = call(first_gamma_kernel, wide, (), (0, 1), 5, dot)(
        pair_code, pair_count, gamma, mt, first
    )
    result = call(
        last_gamma_kernel, shape((vir, aux), BF16),
        [out_scratch[0], pltpu.VMEM((vir, vir), BF16), out_scratch[1]],
        (0, 1, 6, 7), 9, 2 * dot, any_space,
    )(pair_code, pair_count, block, seconda, secondb, base, energy, second_energy, gamma)
    lagrangian = call(
        apply_kernel, shape((vir, aux), BF16), [pltpu.VMEM((vir, vir), BF16), *out_scratch], (), 3, dot,
        any_space,
    )(mine, other, block)
    return (result[None], lagrangian[None])


def solution(mesh):
    in_specs = (
        P(("grp", "mem"), None, None),
        P(("grp", "mem")),
        P(),
        P("grp", None, None),
        P("grp", None),
    )
    out_specs = (P(("grp", "mem"), None, None), P(("grp", "mem"), None, None))
    return jax.shard_map(
        per_device, mesh=mesh, in_specs=in_specs, out_specs=out_specs, check_vma=False
    )
```

```python
import jax
import jax.numpy as jnp
from jax import lax
from jax.experimental import pallas as pl
from jax.experimental.pallas import tpu as pltpu
from jax.sharding import PartitionSpec as P


STRIPS = 4
TILE = 128
F32 = jnp.float32
BF16 = jnp.bfloat16

VMEM = pl.BlockSpec(memory_space=pltpu.VMEM)
SMEM = pl.BlockSpec(memory_space=pltpu.SMEM)


def leads(member):
    return (member & 1) == ((member >> 1) & 1)


def first_round(member):
    return jnp.where(leads(member), 2, 1)


def turn(value, back):
    pairs = []
    for member in range(lax.axis_size("mem")):
        target = member ^ (1 if leads(member) else 2)
        pairs.append((target, member) if back else (member, target))
    return lax.ppermute(value, "mem", pairs)


def swap(value, masks):
    groups, members = lax.axis_size("grp"), lax.axis_size("mem")
    pairs = []
    for g in range(groups):
        for m in range(members):
            grp_mask, mem_mask = masks[0] if leads(m) else masks[1]
            pairs.append((g * members + m, (g ^ grp_mask) * members + (m ^ mem_mask)))
    return lax.ppermute(value, ("grp", "mem"), pairs)


def live(codes, counts, member, round_no):
    total = jnp.int32(0)
    for slot in range(codes.shape[2]):
        hit = (slot < counts[0, member]) & (codes[0, member, slot] == round_no)
        total = total + hit.astype(jnp.int32)
    return total


def weights(codes, counts, round_no):
    me = lax.axis_index("mem")
    other = jnp.where(round_no == 0, me, me ^ round_no)
    own = live(codes, counts, me, round_no)
    far = live(codes, counts, other, round_no)
    return own.astype(F32), far.astype(F32)


def nt(a, b):
    return lax.dot_general(a, b, (((1,), (1,)), ((), ())), preferred_element_type=F32)


def nn(a, b):
    return jnp.dot(a, b, preferred_element_type=F32)


def early_kernel(b_ref, row_ref, e_ref, codes, counts, base_ref, dens_ref, gamma_ref, amp):
    vir, aux = b_ref.shape
    row = row_ref[...]
    col = jnp.broadcast_to(row, (vir, vir)).T
    base_ref[...] = col + row
    own, _ = weights(codes, counts, 0)
    energy = e_ref[0]
    half = vir // 2
    for at in (slice(0, half), slice(half, vir)):
        k = nt(b_ref[...], b_ref[at, :])
        amp[:, at] = (k / (base_ref[:, at] - energy - energy)).astype(BF16)
    a = amp[...]
    dens_ref[...] = own * nn(a, a)
    for p in range(STRIPS):
        at = pl.ds(p * (aux // STRIPS), aux // STRIPS)
        gamma_ref[:, at] = (2.0 * own) * nn(a, b_ref[:, at])


def amp_part(at, b_ref, r_ref, base_ref, e_ref, far_ref):
    k = nt(b_ref[...], r_ref[...])
    return (k / (base_ref[:, at] - e_ref[0] - far_ref[0])).astype(BF16)


def blocks(size):
    count = size // TILE
    return [(i, j) for i in range(count) for j in range(i, count)]


def density_kernel(b_ref, r_ref, base_ref, e_ref, far_ref, codes, counts, dens_in, mt_ref, keep_ref, send_ref, m_ref):
    vir = b_ref.shape[0]
    half = vir // 2
    me = lax.axis_index("mem")
    own, far = weights(codes, counts, first_round(me))
    for at in (slice(0, half), slice(half, vir)):
        mt = amp_part(at, b_ref, r_ref.at[at, :], base_ref, e_ref, far_ref)
        mt_ref[:, at] = mt
        m_ref[at, :] = mt.T
    high, low = slice(0, half), slice(half, vir)

    def sums(rows, columns):
        one = nn(mt_ref[rows, :], m_ref[:, columns])
        two = nn(m_ref[rows, :], mt_ref[:, columns])
        return dens_in[rows, columns] + own * one + far * two

    top, rest = sums(high, slice(0, vir)), sums(low, low)
    pieces = []
    for i, j in blocks(vir):
        if i * TILE < half:
            pieces.append(top[i * TILE : (i + 1) * TILE, j * TILE : (j + 1) * TILE])
        else:
            a, b = i * TILE - half, j * TILE - half
            pieces.append(rest[a : a + TILE, b : b + TILE])
    lead = leads(me)
    count = len(pieces) // 2
    for n in range(count):
        at = pl.ds(n * TILE, TILE)
        keep_ref[at, :] = jnp.where(lead, pieces[n], pieces[n + count])
        send_ref[at, :] = jnp.where(lead, pieces[n + count], pieces[n]).astype(BF16)


def first_gamma_kernel(codes, counts, gamma_in, mt_ref, r_ref, gamma_ref):
    own, far = weights(codes, counts, first_round(lax.axis_index("mem")))
    aux = gamma_ref.shape[1]
    for p in range(STRIPS):
        at = pl.ds(p * (aux // STRIPS), aux // STRIPS)
        gamma_ref[:, at] = gamma_in[:, at] + (own + far) * nn(mt_ref[...], r_ref[:, at])


def strips_out(out_ref, held, sems, compute):
    step = held.shape[1] // STRIPS
    copies = []
    for p in range(STRIPS):
        at = pl.ds(p * step, step)
        held[:, at] = compute(at).astype(held.dtype)
        copies.append(pltpu.make_async_copy(held.at[:, at], out_ref.at[:, at], sems.at[p]))
        copies[-1].start()
    for copy in copies:
        copy.wait()


def second_gamma_kernel(
    codes, counts, b_ref, ra_ref, rb_ref, base_ref, e_ref, far_ref, gamma_in, gamma_ref, mt_ref
):
    own, far = weights(codes, counts, 3 - first_round(lax.axis_index("mem")))
    cut = ra_ref.shape[0]
    end = cut + rb_ref.shape[0]
    for at, r_ref in ((slice(0, cut), ra_ref), (slice(cut, end), rb_ref)):
        mt_ref[:, at] = amp_part(at, b_ref, r_ref, base_ref, e_ref, far_ref)
    aux = gamma_ref.shape[1]
    for p in range(STRIPS):
        at = pl.ds(p * (aux // STRIPS), aux // STRIPS)
        total = nn(mt_ref[:, :cut], ra_ref[:, at]) + nn(mt_ref[:, cut:], rb_ref[:, at])
        gamma_ref[:, at] = gamma_in[:, at] + (own + far) * total


def last_gamma_kernel(
    codes, counts, b_ref, r_ref, base_ref, e_ref, far_ref, gamma_in, out_ref, held, sems
):
    own, far = weights(codes, counts, 3 - first_round(lax.axis_index("mem")))
    vir = b_ref.shape[0]
    mt = amp_part(slice(vir - r_ref.shape[0], vir), b_ref, r_ref, base_ref, e_ref, far_ref)
    strips_out(out_ref, held, sems, lambda at: gamma_in[:, at] + (own + far) * nn(mt, r_ref[:, at]))


def apply_kernel(mine_ref, other_ref, b_ref, out_ref, tile, held, sems):
    lead = leads(lax.axis_index("mem"))
    names = blocks(tile.shape[0])
    half = len(names) // 2
    for n, (i, j) in enumerate(names):
        at = pl.ds((n % half) * TILE, TILE)
        low, high = (mine_ref, other_ref) if n < half else (other_ref, mine_ref)
        block = jnp.where(lead, low[at, :].astype(F32), high[at, :].astype(F32)).astype(BF16)
        tile[pl.ds(i * TILE, TILE), pl.ds(j * TILE, TILE)] = block
        if i != j:
            tile[pl.ds(j * TILE, TILE), pl.ds(i * TILE, TILE)] = block.T
    strips_out(out_ref, held, sems, lambda at: nn(tile[...], b_ref[:, at]))


def call(kernel, outs, scratch=(), smem=(), count=0, flops=0, out_spec=VMEM):
    return lambda *args: kernel_call(kernel, outs, scratch, smem, count, flops, out_spec)(*args)


def kernel_call(kernel, outs, scratch, smem, count, flops, out_spec):
    return pl.pallas_call(
        kernel,
        out_shape=outs,
        in_specs=[SMEM if i in smem else VMEM for i in range(count)],
        out_specs=jax.tree.map(lambda _: out_spec, outs),
        scratch_shapes=scratch,
        compiler_params=pltpu.CompilerParams(vmem_limit_bytes=32 << 20),
        cost_estimate=pl.CostEstimate(flops=flops, bytes_accessed=1 << 20, transcendentals=0),
    )


def per_device(factors, occ_energy, vir_energy, pair_code, pair_count):
    return body(factors[0], occ_energy, vir_energy, pair_code, pair_count)


def body(block, occ_energy, vir_energy, pair_code, pair_count):
    vir, aux = block.shape
    members, groups = lax.axis_size("mem"), lax.axis_size("grp")
    shape = jax.ShapeDtypeStruct
    square = shape((vir, vir), F32)
    wide = shape((vir, aux), F32)
    dot = 2 * vir * vir * aux
    out_scratch = [pltpu.VMEM((vir, aux), BF16), pltpu.SemaphoreType.DMA((STRIPS,))]
    any_space = pl.BlockSpec(memory_space=pl.ANY)

    first_energy = turn(occ_energy, False).astype(F32)
    first = turn(block, False)

    energy = occ_energy.astype(F32)
    row = vir_energy.astype(F32).reshape(1, vir)
    base, dens, gamma = call(
        early_kernel, (square, square, wide), [pltpu.VMEM((vir, vir), BF16)], (2, 3, 4), 5, 2 * dot
    )(block, row, energy, pair_code, pair_count)

    half = len(blocks(vir)) * TILE // 2
    mt, keep, send = call(
        density_kernel,
        (shape((vir, vir), BF16), shape((half, TILE), F32), shape((half, TILE), BF16)),
        [pltpu.VMEM((vir, vir), BF16)], (3, 4, 5, 6), 8, dot,
    )(block, first, base, energy, first_energy, pair_code, pair_count, dens)

    total = keep + swap(send, [(0, 1), (0, 1)]).astype(F32)
    near = [(0, 3)]
    along = [(0, (1 << k) | 3) for k in range(2, members.bit_length() - 1)]
    across = [(1 << k, 0) for k in range(groups.bit_length() - 1)]
    for masks in zip(near + along + across, near + across[1:] + along + across[:1]):
        got = swap(total.astype(BF16), masks)
        total = total + got.astype(F32)
    mine = (total * (1.0 / (8.0 * groups * members))).astype(BF16)
    other = swap(mine, [(0, 1), (0, 1)])

    second_energy = turn(occ_energy, True).astype(F32)
    cuts = (0, vir // 4, vir // 2, vir)
    parts = [block[a:b] for a, b in zip(cuts, cuts[1:])]
    second = [turn(part, True) for part in parts]
    gamma = call(first_gamma_kernel, wide, (), (0, 1), 5, dot)(
        pair_code, pair_count, gamma, mt, first
    )
    gamma = call(
        second_gamma_kernel, wide, [pltpu.VMEM((vir, cuts[2]), BF16)], (0, 1, 6, 7), 9, dot
    )(pair_code, pair_count, block, second[0], second[1], base, energy, second_energy, gamma)
    result = call(
        last_gamma_kernel, shape((vir, aux), BF16), out_scratch, (0, 1, 5, 6), 8, dot, any_space
    )(pair_code, pair_count, block, second[2], base, energy, second_energy, gamma)
    lagrangian = call(
        apply_kernel, shape((vir, aux), BF16), [pltpu.VMEM((vir, vir), BF16), *out_scratch], (), 3, dot,
        any_space,
    )(mine, other, block)
    return (result[None], lagrangian[None])


def solution(mesh):
    in_specs = (
        P(("grp", "mem"), None, None),
        P(("grp", "mem")),
        P(),
        P("grp", None, None),
        P("grp", None),
    )
    out_specs = (P(("grp", "mem"), None, None), P(("grp", "mem"), None, None))
    return jax.shard_map(
        per_device, mesh=mesh, in_specs=in_specs, out_specs=out_specs, check_vma=False
    )
```

```python
import jax
import jax.numpy as jnp
from jax import lax
from jax.experimental import pallas as pl
from jax.experimental.pallas import tpu as pltpu
from jax.sharding import PartitionSpec as P


STRIPS = 4
TILE = 128
F32 = jnp.float32
BF16 = jnp.bfloat16

VMEM = pl.BlockSpec(memory_space=pltpu.VMEM)
SMEM = pl.BlockSpec(memory_space=pltpu.SMEM)


def leads(member):
    return (member & 1) == ((member >> 1) & 1)


def first_round(member):
    return jnp.where(leads(member), 2, 1)


def turn(value, back):
    pairs = []
    for member in range(lax.axis_size("mem")):
        target = member ^ (1 if leads(member) else 2)
        pairs.append((target, member) if back else (member, target))
    return lax.ppermute(value, "mem", pairs)


def swap(value, masks):
    groups, members = lax.axis_size("grp"), lax.axis_size("mem")
    pairs = []
    for g in range(groups):
        for m in range(members):
            grp_mask, mem_mask = masks[0] if leads(m) else masks[1]
            pairs.append((g * members + m, (g ^ grp_mask) * members + (m ^ mem_mask)))
    return lax.ppermute(value, ("grp", "mem"), pairs)


def live(codes, counts, member, round_no):
    total = jnp.int32(0)
    for slot in range(codes.shape[2]):
        hit = (slot < counts[0, member]) & (codes[0, member, slot] == round_no)
        total = total + hit.astype(jnp.int32)
    return total


def weights(codes, counts, round_no):
    me = lax.axis_index("mem")
    other = jnp.where(round_no == 0, me, me ^ round_no)
    own = live(codes, counts, me, round_no)
    far = live(codes, counts, other, round_no)
    return own.astype(F32), far.astype(F32)


def nt(a, b):
    return lax.dot_general(a, b, (((1,), (1,)), ((), ())), preferred_element_type=F32)


def nn(a, b):
    return jnp.dot(a, b, preferred_element_type=F32)


def early_kernel(
    b_ref, row_ref, e_ref, first_ref, second_ref, codes, counts, one_ref, two_ref, dens_ref, gamma_ref, amp
):
    vir, aux = b_ref.shape
    row = row_ref[...]
    sums = jnp.broadcast_to(row, (vir, vir)).T + row - e_ref[0]
    one_ref[...] = 1.0 / (sums - first_ref[0])
    two_ref[...] = 1.0 / (sums - second_ref[0])
    own, _ = weights(codes, counts, 0)
    half = vir // 2
    for at in (slice(0, half), slice(half, vir)):
        k = nt(b_ref[...], b_ref[at, :])
        amp[:, at] = (k / (sums[:, at] - e_ref[0])).astype(BF16)
    a = amp[...]
    dens_ref[...] = own * nn(a, a)
    for p in range(STRIPS):
        at = pl.ds(p * (aux // STRIPS), aux // STRIPS)
        gamma_ref[:, at] = (2.0 * own) * nn(a, b_ref[:, at])


def amp_part(at, b_ref, r_ref, over_ref):
    return (nt(b_ref[...], r_ref[...]) * over_ref[:, at]).astype(BF16)


def blocks(size):
    count = size // TILE
    return [(i, j) for i in range(count) for j in range(i, count)]


def density_kernel(b_ref, r_ref, over_ref, codes, counts, dens_in, mt_ref, keep_ref, send_ref, m_ref):
    vir = b_ref.shape[0]
    half = vir // 2
    me = lax.axis_index("mem")
    own, far = weights(codes, counts, first_round(me))
    for at in (slice(0, half), slice(half, vir)):
        mt = amp_part(at, b_ref, r_ref.at[at, :], over_ref)
        mt_ref[:, at] = mt
        m_ref[at, :] = mt.T
    high, low = slice(0, half), slice(half, vir)

    def sums(rows, columns):
        one = nn(mt_ref[rows, :], m_ref[:, columns])
        two = nn(m_ref[rows, :], mt_ref[:, columns])
        return dens_in[rows, columns] + own * one + far * two

    top, rest = sums(high, slice(0, vir)), sums(low, low)
    pieces = []
    for i, j in blocks(vir):
        if i * TILE < half:
            pieces.append(top[i * TILE : (i + 1) * TILE, j * TILE : (j + 1) * TILE])
        else:
            a, b = i * TILE - half, j * TILE - half
            pieces.append(rest[a : a + TILE, b : b + TILE])
    lead = leads(me)
    count = len(pieces) // 2
    for n in range(count):
        at = pl.ds(n * TILE, TILE)
        keep_ref[at, :] = jnp.where(lead, pieces[n], pieces[n + count])
        send_ref[at, :] = jnp.where(lead, pieces[n + count], pieces[n]).astype(BF16)


def first_gamma_kernel(codes, counts, gamma_in, mt_ref, r_ref, gamma_ref):
    own, far = weights(codes, counts, first_round(lax.axis_index("mem")))
    aux = gamma_ref.shape[1]
    for p in range(STRIPS):
        at = pl.ds(p * (aux // STRIPS), aux // STRIPS)
        gamma_ref[:, at] = gamma_in[:, at] + (own + far) * nn(mt_ref[...], r_ref[:, at])


def strips_out(out_ref, held, sems, strips, compute):
    step = held.shape[1] // strips
    copies = []
    for p in range(strips):
        at = pl.ds(p * step, step)
        held[:, at] = compute(at).astype(held.dtype)
        copies.append(pltpu.make_async_copy(held.at[:, at], out_ref.at[:, at], sems.at[p]))
        copies[-1].start()
    for copy in copies:
        copy.wait()


def second_gamma_kernel(codes, counts, b_ref, over_ref, gamma_in, *refs):
    parts, (gamma_ref, held) = refs[:-2], refs[-2:]
    own, far = weights(codes, counts, 3 - first_round(lax.axis_index("mem")))
    start = 0
    for part in parts:
        held[start : start + part.shape[0], :] = part[...]
        start += part.shape[0]
    mt = amp_part(slice(0, start), b_ref, held, over_ref)
    aux = gamma_ref.shape[1]
    for p in range(STRIPS):
        at = pl.ds(p * (aux // STRIPS), aux // STRIPS)
        gamma_ref[:, at] = gamma_in[:, at] + (own + far) * nn(mt, held[:, at])


def last_gamma_kernel(codes, counts, b_ref, over_ref, gamma_in, r_ref, out_ref, held, sems):
    own, far = weights(codes, counts, 3 - first_round(lax.axis_index("mem")))
    vir = b_ref.shape[0]
    mt = amp_part(slice(vir - r_ref.shape[0], vir), b_ref, r_ref, over_ref)
    strips_out(out_ref, held, sems, 2, lambda at: gamma_in[:, at] + (own + far) * nn(mt, r_ref[:, at]))


def apply_kernel(mine_ref, other_ref, b_ref, out_ref, tile, held, sems):
    lead = leads(lax.axis_index("mem"))
    names = blocks(tile.shape[0])
    half = len(names) // 2
    for n, (i, j) in enumerate(names):
        at = pl.ds((n % half) * TILE, TILE)
        low, high = (mine_ref, other_ref) if n < half else (other_ref, mine_ref)
        block = jnp.where(lead, low[at, :].astype(F32), high[at, :].astype(F32)).astype(BF16)
        tile[pl.ds(i * TILE, TILE), pl.ds(j * TILE, TILE)] = block
        if i != j:
            tile[pl.ds(j * TILE, TILE), pl.ds(i * TILE, TILE)] = block.T
    strips_out(out_ref, held, sems, STRIPS, lambda at: nn(tile[...], b_ref[:, at]))


def call(kernel, outs, scratch=(), smem=(), count=0, flops=0, out_spec=VMEM):
    return lambda *args: kernel_call(kernel, outs, scratch, smem, count, flops, out_spec)(*args)


def kernel_call(kernel, outs, scratch, smem, count, flops, out_spec):
    return pl.pallas_call(
        kernel,
        out_shape=outs,
        in_specs=[SMEM if i in smem else VMEM for i in range(count)],
        out_specs=jax.tree.map(lambda _: out_spec, outs),
        scratch_shapes=scratch,
        compiler_params=pltpu.CompilerParams(vmem_limit_bytes=32 << 20),
        cost_estimate=pl.CostEstimate(flops=flops, bytes_accessed=1 << 20, transcendentals=0),
    )


def per_device(factors, occ_energy, vir_energy, pair_code, pair_count):
    return body(factors[0], occ_energy, vir_energy, pair_code, pair_count)


def body(block, occ_energy, vir_energy, pair_code, pair_count):
    vir, aux = block.shape
    members, groups = lax.axis_size("mem"), lax.axis_size("grp")
    shape = jax.ShapeDtypeStruct
    square = shape((vir, vir), F32)
    wide = shape((vir, aux), F32)
    dot = 2 * vir * vir * aux
    out_scratch = [pltpu.VMEM((vir, aux), BF16), pltpu.SemaphoreType.DMA((STRIPS,))]
    any_space = pl.BlockSpec(memory_space=pl.ANY)

    first_energy = turn(occ_energy, False).astype(F32)
    first = turn(block, False)
    second_energy = turn(occ_energy, True).astype(F32)

    energy = occ_energy.astype(F32)
    row = vir_energy.astype(F32).reshape(1, vir)
    over_first, over_second, dens, gamma = call(
        early_kernel, (square, square, square, wide), [pltpu.VMEM((vir, vir), BF16)],
        (2, 3, 4, 5, 6), 7, 2 * dot,
    )(block, row, energy, first_energy, second_energy, pair_code, pair_count)

    half = len(blocks(vir)) * TILE // 2
    mt, keep, send = call(
        density_kernel,
        (shape((vir, vir), BF16), shape((half, TILE), F32), shape((half, TILE), BF16)),
        [pltpu.VMEM((vir, vir), BF16)], (3, 4), 6, dot,
    )(block, first, over_first, pair_code, pair_count, dens)

    total = keep + swap(send, [(0, 1), (0, 1)]).astype(F32)
    near = [(0, 3)]
    along = [(0, (1 << k) | 3) for k in range(2, members.bit_length() - 1)]
    across = [(1 << k, 0) for k in range(groups.bit_length() - 1)]
    for masks in zip(near + along + across, near + across[1:] + along + across[:1]):
        got = swap(total.astype(BF16), masks)
        total = total + got.astype(F32)
    mine = (total * (1.0 / (8.0 * groups * members))).astype(BF16)
    other = swap(mine, [(0, 1), (0, 1)])

    unit = vir // 32
    cuts = (0, 7 * unit, 13 * unit, 16 * unit, vir)
    parts = [block[a:b] for a, b in zip(cuts, cuts[1:])]
    second = [turn(part, True) for part in parts]
    gamma = call(first_gamma_kernel, wide, (), (0, 1), 5, dot)(
        pair_code, pair_count, gamma, mt, first
    )
    gamma = call(
        second_gamma_kernel, wide, [pltpu.VMEM((cuts[3], aux), BF16)], (0, 1), 8, dot
    )(pair_code, pair_count, block, over_second, gamma, *second[:3])
    result = call(
        last_gamma_kernel, shape((vir, aux), BF16), out_scratch, (0, 1), 6, dot, any_space
    )(pair_code, pair_count, block, over_second, gamma, second[3])
    lagrangian = call(
        apply_kernel, shape((vir, aux), BF16), [pltpu.VMEM((vir, vir), BF16), *out_scratch], (), 3, dot,
        any_space,
    )(mine, other, block)
    return (result[None], lagrangian[None])


def solution(mesh):
    in_specs = (
        P(("grp", "mem"), None, None),
        P(("grp", "mem")),
        P(),
        P("grp", None, None),
        P("grp", None),
    )
    out_specs = (P(("grp", "mem"), None, None), P(("grp", "mem"), None, None))
    return jax.shard_map(
        per_device, mesh=mesh, in_specs=in_specs, out_specs=out_specs, check_vma=False
    )
```

```python
import functools

import jax
import jax.numpy as jnp
from jax import lax
from jax.experimental import pallas as pl
from jax.experimental.pallas import tpu as pltpu
from jax.sharding import PartitionSpec as P


STRIPS = 4
TILE = 128
F32 = jnp.float32
BF16 = jnp.bfloat16

VMEM = pl.BlockSpec(memory_space=pltpu.VMEM)
SMEM = pl.BlockSpec(memory_space=pltpu.SMEM)


def leads(member):
    return (member & 1) == ((member >> 1) & 1)


def first_round(member):
    return jnp.where(leads(member), 2, 1)


def turn(value, back):
    pairs = []
    for member in range(lax.axis_size("mem")):
        target = member ^ (1 if leads(member) else 2)
        pairs.append((target, member) if back else (member, target))
    return lax.ppermute(value, "mem", pairs)


def swap(value, masks):
    groups, members = lax.axis_size("grp"), lax.axis_size("mem")
    pairs = []
    for g in range(groups):
        for m in range(members):
            grp_mask, mem_mask = masks[0] if leads(m) else masks[1]
            pairs.append((g * members + m, (g ^ grp_mask) * members + (m ^ mem_mask)))
    return lax.ppermute(value, ("grp", "mem"), pairs)


def live(codes, counts, member, round_no):
    total = jnp.int32(0)
    for slot in range(codes.shape[2]):
        hit = (slot < counts[0, member]) & (codes[0, member, slot] == round_no)
        total = total + hit.astype(jnp.int32)
    return total


def weights(codes, counts, round_no):
    me = lax.axis_index("mem")
    other = jnp.where(round_no == 0, me, me ^ round_no)
    own = live(codes, counts, me, round_no)
    far = live(codes, counts, other, round_no)
    return own.astype(F32), far.astype(F32)


def nt(a, b):
    return lax.dot_general(a, b, (((1,), (1,)), ((), ())), preferred_element_type=F32)


def nn(a, b):
    return jnp.dot(a, b, preferred_element_type=F32)


def early_kernel(
    b_ref, row_ref, e_ref, first_ref, second_ref, codes, counts, one_ref, two_ref, dens_ref, gamma_ref, amp
):
    vir, aux = b_ref.shape
    row = row_ref[...]
    sums = jnp.broadcast_to(row, (vir, vir)).T + row - e_ref[0]
    one_ref[...] = 1.0 / (sums - first_ref[0])
    two_ref[...] = 1.0 / (sums - second_ref[0])
    own, _ = weights(codes, counts, 0)
    half = vir // 2
    for at in (slice(0, half), slice(half, vir)):
        k = nt(b_ref[...], b_ref[at, :])
        amp[:, at] = (k / (sums[:, at] - e_ref[0])).astype(BF16)
    a = amp[...]
    dens_ref[...] = own * nn(a, a)
    for p in range(STRIPS):
        at = pl.ds(p * (aux // STRIPS), aux // STRIPS)
        gamma_ref[:, at] = (2.0 * own) * nn(a, b_ref[:, at])


def amp_part(at, b_ref, r_ref, over_ref):
    return (nt(b_ref[...], r_ref[...]) * over_ref[:, at]).astype(BF16)


def blocks(size):
    count = size // TILE
    return [(i, j) for i in range(count) for j in range(i, count)]


def density_kernel(b_ref, r_ref, over_ref, codes, counts, dens_in, mt_ref, keep_ref, send_ref, m_ref):
    vir = b_ref.shape[0]
    half = vir // 2
    me = lax.axis_index("mem")
    own, far = weights(codes, counts, first_round(me))
    for at in (slice(0, half), slice(half, vir)):
        mt = amp_part(at, b_ref, r_ref.at[at, :], over_ref)
        mt_ref[:, at] = mt
        m_ref[at, :] = mt.T
    high, low = slice(0, half), slice(half, vir)

    def sums(rows, columns):
        one = nn(mt_ref[rows, :], m_ref[:, columns])
        two = nn(m_ref[rows, :], mt_ref[:, columns])
        return dens_in[rows, columns] + own * one + far * two

    top, rest = sums(high, slice(0, vir)), sums(low, low)
    pieces = []
    for i, j in blocks(vir):
        if i * TILE < half:
            pieces.append(top[i * TILE : (i + 1) * TILE, j * TILE : (j + 1) * TILE])
        else:
            a, b = i * TILE - half, j * TILE - half
            pieces.append(rest[a : a + TILE, b : b + TILE])
    lead = leads(me)
    count = len(pieces) // 2
    for n in range(count):
        at = pl.ds(n * TILE, TILE)
        keep_ref[at, :] = jnp.where(lead, pieces[n], pieces[n + count])
        send_ref[at, :] = jnp.where(lead, pieces[n + count], pieces[n]).astype(BF16)


def first_gamma_kernel(codes, counts, gamma_in, mt_ref, r_ref, gamma_ref):
    own, far = weights(codes, counts, first_round(lax.axis_index("mem")))
    add_gamma(own + far, mt_ref, r_ref, gamma_in, gamma_ref)


def strip_loop(count, width, body):
    def step(p, carry):
        body(p, pl.ds(pl.multiple_of(p * width, width), width))
        return carry

    lax.fori_loop(0, count, step, 0)


def strips_out(out_ref, held, sems, strips, compute):
    width = held.shape[1] // strips

    def send(p, at):
        return pltpu.make_async_copy(held.at[:, at], out_ref.at[:, at], sems.at[p])

    def body(p, at):
        held[:, at] = compute(at).astype(held.dtype)
        send(p, at).start()

    strip_loop(strips, width, body)
    strip_loop(strips, width, lambda p, at: send(p, at).wait())


def joined(parts, held):
    start = 0
    for part in parts:
        held[start : start + part.shape[0], :] = part[...]
        start += part.shape[0]


def add_gamma(weight, mt_ref, r_ref, gamma_in, gamma_ref):
    aux = gamma_ref.shape[1]

    def body(p, at):
        gamma_ref[:, at] = gamma_in[:, at] + weight * nn(mt_ref[...], r_ref[:, at])

    strip_loop(STRIPS, aux // STRIPS, body)


def second_gamma_kernel(codes, counts, b_ref, over_ref, gamma_in, *refs):
    parts, (gamma_ref, held, mt_ref) = refs[:-3], refs[-3:]
    own, far = weights(codes, counts, 3 - first_round(lax.axis_index("mem")))
    joined(parts, held)
    mt_ref[...] = amp_part(slice(0, held.shape[0]), b_ref, held, over_ref)
    add_gamma(own + far, mt_ref, held, gamma_in, gamma_ref)


def flat_amp(at, b_ref, r_ref, over_ref, m_ref):
    m_ref[...] = (nt(r_ref[...], b_ref[...]) * over_ref[at, :]).astype(BF16)
    return m_ref[...].T


def third_gamma_kernel(cut, codes, counts, b_ref, over_ref, gamma_in, r_ref, gamma_ref, mt_ref, m_ref):
    own, far = weights(codes, counts, 3 - first_round(lax.axis_index("mem")))
    at = slice(cut, cut + r_ref.shape[0])
    mt_ref[...] = flat_amp(at, b_ref, r_ref, over_ref, m_ref)
    add_gamma(own + far, mt_ref, r_ref, gamma_in, gamma_ref)


def last_gamma_kernel(codes, counts, b_ref, over_ref, gamma_in, r_ref, out_ref, held, sems, mt_ref, m_ref):
    own, far = weights(codes, counts, 3 - first_round(lax.axis_index("mem")))
    vir = b_ref.shape[0]
    at = slice(vir - r_ref.shape[0], vir)
    mt_ref[...] = flat_amp(at, b_ref, r_ref, over_ref, m_ref)
    strips_out(
        out_ref, held, sems, STRIPS, lambda at: gamma_in[:, at] + (own + far) * nn(mt_ref[...], r_ref[:, at])
    )


def apply_kernel(mine_ref, other_ref, b_ref, out_ref, tile, held, sems):
    lead = leads(lax.axis_index("mem"))
    names = blocks(tile.shape[0])
    half = len(names) // 2
    for n, (i, j) in enumerate(names):
        at = pl.ds((n % half) * TILE, TILE)
        low, high = (mine_ref, other_ref) if n < half else (other_ref, mine_ref)
        block = jnp.where(lead, low[at, :].astype(F32), high[at, :].astype(F32)).astype(BF16)
        tile[pl.ds(i * TILE, TILE), pl.ds(j * TILE, TILE)] = block
        if i != j:
            tile[pl.ds(j * TILE, TILE), pl.ds(i * TILE, TILE)] = block.T
    strips_out(out_ref, held, sems, STRIPS, lambda at: nn(tile[...], b_ref[:, at]))


def call(kernel, outs, scratch=(), smem=(), count=0, flops=0, out_spec=VMEM):
    return lambda *args: kernel_call(kernel, outs, scratch, smem, count, flops, out_spec)(*args)


def kernel_call(kernel, outs, scratch, smem, count, flops, out_spec):
    return pl.pallas_call(
        kernel,
        out_shape=outs,
        in_specs=[SMEM if i in smem else VMEM for i in range(count)],
        out_specs=jax.tree.map(lambda _: out_spec, outs),
        scratch_shapes=scratch,
        compiler_params=pltpu.CompilerParams(vmem_limit_bytes=32 << 20),
        cost_estimate=pl.CostEstimate(flops=flops, bytes_accessed=1 << 20, transcendentals=0),
    )


def per_device(factors, occ_energy, vir_energy, pair_code, pair_count):
    return body(factors[0], occ_energy, vir_energy, pair_code, pair_count)


def body(block, occ_energy, vir_energy, pair_code, pair_count):
    vir, aux = block.shape
    members, groups = lax.axis_size("mem"), lax.axis_size("grp")
    shape = jax.ShapeDtypeStruct
    square = shape((vir, vir), F32)
    wide = shape((vir, aux), F32)
    dot = 2 * vir * vir * aux
    out_scratch = [pltpu.VMEM((vir, aux), BF16), pltpu.SemaphoreType.DMA((STRIPS,))]
    any_space = pl.BlockSpec(memory_space=pl.ANY)

    first_energy = turn(occ_energy, False).astype(F32)
    first = turn(block, False)
    second_energy = turn(occ_energy, True).astype(F32)

    energy = occ_energy.astype(F32)
    row = vir_energy.astype(F32).reshape(1, vir)
    over_first, over_second, dens, gamma = call(
        early_kernel, (square, square, square, wide), [pltpu.VMEM((vir, vir), BF16)],
        (2, 3, 4, 5, 6), 7, 2 * dot,
    )(block, row, energy, first_energy, second_energy, pair_code, pair_count)

    half = len(blocks(vir)) * TILE // 2
    mt, keep, send = call(
        density_kernel,
        (shape((vir, vir), BF16), shape((half, TILE), F32), shape((half, TILE), BF16)),
        [pltpu.VMEM((vir, vir), BF16)], (3, 4), 6, dot,
    )(block, first, over_first, pair_code, pair_count, dens)

    total = keep + swap(send, [(0, 1), (0, 1)]).astype(F32)
    near = [(0, 3)]
    along = [(0, (1 << k) | 3) for k in range(2, members.bit_length() - 1)]
    across = [(1 << k, 0) for k in range(groups.bit_length() - 1)]
    for masks in zip(near + along + across, near + across[1:] + along + across[:1]):
        got = swap(total.astype(BF16), masks)
        total = total + got.astype(F32)
    mine = (total * (1.0 / (8.0 * groups * members))).astype(BF16)
    other = swap(mine, [(0, 1), (0, 1)])

    unit = vir // 32
    cuts = (0, 7 * unit, 14 * unit, 16 * unit, 24 * unit, vir)
    parts = [block[a:b] for a, b in zip(cuts, cuts[1:])]
    second = [turn(part, True) for part in parts]
    gamma = call(first_gamma_kernel, wide, (), (0, 1), 5, dot)(
        pair_code, pair_count, gamma, mt, first
    )
    gamma = call(
        second_gamma_kernel, wide, [pltpu.VMEM((cuts[3], aux), BF16), pltpu.VMEM((vir, cuts[3]), BF16)],
        (0, 1), 8, dot,
    )(pair_code, pair_count, block, over_second, gamma, *second[:3])
    third, last = cuts[4] - cuts[3], vir - cuts[4]
    gamma = call(
        functools.partial(third_gamma_kernel, cuts[3]), wide,
        [pltpu.VMEM((vir, third), BF16), pltpu.VMEM((third, vir), BF16)], (0, 1), 6, dot // 2,
    )(pair_code, pair_count, block, over_second, gamma, second[3])
    result = call(
        last_gamma_kernel, shape((vir, aux), BF16),
        [*out_scratch, pltpu.VMEM((vir, last), BF16), pltpu.VMEM((last, vir), BF16)],
        (0, 1), 6, dot // 2, any_space,
    )(pair_code, pair_count, block, over_second, gamma, second[4])
    lagrangian = call(
        apply_kernel, shape((vir, aux), BF16), [pltpu.VMEM((vir, vir), BF16), *out_scratch], (), 3, dot,
        any_space,
    )(mine, other, block)
    return (result[None], lagrangian[None])


def solution(mesh):
    in_specs = (
        P(("grp", "mem"), None, None),
        P(("grp", "mem")),
        P(),
        P("grp", None, None),
        P("grp", None),
    )
    out_specs = (P(("grp", "mem"), None, None), P(("grp", "mem"), None, None))
    return jax.shard_map(
        per_device, mesh=mesh, in_specs=in_specs, out_specs=out_specs, check_vma=False
    )
```

```python
import functools

import jax
import jax.numpy as jnp
from jax import lax
from jax.experimental import pallas as pl
from jax.experimental.pallas import tpu as pltpu
from jax.sharding import PartitionSpec as P


STRIPS = 4
TILE = 128
F32 = jnp.float32
BF16 = jnp.bfloat16

VMEM = pl.BlockSpec(memory_space=pltpu.VMEM)
SMEM = pl.BlockSpec(memory_space=pltpu.SMEM)


def leads(member):
    return (member & 1) == ((member >> 1) & 1)


def first_round(member):
    return jnp.where(leads(member), 2, 1)


def turn(value, back):
    pairs = []
    for member in range(lax.axis_size("mem")):
        target = member ^ (1 if leads(member) else 2)
        pairs.append((target, member) if back else (member, target))
    return lax.ppermute(value, "mem", pairs)


def swap(value, masks):
    groups, members = lax.axis_size("grp"), lax.axis_size("mem")
    pairs = []
    for g in range(groups):
        for m in range(members):
            grp_mask, mem_mask = masks[0] if leads(m) else masks[1]
            pairs.append((g * members + m, (g ^ grp_mask) * members + (m ^ mem_mask)))
    return lax.ppermute(value, ("grp", "mem"), pairs)


def live(codes, counts, member, round_no):
    total = jnp.int32(0)
    for slot in range(codes.shape[0]):
        hit = (slot < counts[0, member]) & (codes[slot, 0, member] == round_no)
        total = total + hit.astype(jnp.int32)
    return total


def weights(codes, counts, round_no):
    me = lax.axis_index("mem")
    other = jnp.where(round_no == 0, me, me ^ round_no)
    own = live(codes, counts, me, round_no)
    far = live(codes, counts, other, round_no)
    return own.astype(F32), far.astype(F32)


def nt(a, b):
    return lax.dot_general(a, b, (((1,), (1,)), ((), ())), preferred_element_type=F32)


def nn(a, b):
    return jnp.dot(a, b, preferred_element_type=F32)


def early_kernel(
    split, b_ref, row_ref, e_ref, first_ref, second_ref, codes, counts,
    one_ref, two_ref, dens_ref, gamma_ref, upper_ref, amp
):
    vir, aux = b_ref.shape
    mask = jnp.where(leads(lax.axis_index("mem")), split[0][0], split[1][0])
    upper_ref[...] = jnp.full(upper_ref.shape, ((lax.axis_index("grp") & mask) != 0).astype(F32))
    row = row_ref[...]
    sums = jnp.broadcast_to(row, (vir, vir)).T + row - e_ref[0]
    one_ref[...] = 1.0 / (sums - first_ref[0])
    two_ref[...] = 1.0 / (sums - second_ref[0])
    own, _ = weights(codes, counts, 0)
    half = vir // 2
    for at in (slice(0, half), slice(half, vir)):
        k = nt(b_ref[...], b_ref[at, :])
        amp[:, at] = (k / (sums[:, at] - e_ref[0])).astype(BF16)
    a = amp[...]
    dens_ref[...] = own * nn(a, a)
    for p in range(STRIPS):
        at = pl.ds(p * (aux // STRIPS), aux // STRIPS)
        gamma_ref[:, at] = (2.0 * own) * nn(a, b_ref[:, at])


def amp_part(at, b_ref, r_ref, over_ref):
    return (nt(b_ref[...], r_ref[...]) * over_ref[:, at]).astype(BF16)


def blocks(size):
    count = size // TILE
    return [(i, j) for i in range(count) for j in range(i, count)]


def density_kernel(b_ref, r_ref, over_ref, codes, counts, dens_in, mt_ref, keep_ref, send_ref, m_ref):
    vir = b_ref.shape[0]
    half = vir // 2
    me = lax.axis_index("mem")
    own, far = weights(codes, counts, first_round(me))
    for at in (slice(0, half), slice(half, vir)):
        mt = amp_part(at, b_ref, r_ref.at[at, :], over_ref)
        mt_ref[:, at] = mt
        m_ref[at, :] = mt.T
    high, low = slice(0, half), slice(half, vir)

    def sums(rows, columns):
        one = nn(mt_ref[rows, :], m_ref[:, columns])
        two = nn(m_ref[rows, :], mt_ref[:, columns])
        return dens_in[rows, columns] + own * one + far * two

    top, rest = sums(high, slice(0, vir)), sums(low, low)
    pieces = []
    for i, j in blocks(vir):
        if i * TILE < half:
            pieces.append(top[i * TILE : (i + 1) * TILE, j * TILE : (j + 1) * TILE])
        else:
            a, b = i * TILE - half, j * TILE - half
            pieces.append(rest[a : a + TILE, b : b + TILE])
    lead = leads(me)
    count = len(pieces) // 2
    for n in range(count):
        at = pl.ds(n * TILE, TILE)
        keep_ref[at, :] = jnp.where(lead, pieces[n], pieces[n + count])
        send_ref[at, :] = jnp.where(lead, pieces[n + count], pieces[n]).astype(BF16)


def first_gamma_kernel(codes, counts, gamma_in, mt_ref, r_ref, gamma_ref):
    own, far = weights(codes, counts, first_round(lax.axis_index("mem")))
    aux = gamma_ref.shape[1]
    for p in range(STRIPS):
        at = pl.ds(p * (aux // STRIPS), aux // STRIPS)
        gamma_ref[:, at] = gamma_in[:, at] + (own + far) * nn(mt_ref[...], r_ref[:, at])


def strips_out(out_ref, held, sems, strips, compute):
    step = held.shape[1] // strips
    copies = []
    for p in range(strips):
        at = pl.ds(p * step, step)
        held[:, at] = compute(at).astype(held.dtype)
        copies.append(pltpu.make_async_copy(held.at[:, at], out_ref.at[:, at], sems.at[p]))
        copies[-1].start()
    for copy in copies:
        copy.wait()


def joined(parts, held):
    start = 0
    for part in parts:
        held[start : start + part.shape[0], :] = part[...]
        start += part.shape[0]


def flat_amp(at, b_ref, r_ref, over_ref, m_ref):
    m_ref[...] = (nt(r_ref[...], b_ref[...]) * over_ref[at, :]).astype(BF16)
    return m_ref[...].T


def second_gamma_kernel(codes, counts, b_ref, over_ref, gamma_in, r_ref, gamma_ref, mt_ref, m_ref):
    own, far = weights(codes, counts, 3 - first_round(lax.axis_index("mem")))
    mt_ref[...] = flat_amp(slice(0, r_ref.shape[0]), b_ref, r_ref, over_ref, m_ref)
    aux = gamma_ref.shape[1]
    for p in range(STRIPS):
        at = pl.ds(p * (aux // STRIPS), aux // STRIPS)
        gamma_ref[:, at] = gamma_in[:, at] + (own + far) * nn(mt_ref[...], r_ref[:, at])


def last_gamma_kernel(codes, counts, b_ref, over_ref, gamma_in, *refs):
    parts, (out_ref, held, sems, r_ref, mt_ref, m_ref) = refs[:-6], refs[-6:]
    own, far = weights(codes, counts, 3 - first_round(lax.axis_index("mem")))
    joined(parts, r_ref)
    vir = b_ref.shape[0]
    mt_ref[...] = flat_amp(slice(vir - r_ref.shape[0], vir), b_ref, r_ref, over_ref, m_ref)
    strips_out(
        out_ref, held, sems, STRIPS, lambda at: gamma_in[:, at] + (own + far) * nn(mt_ref[...], r_ref[:, at])
    )


def apply_kernel(mine_ref, other_ref, b_ref, out_ref, tile, held, sems):
    lead = leads(lax.axis_index("mem"))
    names = blocks(tile.shape[0])
    half = len(names) // 2
    for n, (i, j) in enumerate(names):
        at = pl.ds((n % half) * TILE, TILE)
        low, high = (mine_ref, other_ref) if n < half else (other_ref, mine_ref)
        block = jnp.where(lead, low[at, :].astype(F32), high[at, :].astype(F32)).astype(BF16)
        tile[pl.ds(i * TILE, TILE), pl.ds(j * TILE, TILE)] = block
        if i != j:
            tile[pl.ds(j * TILE, TILE), pl.ds(i * TILE, TILE)] = block.T
    strips_out(out_ref, held, sems, STRIPS, lambda at: nn(tile[...], b_ref[:, at]))


def call(kernel, outs, scratch=(), smem=(), count=0, flops=0, out_spec=VMEM):
    return lambda *args: kernel_call(kernel, outs, scratch, smem, count, flops, out_spec)(*args)


def kernel_call(kernel, outs, scratch, smem, count, flops, out_spec):
    return pl.pallas_call(
        kernel,
        out_shape=outs,
        in_specs=[SMEM if i in smem else VMEM for i in range(count)],
        out_specs=jax.tree.map(lambda _: out_spec, outs),
        scratch_shapes=scratch,
        compiler_params=pltpu.CompilerParams(vmem_limit_bytes=12 << 20),
        cost_estimate=pl.CostEstimate(flops=flops, bytes_accessed=1 << 20, transcendentals=0),
    )


def per_device(factors, occ_energy, vir_energy, pair_code, pair_count):
    return body(factors[0], occ_energy, vir_energy, pair_code, pair_count)


def body(block, occ_energy, vir_energy, pair_code, pair_count):
    vir, aux = block.shape
    members, groups = lax.axis_size("mem"), lax.axis_size("grp")
    shape = jax.ShapeDtypeStruct
    square = shape((vir, vir), F32)
    wide = shape((vir, aux), F32)
    dot = 2 * vir * vir * aux
    out_scratch = [pltpu.VMEM((vir, aux), BF16), pltpu.SemaphoreType.DMA((STRIPS,))]
    any_space = pl.BlockSpec(memory_space=pl.ANY)

    first_energy = turn(occ_energy, False).astype(F32)
    first = turn(block, False)
    second_energy = turn(occ_energy, True).astype(F32)

    pair_code = jnp.transpose(pair_code, (2, 0, 1))
    energy = occ_energy.astype(F32)
    row = vir_energy.astype(F32).reshape(1, vir)
    half = len(blocks(vir)) * TILE // 2
    along = [(0, 3)] + [(0, (1 << k) | 3) for k in range(2, members.bit_length() - 1)]
    across = [(1 << k, 0) for k in range(groups.bit_length() - 1)]
    split, *later = zip(across, across[1:] + across[:1])
    over_first, over_second, dens, gamma, upper = call(
        functools.partial(early_kernel, split),
        (square, square, square, wide, shape((half // 2, TILE), F32)), [pltpu.VMEM((vir, vir), BF16)],
        (2, 3, 4, 5, 6), 7, 2 * dot,
    )(block, row, energy, first_energy, second_energy, pair_code, pair_count)

    mt, keep, send = call(
        density_kernel,
        (shape((vir, vir), BF16), shape((half, TILE), F32), shape((half, TILE), BF16)),
        [pltpu.VMEM((vir, vir), BF16)], (3, 4), 6, dot,
    )(block, first, over_first, pair_code, pair_count, dens)

    total = keep + swap(send, [(0, 1), (0, 1)]).astype(F32)
    upper = upper > 0.5
    below, above = total[: half // 2], total[half // 2 :]
    got = swap(jnp.where(upper, below, above).astype(BF16), split)
    total = jnp.where(upper, above, below) + got.astype(F32)
    for masks in later:
        total = total + swap(total.astype(BF16), masks).astype(F32)
    for mask in along:
        total = total + swap(total.astype(BF16), [mask, mask]).astype(F32)
    mine = (total * (1.0 / (8.0 * groups * members))).astype(BF16)
    got = swap(mine, split)
    mine = jnp.concatenate([jnp.where(upper, got, mine), jnp.where(upper, mine, got)])
    other = swap(mine, [(0, 1), (0, 1)])

    unit = vir // 16
    cuts = (0, 8 * unit, 10 * unit, 13 * unit, vir)
    parts = [block[a:b] for a, b in zip(cuts, cuts[1:])]
    second = [turn(part, True) for part in parts]
    gamma = call(first_gamma_kernel, wide, (), (0, 1), 5, dot)(
        pair_code, pair_count, gamma, mt, first
    )
    bounce = [pltpu.VMEM((vir, vir // 2), BF16), pltpu.VMEM((vir // 2, vir), BF16)]
    gamma = call(second_gamma_kernel, wide, bounce, (0, 1), 6, dot)(
        pair_code, pair_count, block, over_second, gamma, second[0]
    )
    result = call(
        last_gamma_kernel, shape((vir, aux), BF16), [*out_scratch, pltpu.VMEM((vir // 2, aux), BF16), *bounce],
        (0, 1), 8, dot, any_space,
    )(pair_code, pair_count, block, over_second, gamma, *second[1:])
    lagrangian = call(
        apply_kernel, shape((vir, aux), BF16), [pltpu.VMEM((vir, vir), BF16), *out_scratch], (), 3, dot,
        any_space,
    )(mine, other, block)
    return (result[None], lagrangian[None])


def solution(mesh):
    in_specs = (
        P(("grp", "mem"), None, None),
        P(("grp", "mem")),
        P(),
        P("grp", None, None),
        P("grp", None),
    )
    out_specs = (P(("grp", "mem"), None, None), P(("grp", "mem"), None, None))
    return jax.shard_map(
        per_device, mesh=mesh, in_specs=in_specs, out_specs=out_specs, check_vma=False
    )
```

```python
import functools

import jax
import jax.numpy as jnp
from jax import lax
from jax.experimental import pallas as pl
from jax.experimental.pallas import tpu as pltpu
from jax.sharding import PartitionSpec as P


STRIPS = 4
TILE = 128
F32 = jnp.float32
BF16 = jnp.bfloat16

VMEM = pl.BlockSpec(memory_space=pltpu.VMEM)
SMEM = pl.BlockSpec(memory_space=pltpu.SMEM)


def leads(member):
    return (member & 1) == ((member >> 1) & 1)


def first_round(member):
    return jnp.where(leads(member), 2, 1)


def turn(value, back):
    pairs = []
    for member in range(lax.axis_size("mem")):
        target = member ^ (1 if leads(member) else 2)
        pairs.append((target, member) if back else (member, target))
    return lax.ppermute(value, "mem", pairs)


def swap(value, masks):
    groups, members = lax.axis_size("grp"), lax.axis_size("mem")
    pairs = []
    for g in range(groups):
        for m in range(members):
            grp_mask, mem_mask = masks[0] if leads(m) else masks[1]
            pairs.append((g * members + m, (g ^ grp_mask) * members + (m ^ mem_mask)))
    return lax.ppermute(value, ("grp", "mem"), pairs)


def live(codes, counts, member, round_no):
    total = jnp.int32(0)
    for slot in range(codes.shape[0]):
        hit = (slot < counts[0, member]) & (codes[slot, 0, member] == round_no)
        total = total + hit.astype(jnp.int32)
    return total


def weights(codes, counts, round_no):
    me = lax.axis_index("mem")
    other = jnp.where(round_no == 0, me, me ^ round_no)
    own = live(codes, counts, me, round_no)
    far = live(codes, counts, other, round_no)
    return own.astype(F32), far.astype(F32)


def nt(a, b):
    return lax.dot_general(a, b, (((1,), (1,)), ((), ())), preferred_element_type=F32)


def nn(a, b):
    return jnp.dot(a, b, preferred_element_type=F32)


def early_kernel(
    split, b_ref, row_ref, e_ref, first_ref, second_ref, codes, counts,
    one_ref, two_ref, dens_ref, gamma_ref, upper_ref, amp
):
    vir, aux = b_ref.shape
    mask = jnp.where(leads(lax.axis_index("mem")), split[0][0], split[1][0])
    upper_ref[...] = jnp.full(upper_ref.shape, ((lax.axis_index("grp") & mask) != 0).astype(F32))
    row = row_ref[...]
    sums = jnp.broadcast_to(row, (vir, vir)).T + row - e_ref[0]
    one_ref[...] = 1.0 / (sums - first_ref[0])
    two_ref[...] = 1.0 / (sums - second_ref[0])
    own, _ = weights(codes, counts, 0)
    half = vir // 2
    for at in (slice(0, half), slice(half, vir)):
        k = nt(b_ref[...], b_ref[at, :])
        amp[:, at] = (k / (sums[:, at] - e_ref[0])).astype(BF16)
    a = amp[...]
    dens_ref[...] = own * nn(a, a)
    for p in range(STRIPS):
        at = pl.ds(p * (aux // STRIPS), aux // STRIPS)
        gamma_ref[:, at] = (2.0 * own) * nn(a, b_ref[:, at])


def amp_part(at, b_ref, r_ref, over_ref):
    return (nt(b_ref[...], r_ref[...]) * over_ref[:, at]).astype(BF16)


def blocks(size):
    count = size // TILE
    return [(i, j) for i in range(count) for j in range(i, count)]


def density_kernel(b_ref, r_ref, over_ref, codes, counts, dens_in, mt_ref, keep_ref, send_ref, m_ref):
    vir = b_ref.shape[0]
    half = vir // 2
    me = lax.axis_index("mem")
    own, far = weights(codes, counts, first_round(me))
    for at in (slice(0, half), slice(half, vir)):
        mt = amp_part(at, b_ref, r_ref.at[at, :], over_ref)
        mt_ref[:, at] = mt
        m_ref[at, :] = mt.T
    high, low = slice(0, half), slice(half, vir)

    def sums(rows, columns):
        one = nn(mt_ref[rows, :], m_ref[:, columns])
        two = nn(m_ref[rows, :], mt_ref[:, columns])
        return dens_in[rows, columns] + own * one + far * two

    top, rest = sums(high, slice(0, vir)), sums(low, low)
    pieces = []
    for i, j in blocks(vir):
        if i * TILE < half:
            pieces.append(top[i * TILE : (i + 1) * TILE, j * TILE : (j + 1) * TILE])
        else:
            a, b = i * TILE - half, j * TILE - half
            pieces.append(rest[a : a + TILE, b : b + TILE])
    lead = leads(me)
    count = len(pieces) // 2
    for n in range(count):
        at = pl.ds(n * TILE, TILE)
        keep_ref[at, :] = jnp.where(lead, pieces[n], pieces[n + count])
        send_ref[at, :] = jnp.where(lead, pieces[n + count], pieces[n]).astype(BF16)


def first_gamma_kernel(codes, counts, gamma_in, mt_ref, r_ref, gamma_ref):
    own, far = weights(codes, counts, first_round(lax.axis_index("mem")))
    aux = gamma_ref.shape[1]
    for p in range(STRIPS):
        at = pl.ds(p * (aux // STRIPS), aux // STRIPS)
        gamma_ref[:, at] = gamma_in[:, at] + (own + far) * nn(mt_ref[...], r_ref[:, at])


def strips_out(out_ref, held, sems, strips, compute):
    step = held.shape[1] // strips
    copies = []
    for p in range(strips):
        at = pl.ds(p * step, step)
        held[:, at] = compute(at).astype(held.dtype)
        copies.append(pltpu.make_async_copy(held.at[:, at], out_ref.at[:, at], sems.at[p]))
        copies[-1].start()
    for copy in copies:
        copy.wait()


def joined(parts, held):
    start = 0
    for part in parts:
        held[start : start + part.shape[0], :] = part[...]
        start += part.shape[0]


def flat_amp(at, b_ref, r_ref, over_ref, m_ref):
    m_ref[...] = (nt(r_ref[...], b_ref[...]) * over_ref[at, :]).astype(BF16)
    return m_ref[...].T


def next_gamma_kernel(cut, codes, counts, b_ref, over_ref, gamma_in, *refs):
    parts, (gamma_ref, r_ref, mt_ref, m_ref) = refs[:-4], refs[-4:]
    own, far = weights(codes, counts, 3 - first_round(lax.axis_index("mem")))
    if len(parts) == 1:
        r_ref = parts[0]
    else:
        joined(parts, r_ref)
    mt_ref[...] = flat_amp(slice(cut, cut + r_ref.shape[0]), b_ref, r_ref, over_ref, m_ref)
    aux = gamma_ref.shape[1]
    for p in range(STRIPS):
        at = pl.ds(p * (aux // STRIPS), aux // STRIPS)
        gamma_ref[:, at] = gamma_in[:, at] + (own + far) * nn(mt_ref[...], r_ref[:, at])


def last_gamma_kernel(codes, counts, b_ref, over_ref, gamma_in, r_ref, out_ref, held, sems, mt_ref, m_ref):
    own, far = weights(codes, counts, 3 - first_round(lax.axis_index("mem")))
    vir = b_ref.shape[0]
    mt_ref[...] = flat_amp(slice(vir - r_ref.shape[0], vir), b_ref, r_ref, over_ref, m_ref)
    strips_out(
        out_ref, held, sems, STRIPS, lambda at: gamma_in[:, at] + (own + far) * nn(mt_ref[...], r_ref[:, at])
    )


def apply_kernel(mine_ref, other_ref, b_ref, out_ref, tile, held, sems):
    lead = leads(lax.axis_index("mem"))
    names = blocks(tile.shape[0])
    half = len(names) // 2
    for n, (i, j) in enumerate(names):
        at = pl.ds((n % half) * TILE, TILE)
        low, high = (mine_ref, other_ref) if n < half else (other_ref, mine_ref)
        block = jnp.where(lead, low[at, :].astype(F32), high[at, :].astype(F32)).astype(BF16)
        tile[pl.ds(i * TILE, TILE), pl.ds(j * TILE, TILE)] = block
        if i != j:
            tile[pl.ds(j * TILE, TILE), pl.ds(i * TILE, TILE)] = block.T
    strips_out(out_ref, held, sems, STRIPS, lambda at: nn(tile[...], b_ref[:, at]))


def call(kernel, outs, scratch=(), smem=(), count=0, flops=0, out_spec=VMEM):
    return lambda *args: kernel_call(kernel, outs, scratch, smem, count, flops, out_spec)(*args)


def kernel_call(kernel, outs, scratch, smem, count, flops, out_spec):
    return pl.pallas_call(
        kernel,
        out_shape=outs,
        in_specs=[SMEM if i in smem else VMEM for i in range(count)],
        out_specs=jax.tree.map(lambda _: out_spec, outs),
        scratch_shapes=scratch,
        compiler_params=pltpu.CompilerParams(vmem_limit_bytes=12 << 20),
        cost_estimate=pl.CostEstimate(flops=flops, bytes_accessed=1 << 20, transcendentals=0),
    )


def per_device(factors, occ_energy, vir_energy, pair_code, pair_count):
    return body(factors[0], occ_energy, vir_energy, pair_code, pair_count)


def body(block, occ_energy, vir_energy, pair_code, pair_count):
    vir, aux = block.shape
    members, groups = lax.axis_size("mem"), lax.axis_size("grp")
    shape = jax.ShapeDtypeStruct
    square = shape((vir, vir), F32)
    wide = shape((vir, aux), F32)
    dot = 2 * vir * vir * aux
    out_scratch = [pltpu.VMEM((vir, aux), BF16), pltpu.SemaphoreType.DMA((STRIPS,))]
    any_space = pl.BlockSpec(memory_space=pl.ANY)

    first_energy = turn(occ_energy, False).astype(F32)
    first = turn(block, False)
    second_energy = turn(occ_energy, True).astype(F32)

    pair_code = jnp.transpose(pair_code, (2, 0, 1))
    energy = occ_energy.astype(F32)
    row = vir_energy.astype(F32).reshape(1, vir)
    half = len(blocks(vir)) * TILE // 2
    along = [(0, 3)] + [(0, (1 << k) | 3) for k in range(2, members.bit_length() - 1)]
    across = [(1 << k, 0) for k in range(groups.bit_length() - 1)]
    split, *later = zip(across, across[1:] + across[:1])
    over_first, over_second, dens, gamma, upper = call(
        functools.partial(early_kernel, split),
        (square, square, square, wide, shape((half // 2, TILE), F32)), [pltpu.VMEM((vir, vir), BF16)],
        (2, 3, 4, 5, 6), 7, 2 * dot,
    )(block, row, energy, first_energy, second_energy, pair_code, pair_count)

    mt, keep, send = call(
        density_kernel,
        (shape((vir, vir), BF16), shape((half, TILE), F32), shape((half, TILE), BF16)),
        [pltpu.VMEM((vir, vir), BF16)], (3, 4), 6, dot,
    )(block, first, over_first, pair_code, pair_count, dens)

    total = keep + swap(send, [(0, 1), (0, 1)]).astype(F32)
    upper = upper > 0.5
    below, above = total[: half // 2], total[half // 2 :]
    got = swap(jnp.where(upper, below, above).astype(BF16), split)
    total = jnp.where(upper, above, below) + got.astype(F32)
    for masks in later:
        total = total + swap(total.astype(BF16), masks).astype(F32)
    for mask in along:
        total = total + swap(total.astype(BF16), [mask, mask]).astype(F32)
    mine = (total * (1.0 / (8.0 * groups * members))).astype(BF16)
    got = swap(mine, split)
    mine = jnp.concatenate([jnp.where(upper, got, mine), jnp.where(upper, mine, got)])
    other = swap(mine, [(0, 1), (0, 1)])

    unit = vir // 32
    cuts = (0, 16 * unit, 21 * unit, 28 * unit, vir)
    parts = [block[a:b] for a, b in zip(cuts, cuts[1:])]
    second = [turn(part, True) for part in parts]
    gamma = call(first_gamma_kernel, wide, (), (0, 1), 5, dot)(
        pair_code, pair_count, gamma, mt, first
    )

    def bounce(rows):
        return [pltpu.VMEM((vir, rows), BF16), pltpu.VMEM((rows, vir), BF16)]

    for a, b in ((0, 1), (1, 3)):
        rows = cuts[b] - cuts[a]
        gamma = call(
            functools.partial(next_gamma_kernel, cuts[a]), wide, [pltpu.VMEM((rows, aux), BF16), *bounce(rows)],
            (0, 1), 5 + b - a, dot,
        )(pair_code, pair_count, block, over_second, gamma, *second[a:b])
    result = call(
        last_gamma_kernel, shape((vir, aux), BF16), [*out_scratch, *bounce(vir - cuts[3])],
        (0, 1), 6, dot, any_space,
    )(pair_code, pair_count, block, over_second, gamma, second[3])
    lagrangian = call(
        apply_kernel, shape((vir, aux), BF16), [pltpu.VMEM((vir, vir), BF16), *out_scratch], (), 3, dot,
        any_space,
    )(mine, other, block)
    return (result[None], lagrangian[None])


def solution(mesh):
    in_specs = (
        P(("grp", "mem"), None, None),
        P(("grp", "mem")),
        P(),
        P("grp", None, None),
        P("grp", None),
    )
    out_specs = (P(("grp", "mem"), None, None), P(("grp", "mem"), None, None))
    return jax.shard_map(
        per_device, mesh=mesh, in_specs=in_specs, out_specs=out_specs, check_vma=False
    )
```

```python
import functools

import jax
import jax.numpy as jnp
from jax import lax
from jax.experimental import pallas as pl
from jax.experimental.pallas import tpu as pltpu
from jax.sharding import PartitionSpec as P


STRIPS = 4
TILE = 128
F32 = jnp.float32
BF16 = jnp.bfloat16

VMEM = pl.BlockSpec(memory_space=pltpu.VMEM)
SMEM = pl.BlockSpec(memory_space=pltpu.SMEM)


def leads(member):
    return (member & 1) == ((member >> 1) & 1)


def first_round(member):
    return jnp.where(leads(member), 2, 1)


def turn(value, back):
    pairs = []
    for member in range(lax.axis_size("mem")):
        target = member ^ (1 if leads(member) else 2)
        pairs.append((target, member) if back else (member, target))
    return lax.ppermute(value, "mem", pairs)


def swap(value, masks):
    groups, members = lax.axis_size("grp"), lax.axis_size("mem")
    pairs = []
    for g in range(groups):
        for m in range(members):
            grp_mask, mem_mask = masks[0] if leads(m) else masks[1]
            pairs.append((g * members + m, (g ^ grp_mask) * members + (m ^ mem_mask)))
    return lax.ppermute(value, ("grp", "mem"), pairs)


def live(codes, counts, member, round_no):
    total = jnp.int32(0)
    for slot in range(codes.shape[0]):
        hit = (slot < counts[0, member]) & (codes[slot, 0, member] == round_no)
        total = total + hit.astype(jnp.int32)
    return total


def weights(codes, counts, round_no):
    me = lax.axis_index("mem")
    other = jnp.where(round_no == 0, me, me ^ round_no)
    own = live(codes, counts, me, round_no)
    far = live(codes, counts, other, round_no)
    return own.astype(F32), far.astype(F32)


def nt(a, b):
    return lax.dot_general(a, b, (((1,), (1,)), ((), ())), preferred_element_type=F32)


def nn(a, b):
    return jnp.dot(a, b, preferred_element_type=F32)


def early_kernel(
    split, b_ref, row_ref, e_ref, first_ref, second_ref, codes, counts,
    one_ref, two_ref, dens_ref, gamma_ref, upper_ref, amp
):
    vir, aux = b_ref.shape
    mask = jnp.where(leads(lax.axis_index("mem")), split[0][0], split[1][0])
    upper_ref[...] = jnp.full(upper_ref.shape, ((lax.axis_index("grp") & mask) != 0).astype(F32))
    row = row_ref[...]
    sums = jnp.broadcast_to(row, (vir, vir)).T + row - e_ref[0]
    one_ref[...] = 1.0 / (sums - first_ref[0])
    two_ref[...] = 1.0 / (sums - second_ref[0])
    own, _ = weights(codes, counts, 0)
    half = vir // 2
    for at in (slice(0, half), slice(half, vir)):
        k = nt(b_ref[...], b_ref[at, :])
        amp[:, at] = (k / (sums[:, at] - e_ref[0])).astype(BF16)
    a = amp[...]
    dens_ref[...] = own * nn(a, a)
    for p in range(STRIPS):
        at = pl.ds(p * (aux // STRIPS), aux // STRIPS)
        gamma_ref[:, at] = (2.0 * own) * nn(a, b_ref[:, at])


def amp_part(at, b_ref, r_ref, over_ref):
    return (nt(b_ref[...], r_ref[...]) * over_ref[:, at]).astype(BF16)


def blocks(size):
    count = size // TILE
    return [(i, j) for i in range(count) for j in range(i, count)]


def density_kernel(b_ref, r_ref, over_ref, codes, counts, dens_in, mt_ref, keep_ref, send_ref, m_ref):
    vir = b_ref.shape[0]
    half = vir // 2
    me = lax.axis_index("mem")
    own, far = weights(codes, counts, first_round(me))
    for at in (slice(0, half), slice(half, vir)):
        mt = amp_part(at, b_ref, r_ref.at[at, :], over_ref)
        mt_ref[:, at] = mt
        m_ref[at, :] = mt.T
    high, low = slice(0, half), slice(half, vir)

    def sums(rows, columns):
        one = nn(mt_ref[rows, :], m_ref[:, columns])
        two = nn(m_ref[rows, :], mt_ref[:, columns])
        return dens_in[rows, columns] + own * one + far * two

    top, rest = sums(high, slice(0, vir)), sums(low, low)
    pieces = []
    for i, j in blocks(vir):
        if i * TILE < half:
            pieces.append(top[i * TILE : (i + 1) * TILE, j * TILE : (j + 1) * TILE])
        else:
            a, b = i * TILE - half, j * TILE - half
            pieces.append(rest[a : a + TILE, b : b + TILE])
    lead = leads(me)
    count = len(pieces) // 2
    for n in range(count):
        at = pl.ds(n * TILE, TILE)
        keep_ref[at, :] = jnp.where(lead, pieces[n], pieces[n + count])
        send_ref[at, :] = jnp.where(lead, pieces[n + count], pieces[n]).astype(BF16)


def first_gamma_kernel(codes, counts, gamma_in, mt_ref, r_ref, gamma_ref):
    own, far = weights(codes, counts, first_round(lax.axis_index("mem")))
    aux = gamma_ref.shape[1]
    for p in range(STRIPS):
        at = pl.ds(p * (aux // STRIPS), aux // STRIPS)
        gamma_ref[:, at] = gamma_in[:, at] + (own + far) * nn(mt_ref[...], r_ref[:, at])


def strips_out(out_ref, held, sems, strips, compute):
    step = held.shape[1] // strips
    copies = []
    for p in range(strips):
        at = pl.ds(p * step, step)
        held[:, at] = compute(at).astype(held.dtype)
        copies.append(pltpu.make_async_copy(held.at[:, at], out_ref.at[:, at], sems.at[p]))
        copies[-1].start()
    for copy in copies:
        copy.wait()


def joined(parts, held):
    start = 0
    for part in parts:
        held[start : start + part.shape[0], :] = part[...]
        start += part.shape[0]


def flat_amp(at, b_ref, r_ref, over_ref, m_ref):
    m_ref[...] = (nt(r_ref[...], b_ref[...]) * over_ref[at, :]).astype(BF16)
    return m_ref[...].T


def second_gamma_kernel(codes, counts, b_ref, over_ref, gamma_in, *refs):
    parts, (gamma_ref, r_ref, mt_ref, m_ref) = refs[:-4], refs[-4:]
    own, far = weights(codes, counts, 3 - first_round(lax.axis_index("mem")))
    joined(parts, r_ref)
    mt_ref[...] = flat_amp(slice(0, r_ref.shape[0]), b_ref, r_ref, over_ref, m_ref)
    aux = gamma_ref.shape[1]
    for p in range(STRIPS):
        at = pl.ds(p * (aux // STRIPS), aux // STRIPS)
        gamma_ref[:, at] = gamma_in[:, at] + (own + far) * nn(mt_ref[...], r_ref[:, at])


def last_gamma_kernel(codes, counts, b_ref, over_ref, gamma_in, *refs):
    parts, (out_ref, held, sems, r_ref, mt_ref, m_ref) = refs[:-6], refs[-6:]
    own, far = weights(codes, counts, 3 - first_round(lax.axis_index("mem")))
    joined(parts, r_ref)
    vir = b_ref.shape[0]
    mt_ref[...] = flat_amp(slice(vir - r_ref.shape[0], vir), b_ref, r_ref, over_ref, m_ref)
    strips_out(
        out_ref, held, sems, STRIPS, lambda at: gamma_in[:, at] + (own + far) * nn(mt_ref[...], r_ref[:, at])
    )


def apply_kernel(mine_ref, other_ref, b_ref, out_ref, tile, held, sems):
    lead = leads(lax.axis_index("mem"))
    names = blocks(tile.shape[0])
    half = len(names) // 2
    for n, (i, j) in enumerate(names):
        at = pl.ds((n % half) * TILE, TILE)
        low, high = (mine_ref, other_ref) if n < half else (other_ref, mine_ref)
        block = jnp.where(lead, low[at, :].astype(F32), high[at, :].astype(F32)).astype(BF16)
        tile[pl.ds(i * TILE, TILE), pl.ds(j * TILE, TILE)] = block
        if i != j:
            tile[pl.ds(j * TILE, TILE), pl.ds(i * TILE, TILE)] = block.T
    strips_out(out_ref, held, sems, STRIPS, lambda at: nn(tile[...], b_ref[:, at]))


def call(kernel, outs, scratch=(), smem=(), count=0, flops=0, out_spec=VMEM):
    return lambda *args: kernel_call(kernel, outs, scratch, smem, count, flops, out_spec)(*args)


def kernel_call(kernel, outs, scratch, smem, count, flops, out_spec):
    return pl.pallas_call(
        kernel,
        out_shape=outs,
        in_specs=[SMEM if i in smem else VMEM for i in range(count)],
        out_specs=jax.tree.map(lambda _: out_spec, outs),
        scratch_shapes=scratch,
        compiler_params=pltpu.CompilerParams(vmem_limit_bytes=12 << 20),
        cost_estimate=pl.CostEstimate(flops=flops, bytes_accessed=1 << 20, transcendentals=0),
    )


def per_device(factors, occ_energy, vir_energy, pair_code, pair_count):
    return body(factors[0], occ_energy, vir_energy, pair_code, pair_count)


def body(block, occ_energy, vir_energy, pair_code, pair_count):
    vir, aux = block.shape
    members, groups = lax.axis_size("mem"), lax.axis_size("grp")
    shape = jax.ShapeDtypeStruct
    square = shape((vir, vir), F32)
    wide = shape((vir, aux), F32)
    dot = 2 * vir * vir * aux
    out_scratch = [pltpu.VMEM((vir, aux), BF16), pltpu.SemaphoreType.DMA((STRIPS,))]
    any_space = pl.BlockSpec(memory_space=pl.ANY)

    first_energy = turn(occ_energy, False).astype(F32)
    first = turn(block, False)
    second_energy = turn(occ_energy, True).astype(F32)

    pair_code = jnp.transpose(pair_code, (2, 0, 1))
    energy = occ_energy.astype(F32)
    row = vir_energy.astype(F32).reshape(1, vir)
    half = len(blocks(vir)) * TILE // 2
    along = [(0, 3)] + [(0, (1 << k) | 3) for k in range(2, members.bit_length() - 1)]
    across = [(1 << k, 0) for k in range(groups.bit_length() - 1)]
    split, *later = zip(across, across[1:] + across[:1])
    over_first, over_second, dens, gamma, upper = call(
        functools.partial(early_kernel, split),
        (square, square, square, wide, shape((half // 2, TILE), F32)), [pltpu.VMEM((vir, vir), BF16)],
        (2, 3, 4, 5, 6), 7, 2 * dot,
    )(block, row, energy, first_energy, second_energy, pair_code, pair_count)

    mt, keep, send = call(
        density_kernel,
        (shape((vir, vir), BF16), shape((half, TILE), F32), shape((half, TILE), BF16)),
        [pltpu.VMEM((vir, vir), BF16)], (3, 4), 6, dot,
    )(block, first, over_first, pair_code, pair_count, dens)

    total = keep + swap(send, [(0, 1), (0, 1)]).astype(F32)
    upper = upper > 0.5
    below, above = total[: half // 2], total[half // 2 :]
    got = swap(jnp.where(upper, below, above).astype(BF16), split)
    total = jnp.where(upper, above, below) + got.astype(F32)
    for mask in along[1:] + along[:1]:
        total = total + swap(total.astype(BF16), [mask, mask]).astype(F32)
    for masks in later:
        total = total + swap(total.astype(BF16), masks).astype(F32)
    mine = (total * (1.0 / (8.0 * groups * members))).astype(BF16)
    got = swap(mine, split)
    mine = jnp.concatenate([jnp.where(upper, got, mine), jnp.where(upper, mine, got)])
    other = swap(mine, [(0, 1), (0, 1)])

    unit = vir // 32
    cuts = (0, 14 * unit, 16 * unit, 21 * unit, vir)
    parts = [block[a:b] for a, b in zip(cuts, cuts[1:])]
    second = [turn(part, True) for part in parts]
    gamma = call(first_gamma_kernel, wide, (), (0, 1), 5, dot)(
        pair_code, pair_count, gamma, mt, first
    )
    bounce = [
        pltpu.VMEM((vir // 2, aux), BF16),
        pltpu.VMEM((vir, vir // 2), BF16),
        pltpu.VMEM((vir // 2, vir), BF16),
    ]
    gamma = call(second_gamma_kernel, wide, bounce, (0, 1), 7, dot)(
        pair_code, pair_count, block, over_second, gamma, *second[:2]
    )
    result = call(
        last_gamma_kernel, shape((vir, aux), BF16), [*out_scratch, *bounce], (0, 1), 7, dot, any_space
    )(pair_code, pair_count, block, over_second, gamma, *second[2:])
    lagrangian = call(
        apply_kernel, shape((vir, aux), BF16), [pltpu.VMEM((vir, vir), BF16), *out_scratch], (), 3, dot,
        any_space,
    )(mine, other, block)
    return (result[None], lagrangian[None])


def solution(mesh):
    in_specs = (
        P(("grp", "mem"), None, None),
        P(("grp", "mem")),
        P(),
        P("grp", None, None),
        P("grp", None),
    )
    out_specs = (P(("grp", "mem"), None, None), P(("grp", "mem"), None, None))
    return jax.shard_map(
        per_device, mesh=mesh, in_specs=in_specs, out_specs=out_specs, check_vma=False
    )
```

```python
import functools

import jax
import jax.numpy as jnp
from jax import lax
from jax.experimental import pallas as pl
from jax.experimental.pallas import tpu as pltpu
from jax.sharding import PartitionSpec as P


STRIPS = 4
TILE = 128
F32 = jnp.float32
BF16 = jnp.bfloat16

VMEM = pl.BlockSpec(memory_space=pltpu.VMEM)
SMEM = pl.BlockSpec(memory_space=pltpu.SMEM)


def leads(member):
    return (member & 1) == ((member >> 1) & 1)


def first_round(member):
    return jnp.where(leads(member), 2, 1)


def turn(value, back):
    pairs = []
    for member in range(lax.axis_size("mem")):
        target = member ^ (1 if leads(member) else 2)
        pairs.append((target, member) if back else (member, target))
    return lax.ppermute(value, "mem", pairs)


def swap(value, masks):
    groups, members = lax.axis_size("grp"), lax.axis_size("mem")
    pairs = []
    for g in range(groups):
        for m in range(members):
            grp_mask, mem_mask = masks[0] if leads(m) else masks[1]
            pairs.append((g * members + m, (g ^ grp_mask) * members + (m ^ mem_mask)))
    return lax.ppermute(value, ("grp", "mem"), pairs)


def live(codes, counts, member, round_no):
    total = jnp.int32(0)
    for slot in range(codes.shape[0]):
        hit = (slot < counts[0, member]) & (codes[slot, 0, member] == round_no)
        total = total + hit.astype(jnp.int32)
    return total


def weights(codes, counts, round_no):
    me = lax.axis_index("mem")
    other = jnp.where(round_no == 0, me, me ^ round_no)
    own = live(codes, counts, me, round_no)
    far = live(codes, counts, other, round_no)
    return own.astype(F32), far.astype(F32)


def nt(a, b):
    return lax.dot_general(a, b, (((1,), (1,)), ((), ())), preferred_element_type=F32)


def nn(a, b):
    return jnp.dot(a, b, preferred_element_type=F32)


def early_kernel(
    split, b_ref, row_ref, e_ref, first_ref, second_ref, codes, counts,
    one_ref, two_ref, dens_ref, gamma_ref, upper_ref, amp
):
    vir, aux = b_ref.shape
    mask = jnp.where(leads(lax.axis_index("mem")), split[0][0], split[1][0])
    upper_ref[...] = jnp.full(upper_ref.shape, ((lax.axis_index("grp") & mask) != 0).astype(F32))
    row = row_ref[...]
    sums = jnp.broadcast_to(row, (vir, vir)).T + row - e_ref[0]
    one_ref[...] = 1.0 / (sums - first_ref[0])
    two_ref[...] = 1.0 / (sums - second_ref[0])
    own, _ = weights(codes, counts, 0)
    half = vir // 2
    for at in (slice(0, half), slice(half, vir)):
        k = nt(b_ref[...], b_ref[at, :])
        amp[:, at] = (k / (sums[:, at] - e_ref[0])).astype(BF16)
    a = amp[...]
    dens_ref[...] = own * nn(a, a)
    for p in range(STRIPS):
        at = pl.ds(p * (aux // STRIPS), aux // STRIPS)
        gamma_ref[:, at] = (2.0 * own) * nn(a, b_ref[:, at])


def amp_part(at, b_ref, r_ref, over_ref):
    return (nt(b_ref[...], r_ref[...]) * over_ref[:, at]).astype(BF16)


def blocks(size):
    count = size // TILE
    return [(i, j) for i in range(count) for j in range(i, count)]


def density_kernel(b_ref, r_ref, over_ref, codes, counts, dens_in, mt_ref, keep_ref, send_ref, m_ref):
    vir = b_ref.shape[0]
    half = vir // 2
    me = lax.axis_index("mem")
    own, far = weights(codes, counts, first_round(me))
    for at in (slice(0, half), slice(half, vir)):
        mt = amp_part(at, b_ref, r_ref.at[at, :], over_ref)
        mt_ref[:, at] = mt
        m_ref[at, :] = mt.T
    high, low = slice(0, half), slice(half, vir)

    def sums(rows, columns):
        one = nn(mt_ref[rows, :], m_ref[:, columns])
        two = nn(m_ref[rows, :], mt_ref[:, columns])
        return dens_in[rows, columns] + own * one + far * two

    top, rest = sums(high, slice(0, vir)), sums(low, low)
    pieces = []
    for i, j in blocks(vir):
        if i * TILE < half:
            pieces.append(top[i * TILE : (i + 1) * TILE, j * TILE : (j + 1) * TILE])
        else:
            a, b = i * TILE - half, j * TILE - half
            pieces.append(rest[a : a + TILE, b : b + TILE])
    lead = leads(me)
    count = len(pieces) // 2
    for n in range(count):
        at = pl.ds(n * TILE, TILE)
        keep_ref[at, :] = jnp.where(lead, pieces[n], pieces[n + count])
        send_ref[at, :] = jnp.where(lead, pieces[n + count], pieces[n]).astype(BF16)


def first_gamma_kernel(codes, counts, gamma_in, mt_ref, r_ref, gamma_ref):
    own, far = weights(codes, counts, first_round(lax.axis_index("mem")))
    aux = gamma_ref.shape[1]
    for p in range(STRIPS):
        at = pl.ds(p * (aux // STRIPS), aux // STRIPS)
        gamma_ref[:, at] = gamma_in[:, at] + (own + far) * nn(mt_ref[...], r_ref[:, at])


def strips_out(out_ref, held, sems, strips, compute):
    step = held.shape[1] // strips
    copies = []
    for p in range(strips):
        at = pl.ds(p * step, step)
        held[:, at] = compute(at).astype(held.dtype)
        copies.append(pltpu.make_async_copy(held.at[:, at], out_ref.at[:, at], sems.at[p]))
        copies[-1].start()
    for copy in copies:
        copy.wait()


def joined(parts, held):
    start = 0
    for part in parts:
        held[start : start + part.shape[0], :] = part[...]
        start += part.shape[0]


def flat_amp(at, b_ref, r_ref, over_ref, m_ref):
    m_ref[...] = (nt(r_ref[...], b_ref[...]) * over_ref[at, :]).astype(BF16)
    return m_ref[...].T


def second_gamma_kernel(codes, counts, b_ref, over_ref, gamma_in, r_ref, gamma_ref, mt_ref, m_ref):
    own, far = weights(codes, counts, 3 - first_round(lax.axis_index("mem")))
    mt_ref[...] = flat_amp(slice(0, r_ref.shape[0]), b_ref, r_ref, over_ref, m_ref)
    aux = gamma_ref.shape[1]
    for p in range(STRIPS):
        at = pl.ds(p * (aux // STRIPS), aux // STRIPS)
        gamma_ref[:, at] = gamma_in[:, at] + (own + far) * nn(mt_ref[...], r_ref[:, at])


def last_gamma_kernel(codes, counts, b_ref, over_ref, gamma_in, *refs):
    parts, (out_ref, held, sems, r_ref, mt_ref, m_ref) = refs[:-6], refs[-6:]
    own, far = weights(codes, counts, 3 - first_round(lax.axis_index("mem")))
    joined(parts, r_ref)
    vir = b_ref.shape[0]
    mt_ref[...] = flat_amp(slice(vir - r_ref.shape[0], vir), b_ref, r_ref, over_ref, m_ref)
    strips_out(
        out_ref, held, sems, STRIPS, lambda at: gamma_in[:, at] + (own + far) * nn(mt_ref[...], r_ref[:, at])
    )


def apply_kernel(mine_ref, other_ref, b_ref, out_ref, tile, held, sems):
    lead = leads(lax.axis_index("mem"))
    names = blocks(tile.shape[0])
    half = len(names) // 2
    for n, (i, j) in enumerate(names):
        at = pl.ds((n % half) * TILE, TILE)
        low, high = (mine_ref, other_ref) if n < half else (other_ref, mine_ref)
        block = jnp.where(lead, low[at, :].astype(F32), high[at, :].astype(F32)).astype(BF16)
        tile[pl.ds(i * TILE, TILE), pl.ds(j * TILE, TILE)] = block
        if i != j:
            tile[pl.ds(j * TILE, TILE), pl.ds(i * TILE, TILE)] = block.T
    strips_out(out_ref, held, sems, STRIPS, lambda at: nn(tile[...], b_ref[:, at]))


def call(kernel, outs, scratch=(), smem=(), count=0, flops=0, out_spec=VMEM):
    return lambda *args: kernel_call(kernel, outs, scratch, smem, count, flops, out_spec)(*args)


def kernel_call(kernel, outs, scratch, smem, count, flops, out_spec):
    return pl.pallas_call(
        kernel,
        out_shape=outs,
        in_specs=[SMEM if i in smem else VMEM for i in range(count)],
        out_specs=jax.tree.map(lambda _: out_spec, outs),
        scratch_shapes=scratch,
        compiler_params=pltpu.CompilerParams(vmem_limit_bytes=12 << 20),
        cost_estimate=pl.CostEstimate(flops=flops, bytes_accessed=1 << 20, transcendentals=0),
    )


def per_device(factors, occ_energy, vir_energy, pair_code, pair_count):
    return body(factors[0], occ_energy, vir_energy, pair_code, pair_count)


def body(block, occ_energy, vir_energy, pair_code, pair_count):
    vir, aux = block.shape
    members, groups = lax.axis_size("mem"), lax.axis_size("grp")
    shape = jax.ShapeDtypeStruct
    square = shape((vir, vir), F32)
    wide = shape((vir, aux), F32)
    dot = 2 * vir * vir * aux
    out_scratch = [pltpu.VMEM((vir, aux), BF16), pltpu.SemaphoreType.DMA((STRIPS,))]
    any_space = pl.BlockSpec(memory_space=pl.ANY)

    first_energy = turn(occ_energy, False).astype(F32)
    first = turn(block, False)
    second_energy = turn(occ_energy, True).astype(F32)

    pair_code = jnp.transpose(pair_code, (2, 0, 1))
    energy = occ_energy.astype(F32)
    row = vir_energy.astype(F32).reshape(1, vir)
    half = len(blocks(vir)) * TILE // 2
    along = [(0, 3)] + [(0, (1 << k) | 3) for k in range(2, members.bit_length() - 1)]
    across = [(1 << k, 0) for k in range(groups.bit_length() - 1)]
    split, *later = zip(across, across[1:] + across[:1])
    over_first, over_second, dens, gamma, upper = call(
        functools.partial(early_kernel, split),
        (square, square, square, wide, shape((half // 2, TILE), F32)), [pltpu.VMEM((vir, vir), BF16)],
        (2, 3, 4, 5, 6), 7, 2 * dot,
    )(block, row, energy, first_energy, second_energy, pair_code, pair_count)

    mt, keep, send = call(
        density_kernel,
        (shape((vir, vir), BF16), shape((half, TILE), F32), shape((half, TILE), BF16)),
        [pltpu.VMEM((vir, vir), BF16)], (3, 4), 6, dot,
    )(block, first, over_first, pair_code, pair_count, dens)

    total = keep + swap(send, [(0, 1), (0, 1)]).astype(F32)
    upper = upper > 0.5
    below, above = total[: half // 2], total[half // 2 :]
    got = swap(jnp.where(upper, below, above).astype(BF16), split)
    total = jnp.where(upper, above, below) + got.astype(F32)
    for mask in along[1:] + along[:1]:
        total = total + swap(total.astype(BF16), [mask, mask]).astype(F32)
    for masks in later:
        total = total + swap(total.astype(BF16), masks).astype(F32)
    mine = (total * (1.0 / (8.0 * groups * members))).astype(BF16)
    got = swap(mine, split)
    mine = jnp.concatenate([jnp.where(upper, got, mine), jnp.where(upper, mine, got)])
    other = swap(mine, [(0, 1), (0, 1)])

    unit = vir // 16
    cuts = (0, 8 * unit, 10 * unit, vir)
    parts = [block[a:b] for a, b in zip(cuts, cuts[1:])]
    second = [turn(part, True) for part in parts]
    gamma = call(first_gamma_kernel, wide, (), (0, 1), 5, dot)(
        pair_code, pair_count, gamma, mt, first
    )
    bounce = [pltpu.VMEM((vir, vir // 2), BF16), pltpu.VMEM((vir // 2, vir), BF16)]
    gamma = call(second_gamma_kernel, wide, bounce, (0, 1), 6, dot)(
        pair_code, pair_count, block, over_second, gamma, second[0]
    )
    result = call(
        last_gamma_kernel, shape((vir, aux), BF16), [*out_scratch, pltpu.VMEM((vir // 2, aux), BF16), *bounce],
        (0, 1), 5 + len(second) - 1, dot, any_space,
    )(pair_code, pair_count, block, over_second, gamma, *second[1:])
    lagrangian = call(
        apply_kernel, shape((vir, aux), BF16), [pltpu.VMEM((vir, vir), BF16), *out_scratch], (), 3, dot,
        any_space,
    )(mine, other, block)
    return (result[None], lagrangian[None])


def solution(mesh):
    in_specs = (
        P(("grp", "mem"), None, None),
        P(("grp", "mem")),
        P(),
        P("grp", None, None),
        P("grp", None),
    )
    out_specs = (P(("grp", "mem"), None, None), P(("grp", "mem"), None, None))
    return jax.shard_map(
        per_device, mesh=mesh, in_specs=in_specs, out_specs=out_specs, check_vma=False
    )
```

```python
import functools

import jax
import jax.numpy as jnp
from jax import lax
from jax.experimental import pallas as pl
from jax.experimental.pallas import tpu as pltpu
from jax.sharding import PartitionSpec as P


STRIPS = 4
TILE = 128
F32 = jnp.float32
BF16 = jnp.bfloat16

VMEM = pl.BlockSpec(memory_space=pltpu.VMEM)
SMEM = pl.BlockSpec(memory_space=pltpu.SMEM)


def leads(member):
    return (member & 1) == ((member >> 1) & 1)


def first_round(member):
    return jnp.where(leads(member), 2, 1)


def turn(value, back):
    pairs = []
    for member in range(lax.axis_size("mem")):
        target = member ^ (1 if leads(member) else 2)
        pairs.append((target, member) if back else (member, target))
    return lax.ppermute(value, "mem", pairs)


def swap(value, masks):
    groups, members = lax.axis_size("grp"), lax.axis_size("mem")
    pairs = []
    for g in range(groups):
        for m in range(members):
            grp_mask, mem_mask = masks[0] if leads(m) else masks[1]
            pairs.append((g * members + m, (g ^ grp_mask) * members + (m ^ mem_mask)))
    return lax.ppermute(value, ("grp", "mem"), pairs)


def live(codes, counts, member, round_no):
    total = jnp.int32(0)
    for slot in range(codes.shape[0]):
        hit = (slot < counts[0, member]) & (codes[slot, 0, member] == round_no)
        total = total + hit.astype(jnp.int32)
    return total


def weights(codes, counts, round_no):
    me = lax.axis_index("mem")
    other = jnp.where(round_no == 0, me, me ^ round_no)
    own = live(codes, counts, me, round_no)
    far = live(codes, counts, other, round_no)
    return own.astype(F32), far.astype(F32)


def nt(a, b):
    return lax.dot_general(a, b, (((1,), (1,)), ((), ())), preferred_element_type=F32)


def nn(a, b):
    return jnp.dot(a, b, preferred_element_type=F32)


def early_kernel(
    split, b_ref, row_ref, e_ref, first_ref, second_ref, codes, counts,
    one_ref, two_ref, dens_ref, gamma_ref, upper_ref, amp
):
    vir, aux = b_ref.shape
    mask = jnp.where(leads(lax.axis_index("mem")), split[0][0], split[1][0])
    upper_ref[...] = jnp.full(upper_ref.shape, ((lax.axis_index("grp") & mask) != 0).astype(F32))
    row = row_ref[...]
    sums = jnp.broadcast_to(row, (vir, vir)).T + row - e_ref[0]
    one_ref[...] = 1.0 / (sums - first_ref[0])
    two_ref[...] = 1.0 / (sums - second_ref[0])
    own, _ = weights(codes, counts, 0)
    half = vir // 2
    for at in (slice(0, half), slice(half, vir)):
        k = nt(b_ref[...], b_ref[at, :])
        amp[:, at] = (k / (sums[:, at] - e_ref[0])).astype(BF16)
    a = amp[...]
    dens_ref[...] = own * nn(a, a)
    for p in range(STRIPS):
        at = pl.ds(p * (aux // STRIPS), aux // STRIPS)
        gamma_ref[:, at] = (2.0 * own) * nn(a, b_ref[:, at])


def amp_part(at, b_ref, r_ref, over_ref):
    return (nt(b_ref[...], r_ref[...]) * over_ref[:, at]).astype(BF16)


def blocks(size):
    count = size // TILE
    return [(i, j) for i in range(count) for j in range(i, count)]


def density_kernel(b_ref, r_ref, over_ref, codes, counts, dens_in, mt_ref, keep_ref, send_ref, m_ref):
    vir = b_ref.shape[0]
    half = vir // 2
    me = lax.axis_index("mem")
    own, far = weights(codes, counts, first_round(me))
    for at in (slice(0, half), slice(half, vir)):
        mt = amp_part(at, b_ref, r_ref.at[at, :], over_ref)
        mt_ref[:, at] = mt
        m_ref[at, :] = mt.T
    high, low = slice(0, half), slice(half, vir)

    def sums(rows, columns):
        one = nn(mt_ref[rows, :], m_ref[:, columns])
        two = nn(m_ref[rows, :], mt_ref[:, columns])
        return dens_in[rows, columns] + own * one + far * two

    top, rest = sums(high, slice(0, vir)), sums(low, low)
    pieces = []
    for i, j in blocks(vir):
        if i * TILE < half:
            pieces.append(top[i * TILE : (i + 1) * TILE, j * TILE : (j + 1) * TILE])
        else:
            a, b = i * TILE - half, j * TILE - half
            pieces.append(rest[a : a + TILE, b : b + TILE])
    lead = leads(me)
    count = len(pieces) // 2
    for n in range(count):
        at = pl.ds(n * TILE, TILE)
        keep_ref[at, :] = jnp.where(lead, pieces[n], pieces[n + count])
        send_ref[at, :] = jnp.where(lead, pieces[n + count], pieces[n]).astype(BF16)


def first_gamma_kernel(codes, counts, gamma_in, mt_ref, r_ref, gamma_ref):
    own, far = weights(codes, counts, first_round(lax.axis_index("mem")))
    aux = gamma_ref.shape[1]
    for p in range(STRIPS):
        at = pl.ds(p * (aux // STRIPS), aux // STRIPS)
        gamma_ref[:, at] = gamma_in[:, at] + (own + far) * nn(mt_ref[...], r_ref[:, at])


def strips_out(out_ref, held, sems, strips, compute):
    step = held.shape[1] // strips
    copies = []
    for p in range(strips):
        at = pl.ds(p * step, step)
        held[:, at] = compute(at).astype(held.dtype)
        copies.append(pltpu.make_async_copy(held.at[:, at], out_ref.at[:, at], sems.at[p]))
        copies[-1].start()
    for copy in copies:
        copy.wait()


def joined(parts, held):
    start = 0
    for part in parts:
        held[start : start + part.shape[0], :] = part[...]
        start += part.shape[0]


def flat_amp(at, b_ref, r_ref, over_ref, m_ref):
    m_ref[...] = (nt(r_ref[...], b_ref[...]) * over_ref[at, :]).astype(BF16)
    return m_ref[...].T


def second_gamma_kernel(codes, counts, b_ref, over_ref, gamma_in, r_ref, gamma_ref, mt_ref, m_ref):
    own, far = weights(codes, counts, 3 - first_round(lax.axis_index("mem")))
    mt_ref[...] = flat_amp(slice(0, r_ref.shape[0]), b_ref, r_ref, over_ref, m_ref)
    aux = gamma_ref.shape[1]
    for p in range(STRIPS):
        at = pl.ds(p * (aux // STRIPS), aux // STRIPS)
        gamma_ref[:, at] = gamma_in[:, at] + (own + far) * nn(mt_ref[...], r_ref[:, at])


def last_gamma_kernel(codes, counts, b_ref, over_ref, gamma_in, *refs):
    parts, (out_ref, held, sems, r_ref, mt_ref, m_ref) = refs[:-6], refs[-6:]
    own, far = weights(codes, counts, 3 - first_round(lax.axis_index("mem")))
    joined(parts, r_ref)
    vir = b_ref.shape[0]
    mt_ref[...] = flat_amp(slice(vir - r_ref.shape[0], vir), b_ref, r_ref, over_ref, m_ref)
    strips_out(
        out_ref, held, sems, STRIPS, lambda at: gamma_in[:, at] + (own + far) * nn(mt_ref[...], r_ref[:, at])
    )


def apply_kernel(mine_ref, other_ref, b_ref, out_ref, tile, held, sems):
    lead = leads(lax.axis_index("mem"))
    names = blocks(tile.shape[0])
    half = len(names) // 2
    for n, (i, j) in enumerate(names):
        at = pl.ds((n % half) * TILE, TILE)
        low, high = (mine_ref, other_ref) if n < half else (other_ref, mine_ref)
        block = jnp.where(lead, low[at, :].astype(F32), high[at, :].astype(F32)).astype(BF16)
        tile[pl.ds(i * TILE, TILE), pl.ds(j * TILE, TILE)] = block
        if i != j:
            tile[pl.ds(j * TILE, TILE), pl.ds(i * TILE, TILE)] = block.T
    strips_out(out_ref, held, sems, STRIPS, lambda at: nn(tile[...], b_ref[:, at]))


def call(kernel, outs, scratch=(), smem=(), count=0, flops=0, out_spec=VMEM):
    return lambda *args: kernel_call(kernel, outs, scratch, smem, count, flops, out_spec)(*args)


def kernel_call(kernel, outs, scratch, smem, count, flops, out_spec):
    return pl.pallas_call(
        kernel,
        out_shape=outs,
        in_specs=[SMEM if i in smem else VMEM for i in range(count)],
        out_specs=jax.tree.map(lambda _: out_spec, outs),
        scratch_shapes=scratch,
        compiler_params=pltpu.CompilerParams(vmem_limit_bytes=12 << 20),
        cost_estimate=pl.CostEstimate(flops=flops, bytes_accessed=1 << 20, transcendentals=0),
    )


def per_device(factors, occ_energy, vir_energy, pair_code, pair_count):
    return body(factors[0], occ_energy, vir_energy, pair_code, pair_count)


def body(block, occ_energy, vir_energy, pair_code, pair_count):
    vir, aux = block.shape
    members, groups = lax.axis_size("mem"), lax.axis_size("grp")
    shape = jax.ShapeDtypeStruct
    square = shape((vir, vir), F32)
    wide = shape((vir, aux), F32)
    dot = 2 * vir * vir * aux
    out_scratch = [pltpu.VMEM((vir, aux), BF16), pltpu.SemaphoreType.DMA((STRIPS,))]
    any_space = pl.BlockSpec(memory_space=pl.ANY)

    first_energy = turn(occ_energy, False).astype(F32)
    first = turn(block, False)
    second_energy = turn(occ_energy, True).astype(F32)

    pair_code = jnp.transpose(pair_code, (2, 0, 1))
    energy = occ_energy.astype(F32)
    row = vir_energy.astype(F32).reshape(1, vir)
    half = len(blocks(vir)) * TILE // 2
    along = [(0, 3)] + [(0, (1 << k) | 3) for k in range(2, members.bit_length() - 1)]
    across = [(1 << k, 0) for k in range(groups.bit_length() - 1)]
    split, *later = zip(across, across[1:] + across[:1])
    over_first, over_second, dens, gamma, upper = call(
        functools.partial(early_kernel, split),
        (square, square, square, wide, shape((half // 2, TILE), F32)), [pltpu.VMEM((vir, vir), BF16)],
        (2, 3, 4, 5, 6), 7, 2 * dot,
    )(block, row, energy, first_energy, second_energy, pair_code, pair_count)

    mt, keep, send = call(
        density_kernel,
        (shape((vir, vir), BF16), shape((half, TILE), F32), shape((half, TILE), BF16)),
        [pltpu.VMEM((vir, vir), BF16)], (3, 4), 6, dot,
    )(block, first, over_first, pair_code, pair_count, dens)

    total = keep + swap(send, [(0, 1), (0, 1)]).astype(F32)
    upper = upper > 0.5
    below, above = total[: half // 2], total[half // 2 :]
    got = swap(jnp.where(upper, below, above).astype(BF16), split)
    total = jnp.where(upper, above, below) + got.astype(F32)
    out = total.astype(BF16)
    near = [m for _, m in along[:2]]
    masks = (near + [near[0] ^ near[1]])[::-1] if len(near) > 1 else near
    masks = sorted(masks, key=lambda m: -(m >> 1))
    for got in [swap(out, [(0, m), (0, m)]) for m in masks]:
        total = total + got.astype(F32)
    for mask in along[2:]:
        total = total + swap(total.astype(BF16), [mask, mask]).astype(F32)
    for masks in later:
        total = total + swap(total.astype(BF16), masks).astype(F32)
    mine = (total * (1.0 / (8.0 * groups * members))).astype(BF16)
    got = swap(mine, split)
    mine = jnp.concatenate([jnp.where(upper, got, mine), jnp.where(upper, mine, got)])
    other = swap(mine, [(0, 1), (0, 1)])

    unit = vir // 16
    cuts = (0, 8 * unit, vir)
    parts = [block[a:b] for a, b in zip(cuts, cuts[1:])]
    second = [turn(part, True) for part in parts]
    gamma = call(first_gamma_kernel, wide, (), (0, 1), 5, dot)(
        pair_code, pair_count, gamma, mt, first
    )
    bounce = [pltpu.VMEM((vir, vir // 2), BF16), pltpu.VMEM((vir // 2, vir), BF16)]
    gamma = call(second_gamma_kernel, wide, bounce, (0, 1), 6, dot)(
        pair_code, pair_count, block, over_second, gamma, second[0]
    )
    result = call(
        last_gamma_kernel, shape((vir, aux), BF16), [*out_scratch, pltpu.VMEM((vir // 2, aux), BF16), *bounce],
        (0, 1), 5 + len(second) - 1, dot, any_space,
    )(pair_code, pair_count, block, over_second, gamma, *second[1:])
    lagrangian = call(
        apply_kernel, shape((vir, aux), BF16), [pltpu.VMEM((vir, vir), BF16), *out_scratch], (), 3, dot,
        any_space,
    )(mine, other, block)
    return (result[None], lagrangian[None])


def solution(mesh):
    in_specs = (
        P(("grp", "mem"), None, None),
        P(("grp", "mem")),
        P(),
        P("grp", None, None),
        P("grp", None),
    )
    out_specs = (P(("grp", "mem"), None, None), P(("grp", "mem"), None, None))
    return jax.shard_map(
        per_device, mesh=mesh, in_specs=in_specs, out_specs=out_specs, check_vma=False
    )
```

```python
import functools

import jax
import jax.numpy as jnp
from jax import lax
from jax.experimental import pallas as pl
from jax.experimental.pallas import tpu as pltpu
from jax.sharding import PartitionSpec as P


STRIPS = 4
TILE = 128
F32 = jnp.float32
BF16 = jnp.bfloat16

VMEM = pl.BlockSpec(memory_space=pltpu.VMEM)
SMEM = pl.BlockSpec(memory_space=pltpu.SMEM)


def leads(member):
    return (member & 1) == ((member >> 1) & 1)


def first_round(member):
    return jnp.where(leads(member), 2, 1)


def turn(value, back):
    pairs = []
    for member in range(lax.axis_size("mem")):
        target = member ^ (1 if leads(member) else 2)
        pairs.append((target, member) if back else (member, target))
    return lax.ppermute(value, "mem", pairs)


def swap(value, masks):
    groups, members = lax.axis_size("grp"), lax.axis_size("mem")
    pairs = []
    for g in range(groups):
        for m in range(members):
            grp_mask, mem_mask = masks[0] if leads(m) else masks[1]
            pairs.append((g * members + m, (g ^ grp_mask) * members + (m ^ mem_mask)))
    return lax.ppermute(value, ("grp", "mem"), pairs)


def live(codes, counts, member, round_no):
    total = jnp.int32(0)
    for slot in range(codes.shape[0]):
        hit = (slot < counts[0, member]) & (codes[slot, 0, member] == round_no)
        total = total + hit.astype(jnp.int32)
    return total


def weights(codes, counts, round_no):
    me = lax.axis_index("mem")
    other = jnp.where(round_no == 0, me, me ^ round_no)
    own = live(codes, counts, me, round_no)
    far = live(codes, counts, other, round_no)
    return own.astype(F32), far.astype(F32)


def nt(a, b):
    return lax.dot_general(a, b, (((1,), (1,)), ((), ())), preferred_element_type=F32)


def nn(a, b):
    return jnp.dot(a, b, preferred_element_type=F32)


def early_kernel(
    splits, b_ref, row_ref, e_ref, first_ref, second_ref, codes, counts,
    one_ref, two_ref, dens_ref, gamma_ref, upper_ref, upper2_ref, amp
):
    vir, aux = b_ref.shape
    for split, ref in zip(splits, (upper_ref, upper2_ref)):
        mask = jnp.where(leads(lax.axis_index("mem")), split[0][0], split[1][0])
        ref[...] = jnp.full(ref.shape, ((lax.axis_index("grp") & mask) != 0).astype(F32))
    row = row_ref[...]
    sums = jnp.broadcast_to(row, (vir, vir)).T + row - e_ref[0]
    one_ref[...] = 1.0 / (sums - first_ref[0])
    two_ref[...] = 1.0 / (sums - second_ref[0])
    own, _ = weights(codes, counts, 0)
    half = vir // 2
    for at in (slice(0, half), slice(half, vir)):
        k = nt(b_ref[...], b_ref[at, :])
        amp[:, at] = (k / (sums[:, at] - e_ref[0])).astype(BF16)
    a = amp[...]
    dens_ref[...] = own * nn(a, a)
    for p in range(STRIPS):
        at = pl.ds(p * (aux // STRIPS), aux // STRIPS)
        gamma_ref[:, at] = (2.0 * own) * nn(a, b_ref[:, at])


def amp_part(at, b_ref, r_ref, over_ref):
    return (nt(b_ref[...], r_ref[...]) * over_ref[:, at]).astype(BF16)


def blocks(size):
    count = size // TILE
    return [(i, j) for i in range(count) for j in range(i, count)]


def density_kernel(b_ref, r_ref, over_ref, codes, counts, dens_in, mt_ref, keep_ref, send_ref, m_ref):
    vir = b_ref.shape[0]
    half = vir // 2
    me = lax.axis_index("mem")
    own, far = weights(codes, counts, first_round(me))
    for at in (slice(0, half), slice(half, vir)):
        mt = amp_part(at, b_ref, r_ref.at[at, :], over_ref)
        mt_ref[:, at] = mt
        m_ref[at, :] = mt.T
    high, low = slice(0, half), slice(half, vir)

    def sums(rows, columns):
        one = nn(mt_ref[rows, :], m_ref[:, columns])
        two = nn(m_ref[rows, :], mt_ref[:, columns])
        return dens_in[rows, columns] + own * one + far * two

    top, rest = sums(high, slice(0, vir)), sums(low, low)
    pieces = []
    for i, j in blocks(vir):
        if i * TILE < half:
            pieces.append(top[i * TILE : (i + 1) * TILE, j * TILE : (j + 1) * TILE])
        else:
            a, b = i * TILE - half, j * TILE - half
            pieces.append(rest[a : a + TILE, b : b + TILE])
    lead = leads(me)
    count = len(pieces) // 2
    for n in range(count):
        at = pl.ds(n * TILE, TILE)
        keep_ref[at, :] = jnp.where(lead, pieces[n], pieces[n + count])
        send_ref[at, :] = jnp.where(lead, pieces[n + count], pieces[n]).astype(BF16)


def first_gamma_kernel(codes, counts, gamma_in, mt_ref, r_ref, gamma_ref):
    own, far = weights(codes, counts, first_round(lax.axis_index("mem")))
    aux = gamma_ref.shape[1]
    for p in range(STRIPS):
        at = pl.ds(p * (aux // STRIPS), aux // STRIPS)
        gamma_ref[:, at] = gamma_in[:, at] + (own + far) * nn(mt_ref[...], r_ref[:, at])


def strips_out(out_ref, held, sems, strips, compute):
    step = held.shape[1] // strips
    copies = []
    for p in range(strips):
        at = pl.ds(p * step, step)
        held[:, at] = compute(at).astype(held.dtype)
        copies.append(pltpu.make_async_copy(held.at[:, at], out_ref.at[:, at], sems.at[p]))
        copies[-1].start()
    for copy in copies:
        copy.wait()


def joined(parts, held):
    start = 0
    for part in parts:
        held[start : start + part.shape[0], :] = part[...]
        start += part.shape[0]


def flat_amp(at, b_ref, r_ref, over_ref, m_ref):
    m_ref[...] = (nt(r_ref[...], b_ref[...]) * over_ref[at, :]).astype(BF16)
    return m_ref[...].T


def next_gamma_kernel(cut, codes, counts, b_ref, over_ref, gamma_in, *refs):
    parts, (gamma_ref, r_ref, mt_ref, m_ref) = refs[:-4], refs[-4:]
    own, far = weights(codes, counts, 3 - first_round(lax.axis_index("mem")))
    if len(parts) == 1:
        r_ref = parts[0]
    else:
        joined(parts, r_ref)
    mt_ref[...] = flat_amp(slice(cut, cut + r_ref.shape[0]), b_ref, r_ref, over_ref, m_ref)
    aux = gamma_ref.shape[1]
    for p in range(STRIPS):
        at = pl.ds(p * (aux // STRIPS), aux // STRIPS)
        gamma_ref[:, at] = gamma_in[:, at] + (own + far) * nn(mt_ref[...], r_ref[:, at])


def last_gamma_kernel(codes, counts, b_ref, over_ref, gamma_in, r_ref, out_ref, held, sems, mt_ref, m_ref):
    own, far = weights(codes, counts, 3 - first_round(lax.axis_index("mem")))
    vir = b_ref.shape[0]
    mt_ref[...] = flat_amp(slice(vir - r_ref.shape[0], vir), b_ref, r_ref, over_ref, m_ref)
    strips_out(
        out_ref, held, sems, STRIPS, lambda at: gamma_in[:, at] + (own + far) * nn(mt_ref[...], r_ref[:, at])
    )


def apply_kernel(mine_ref, other_ref, b_ref, out_ref, tile, held, sems):
    lead = leads(lax.axis_index("mem"))
    names = blocks(tile.shape[0])
    half = len(names) // 2
    for n, (i, j) in enumerate(names):
        at = pl.ds((n % half) * TILE, TILE)
        low, high = (mine_ref, other_ref) if n < half else (other_ref, mine_ref)
        block = jnp.where(lead, low[at, :].astype(F32), high[at, :].astype(F32)).astype(BF16)
        tile[pl.ds(i * TILE, TILE), pl.ds(j * TILE, TILE)] = block
        if i != j:
            tile[pl.ds(j * TILE, TILE), pl.ds(i * TILE, TILE)] = block.T
    strips_out(out_ref, held, sems, STRIPS, lambda at: nn(tile[...], b_ref[:, at]))


def call(kernel, outs, scratch=(), smem=(), count=0, flops=0, out_spec=VMEM):
    return lambda *args: kernel_call(kernel, outs, scratch, smem, count, flops, out_spec)(*args)


def kernel_call(kernel, outs, scratch, smem, count, flops, out_spec):
    return pl.pallas_call(
        kernel,
        out_shape=outs,
        in_specs=[SMEM if i in smem else VMEM for i in range(count)],
        out_specs=jax.tree.map(lambda _: out_spec, outs),
        scratch_shapes=scratch,
        compiler_params=pltpu.CompilerParams(vmem_limit_bytes=12 << 20),
        cost_estimate=pl.CostEstimate(flops=flops, bytes_accessed=1 << 20, transcendentals=0),
    )


def per_device(factors, occ_energy, vir_energy, pair_code, pair_count):
    return body(factors[0], occ_energy, vir_energy, pair_code, pair_count)


def body(block, occ_energy, vir_energy, pair_code, pair_count):
    vir, aux = block.shape
    members, groups = lax.axis_size("mem"), lax.axis_size("grp")
    shape = jax.ShapeDtypeStruct
    square = shape((vir, vir), F32)
    wide = shape((vir, aux), F32)
    dot = 2 * vir * vir * aux
    out_scratch = [pltpu.VMEM((vir, aux), BF16), pltpu.SemaphoreType.DMA((STRIPS,))]
    any_space = pl.BlockSpec(memory_space=pl.ANY)

    first_energy = turn(occ_energy, False).astype(F32)
    first = turn(block, False)
    second_energy = turn(occ_energy, True).astype(F32)

    pair_code = jnp.transpose(pair_code, (2, 0, 1))
    energy = occ_energy.astype(F32)
    row = vir_energy.astype(F32).reshape(1, vir)
    half = len(blocks(vir)) * TILE // 2
    along = [(0, 3)] + [(0, (1 << k) | 3) for k in range(2, members.bit_length() - 1)]
    across = [(1 << k, 0) for k in range(groups.bit_length() - 1)]
    splits = list(zip(across, across[1:] + across[:1]))
    splits, later = splits[:2], splits[2:]
    over_first, over_second, dens, gamma, *uppers = call(
        functools.partial(early_kernel, splits),
        (square, square, square, wide, shape((half // 2, TILE), F32), shape((half // 4, TILE), F32)),
        [pltpu.VMEM((vir, vir), BF16)],
        (2, 3, 4, 5, 6), 7, 2 * dot,
    )(block, row, energy, first_energy, second_energy, pair_code, pair_count)

    mt, keep, send = call(
        density_kernel,
        (shape((vir, vir), BF16), shape((half, TILE), F32), shape((half, TILE), BF16)),
        [pltpu.VMEM((vir, vir), BF16)], (3, 4), 6, dot,
    )(block, first, over_first, pair_code, pair_count, dens)

    total = keep + swap(send, [(0, 1), (0, 1)]).astype(F32)
    uppers = [upper > 0.5 for upper in uppers]
    for k, (split, upper) in enumerate(zip(splits, uppers)):
        below, above = total[: half // 2 >> k], total[half // 2 >> k :]
        got = swap(jnp.where(upper, below, above).astype(BF16), split)
        total = jnp.where(upper, above, below) + got.astype(F32)
    for masks in later:
        total = total + swap(total.astype(BF16), masks).astype(F32)
    out = total.astype(BF16)
    near = [m for _, m in along[:2]]
    masks = (near + [near[0] ^ near[1]])[::-1] if len(near) > 1 else near
    masks = sorted(masks, key=lambda m: -(m >> 1))
    for got in [swap(out, [(0, m), (0, m)]) for m in masks]:
        total = total + got.astype(F32)
    for mask in along[2:]:
        total = total + swap(total.astype(BF16), [mask, mask]).astype(F32)
    mine = (total * (1.0 / (8.0 * groups * members))).astype(BF16)
    for k, (split, upper) in reversed(list(enumerate(zip(splits, uppers)))):
        got = swap(mine, split)
        mine = jnp.concatenate([jnp.where(upper, got, mine), jnp.where(upper, mine, got)])
    other = swap(mine, [(0, 1), (0, 1)])

    unit = vir // 32
    cuts = (0, 16 * unit, 20 * unit, 28 * unit, vir)
    parts = [block[a:b] for a, b in zip(cuts, cuts[1:])]
    second = [turn(part, True) for part in parts]
    gamma = call(first_gamma_kernel, wide, (), (0, 1), 5, dot)(
        pair_code, pair_count, gamma, mt, first
    )

    def bounce(rows):
        return [pltpu.VMEM((vir, rows), BF16), pltpu.VMEM((rows, vir), BF16)]

    for a, b in ((0, 1), (1, 3)):
        rows = cuts[b] - cuts[a]
        gamma = call(
            functools.partial(next_gamma_kernel, cuts[a]), wide, [pltpu.VMEM((rows, aux), BF16), *bounce(rows)],
            (0, 1), 5 + b - a, dot,
        )(pair_code, pair_count, block, over_second, gamma, *second[a:b])
    result = call(
        last_gamma_kernel, shape((vir, aux), BF16), [*out_scratch, *bounce(vir - cuts[3])],
        (0, 1), 6, dot, any_space,
    )(pair_code, pair_count, block, over_second, gamma, second[3])
    lagrangian = call(
        apply_kernel, shape((vir, aux), BF16), [pltpu.VMEM((vir, vir), BF16), *out_scratch], (), 3, dot,
        any_space,
    )(mine, other, block)
    return (result[None], lagrangian[None])


def solution(mesh):
    in_specs = (
        P(("grp", "mem"), None, None),
        P(("grp", "mem")),
        P(),
        P("grp", None, None),
        P("grp", None),
    )
    out_specs = (P(("grp", "mem"), None, None), P(("grp", "mem"), None, None))
    return jax.shard_map(
        per_device, mesh=mesh, in_specs=in_specs, out_specs=out_specs, check_vma=False
    )
```

```python
import functools

import jax
import jax.numpy as jnp
from jax import lax
from jax.experimental import pallas as pl
from jax.experimental.pallas import tpu as pltpu
from jax.sharding import PartitionSpec as P


STRIPS = 4
TILE = 128
F32 = jnp.float32
BF16 = jnp.bfloat16

VMEM = pl.BlockSpec(memory_space=pltpu.VMEM)
SMEM = pl.BlockSpec(memory_space=pltpu.SMEM)


def leads(member):
    return (member & 1) == ((member >> 1) & 1)


def first_round(member):
    return jnp.where(leads(member), 2, 1)


def turn(value, back):
    pairs = []
    for member in range(lax.axis_size("mem")):
        target = member ^ (1 if leads(member) else 2)
        pairs.append((target, member) if back else (member, target))
    return lax.ppermute(value, "mem", pairs)


def swap(value, masks):
    groups, members = lax.axis_size("grp"), lax.axis_size("mem")
    pairs = []
    for g in range(groups):
        for m in range(members):
            grp_mask, mem_mask = masks[0] if leads(m) else masks[1]
            pairs.append((g * members + m, (g ^ grp_mask) * members + (m ^ mem_mask)))
    return lax.ppermute(value, ("grp", "mem"), pairs)


def live(codes, counts, member, round_no):
    total = jnp.int32(0)
    for slot in range(codes.shape[0]):
        hit = (slot < counts[0, member]) & (codes[slot, 0, member] == round_no)
        total = total + hit.astype(jnp.int32)
    return total


def weights(codes, counts, round_no):
    me = lax.axis_index("mem")
    other = jnp.where(round_no == 0, me, me ^ round_no)
    own = live(codes, counts, me, round_no)
    far = live(codes, counts, other, round_no)
    return own.astype(F32), far.astype(F32)


def nt(a, b):
    return lax.dot_general(a, b, (((1,), (1,)), ((), ())), preferred_element_type=F32)


def nn(a, b):
    return jnp.dot(a, b, preferred_element_type=F32)


def early_kernel(
    splits, b_ref, row_ref, e_ref, first_ref, second_ref, codes, counts,
    one_ref, two_ref, dens_ref, gamma_ref, upper_ref, upper2_ref, amp
):
    vir, aux = b_ref.shape
    for split, ref in zip(splits, (upper_ref, upper2_ref)):
        mask = jnp.where(leads(lax.axis_index("mem")), split[0][0], split[1][0])
        ref[...] = jnp.full(ref.shape, ((lax.axis_index("grp") & mask) != 0).astype(F32))
    row = row_ref[...]
    sums = jnp.broadcast_to(row, (vir, vir)).T + row - e_ref[0]
    one_ref[...] = 1.0 / (sums - first_ref[0])
    two_ref[...] = 1.0 / (sums - second_ref[0])
    own, _ = weights(codes, counts, 0)
    half = vir // 2
    for at in (slice(0, half), slice(half, vir)):
        k = nt(b_ref[...], b_ref[at, :])
        amp[:, at] = (k / (sums[:, at] - e_ref[0])).astype(BF16)
    a = amp[...]
    dens_ref[...] = own * nn(a, a)
    for p in range(STRIPS):
        at = pl.ds(p * (aux // STRIPS), aux // STRIPS)
        gamma_ref[:, at] = (2.0 * own) * nn(a, b_ref[:, at])


def amp_part(at, b_ref, r_ref, over_ref):
    return (nt(b_ref[...], r_ref[...]) * over_ref[:, at]).astype(BF16)


def blocks(size):
    count = size // TILE
    return [(i, j) for i in range(count) for j in range(i, count)]


def density_kernel(b_ref, r_ref, over_ref, codes, counts, dens_in, mt_ref, keep_ref, send_ref, m_ref):
    vir = b_ref.shape[0]
    half = vir // 2
    me = lax.axis_index("mem")
    own, far = weights(codes, counts, first_round(me))
    for at in (slice(0, half), slice(half, vir)):
        mt = amp_part(at, b_ref, r_ref.at[at, :], over_ref)
        mt_ref[:, at] = mt
        m_ref[at, :] = mt.T
    high, low = slice(0, half), slice(half, vir)

    def sums(rows, columns):
        one = nn(mt_ref[rows, :], m_ref[:, columns])
        two = nn(m_ref[rows, :], mt_ref[:, columns])
        return dens_in[rows, columns] + own * one + far * two

    top, rest = sums(high, slice(0, vir)), sums(low, low)
    pieces = []
    for i, j in blocks(vir):
        if i * TILE < half:
            pieces.append(top[i * TILE : (i + 1) * TILE, j * TILE : (j + 1) * TILE])
        else:
            a, b = i * TILE - half, j * TILE - half
            pieces.append(rest[a : a + TILE, b : b + TILE])
    lead = leads(me)
    count = len(pieces) // 2
    for n in range(count):
        at = pl.ds(n * TILE, TILE)
        keep_ref[at, :] = jnp.where(lead, pieces[n], pieces[n + count])
        send_ref[at, :] = jnp.where(lead, pieces[n + count], pieces[n]).astype(BF16)


def first_gamma_kernel(codes, counts, gamma_in, mt_ref, r_ref, gamma_ref):
    own, far = weights(codes, counts, first_round(lax.axis_index("mem")))
    aux = gamma_ref.shape[1]
    for p in range(STRIPS):
        at = pl.ds(p * (aux // STRIPS), aux // STRIPS)
        gamma_ref[:, at] = gamma_in[:, at] + (own + far) * nn(mt_ref[...], r_ref[:, at])


def strips_out(out_ref, held, sems, strips, compute):
    step = held.shape[1] // strips
    copies = []
    for p in range(strips):
        at = pl.ds(p * step, step)
        held[:, at] = compute(at).astype(held.dtype)
        copies.append(pltpu.make_async_copy(held.at[:, at], out_ref.at[:, at], sems.at[p]))
        copies[-1].start()
    for copy in copies:
        copy.wait()


def joined(parts, held):
    start = 0
    for part in parts:
        held[start : start + part.shape[0], :] = part[...]
        start += part.shape[0]


def flat_amp(at, b_ref, r_ref, over_ref, m_ref):
    m_ref[...] = (nt(r_ref[...], b_ref[...]) * over_ref[at, :]).astype(BF16)
    return m_ref[...].T


def second_gamma_kernel(codes, counts, b_ref, over_ref, gamma_in, r_ref, gamma_ref, mt_ref, m_ref):
    own, far = weights(codes, counts, 3 - first_round(lax.axis_index("mem")))
    mt_ref[...] = flat_amp(slice(0, r_ref.shape[0]), b_ref, r_ref, over_ref, m_ref)
    aux = gamma_ref.shape[1]
    for p in range(STRIPS):
        at = pl.ds(p * (aux // STRIPS), aux // STRIPS)
        gamma_ref[:, at] = gamma_in[:, at] + (own + far) * nn(mt_ref[...], r_ref[:, at])


def last_gamma_kernel(codes, counts, b_ref, over_ref, gamma_in, *refs):
    parts, (out_ref, held, sems, r_ref, mt_ref, m_ref) = refs[:-6], refs[-6:]
    own, far = weights(codes, counts, 3 - first_round(lax.axis_index("mem")))
    joined(parts, r_ref)
    vir = b_ref.shape[0]
    mt_ref[...] = flat_amp(slice(vir - r_ref.shape[0], vir), b_ref, r_ref, over_ref, m_ref)
    strips_out(
        out_ref, held, sems, STRIPS, lambda at: gamma_in[:, at] + (own + far) * nn(mt_ref[...], r_ref[:, at])
    )


def apply_kernel(mine_ref, other_ref, b_ref, out_ref, tile, held, sems):
    lead = leads(lax.axis_index("mem"))
    names = blocks(tile.shape[0])
    half = len(names) // 2
    for n, (i, j) in enumerate(names):
        at = pl.ds((n % half) * TILE, TILE)
        low, high = (mine_ref, other_ref) if n < half else (other_ref, mine_ref)
        block = jnp.where(lead, low[at, :].astype(F32), high[at, :].astype(F32)).astype(BF16)
        tile[pl.ds(i * TILE, TILE), pl.ds(j * TILE, TILE)] = block
        if i != j:
            tile[pl.ds(j * TILE, TILE), pl.ds(i * TILE, TILE)] = block.T
    strips_out(out_ref, held, sems, STRIPS, lambda at: nn(tile[...], b_ref[:, at]))


def call(kernel, outs, scratch=(), smem=(), count=0, flops=0, out_spec=VMEM):
    return lambda *args: kernel_call(kernel, outs, scratch, smem, count, flops, out_spec)(*args)


def kernel_call(kernel, outs, scratch, smem, count, flops, out_spec):
    return pl.pallas_call(
        kernel,
        out_shape=outs,
        in_specs=[SMEM if i in smem else VMEM for i in range(count)],
        out_specs=jax.tree.map(lambda _: out_spec, outs),
        scratch_shapes=scratch,
        compiler_params=pltpu.CompilerParams(vmem_limit_bytes=12 << 20),
        cost_estimate=pl.CostEstimate(flops=flops, bytes_accessed=1 << 20, transcendentals=0),
    )


def per_device(factors, occ_energy, vir_energy, pair_code, pair_count):
    return body(factors[0], occ_energy, vir_energy, pair_code, pair_count)


def body(block, occ_energy, vir_energy, pair_code, pair_count):
    vir, aux = block.shape
    members, groups = lax.axis_size("mem"), lax.axis_size("grp")
    shape = jax.ShapeDtypeStruct
    square = shape((vir, vir), F32)
    wide = shape((vir, aux), F32)
    dot = 2 * vir * vir * aux
    out_scratch = [pltpu.VMEM((vir, aux), BF16), pltpu.SemaphoreType.DMA((STRIPS,))]
    any_space = pl.BlockSpec(memory_space=pl.ANY)

    first_energy = turn(occ_energy, False).astype(F32)
    first = turn(block, False)
    second_energy = turn(occ_energy, True).astype(F32)

    pair_code = jnp.transpose(pair_code, (2, 0, 1))
    energy = occ_energy.astype(F32)
    row = vir_energy.astype(F32).reshape(1, vir)
    half = len(blocks(vir)) * TILE // 2
    along = [(0, 3)] + [(0, (1 << k) | 3) for k in range(2, members.bit_length() - 1)]
    across = [(1 << k, 0) for k in range(groups.bit_length() - 1)]
    splits = list(zip(across, across[1:] + across[:1]))
    splits, later = splits[:2], splits[2:]
    over_first, over_second, dens, gamma, *uppers = call(
        functools.partial(early_kernel, splits),
        (square, square, square, wide, shape((half // 2, TILE), F32), shape((half // 4, TILE), F32)),
        [pltpu.VMEM((vir, vir), BF16)],
        (2, 3, 4, 5, 6), 7, 2 * dot,
    )(block, row, energy, first_energy, second_energy, pair_code, pair_count)

    mt, keep, send = call(
        density_kernel,
        (shape((vir, vir), BF16), shape((half, TILE), F32), shape((half, TILE), BF16)),
        [pltpu.VMEM((vir, vir), BF16)], (3, 4), 6, dot,
    )(block, first, over_first, pair_code, pair_count, dens)

    total = keep + swap(send, [(0, 1), (0, 1)]).astype(F32)
    uppers = [upper > 0.5 for upper in uppers]
    for k, (split, upper) in enumerate(zip(splits, uppers)):
        below, above = total[: half // 2 >> k], total[half // 2 >> k :]
        got = swap(jnp.where(upper, below, above).astype(BF16), split)
        total = jnp.where(upper, above, below) + got.astype(F32)
    for masks in later:
        total = total + swap(total.astype(BF16), masks).astype(F32)
    out = total.astype(BF16)
    near = [m for _, m in along[:2]]
    masks = (near + [near[0] ^ near[1]])[::-1] if len(near) > 1 else near
    masks = sorted(masks, key=lambda m: -(m >> 1))
    for got in [swap(out, [(0, m), (0, m)]) for m in masks]:
        total = total + got.astype(F32)
    for mask in along[2:]:
        total = total + swap(total.astype(BF16), [mask, mask]).astype(F32)
    mine = (total * (1.0 / (8.0 * groups * members))).astype(BF16)
    for k, (split, upper) in reversed(list(enumerate(zip(splits, uppers)))):
        got = swap(mine, split)
        mine = jnp.concatenate([jnp.where(upper, got, mine), jnp.where(upper, mine, got)])
    other = swap(mine, [(0, 1), (0, 1)])

    unit = vir // 16
    cuts = (0, 8 * unit, 11 * unit, vir)
    parts = [block[a:b] for a, b in zip(cuts, cuts[1:])]
    second = [turn(part, True) for part in parts]
    gamma = call(first_gamma_kernel, wide, (), (0, 1), 5, dot)(
        pair_code, pair_count, gamma, mt, first
    )
    bounce = [pltpu.VMEM((vir, vir // 2), BF16), pltpu.VMEM((vir // 2, vir), BF16)]
    gamma = call(second_gamma_kernel, wide, bounce, (0, 1), 6, dot)(
        pair_code, pair_count, block, over_second, gamma, second[0]
    )
    result = call(
        last_gamma_kernel, shape((vir, aux), BF16), [*out_scratch, pltpu.VMEM((vir // 2, aux), BF16), *bounce],
        (0, 1), 7, dot, any_space,
    )(pair_code, pair_count, block, over_second, gamma, *second[1:])
    lagrangian = call(
        apply_kernel, shape((vir, aux), BF16), [pltpu.VMEM((vir, vir), BF16), *out_scratch], (), 3, dot,
        any_space,
    )(mine, other, block)
    return (result[None], lagrangian[None])


def solution(mesh):
    in_specs = (
        P(("grp", "mem"), None, None),
        P(("grp", "mem")),
        P(),
        P("grp", None, None),
        P("grp", None),
    )
    out_specs = (P(("grp", "mem"), None, None), P(("grp", "mem"), None, None))
    return jax.shard_map(
        per_device, mesh=mesh, in_specs=in_specs, out_specs=out_specs, check_vma=False
    )
```

```python
import functools

import jax
import jax.numpy as jnp
from jax import lax
from jax.experimental import pallas as pl
from jax.experimental.pallas import tpu as pltpu
from jax.sharding import PartitionSpec as P


STRIPS = 4
TILE = 128
F32 = jnp.float32
BF16 = jnp.bfloat16

VMEM = pl.BlockSpec(memory_space=pltpu.VMEM)
SMEM = pl.BlockSpec(memory_space=pltpu.SMEM)


def leads(member):
    return (member & 1) == ((member >> 1) & 1)


def first_round(member):
    return jnp.where(leads(member), 2, 1)


def turn(value, back):
    pairs = []
    for member in range(lax.axis_size("mem")):
        target = member ^ (1 if leads(member) else 2)
        pairs.append((target, member) if back else (member, target))
    return lax.ppermute(value, "mem", pairs)


def swap(value, masks):
    groups, members = lax.axis_size("grp"), lax.axis_size("mem")
    pairs = []
    for g in range(groups):
        for m in range(members):
            grp_mask, mem_mask = masks[0] if leads(m) else masks[1]
            pairs.append((g * members + m, (g ^ grp_mask) * members + (m ^ mem_mask)))
    return lax.ppermute(value, ("grp", "mem"), pairs)


def live(codes, counts, member, round_no):
    total = jnp.int32(0)
    for slot in range(codes.shape[0]):
        hit = (slot < counts[0, member]) & (codes[slot, 0, member] == round_no)
        total = total + hit.astype(jnp.int32)
    return total


def weights(codes, counts, round_no):
    me = lax.axis_index("mem")
    other = jnp.where(round_no == 0, me, me ^ round_no)
    own = live(codes, counts, me, round_no)
    far = live(codes, counts, other, round_no)
    return own.astype(F32), far.astype(F32)


def nt(a, b):
    return lax.dot_general(a, b, (((1,), (1,)), ((), ())), preferred_element_type=F32)


def nn(a, b):
    return jnp.dot(a, b, preferred_element_type=F32)


def early_kernel(
    splits, b_ref, row_ref, e_ref, first_ref, second_ref, codes, counts,
    one_ref, two_ref, dens_ref, gamma_ref, upper_ref, upper2_ref, amp
):
    vir, aux = b_ref.shape
    for split, ref in zip(splits, (upper_ref, upper2_ref)):
        mask = jnp.where(leads(lax.axis_index("mem")), split[0][0], split[1][0])
        ref[...] = jnp.full(ref.shape, ((lax.axis_index("grp") & mask) != 0).astype(F32))
    row = row_ref[...]
    sums = jnp.broadcast_to(row, (vir, vir)).T + row - e_ref[0]
    one_ref[...] = 1.0 / (sums - first_ref[0])
    two_ref[...] = 1.0 / (sums - second_ref[0])
    own, _ = weights(codes, counts, 0)
    half = vir // 2
    for at in (slice(0, half), slice(half, vir)):
        k = nt(b_ref[...], b_ref[at, :])
        amp[:, at] = (k / (sums[:, at] - e_ref[0])).astype(BF16)
    a = amp[...]
    dens_ref[...] = own * nn(a, a)
    for p in range(STRIPS):
        at = pl.ds(p * (aux // STRIPS), aux // STRIPS)
        gamma_ref[:, at] = (2.0 * own) * nn(a, b_ref[:, at])


def amp_part(at, b_ref, r_ref, over_ref):
    return (nt(b_ref[...], r_ref[...]) * over_ref[:, at]).astype(BF16)


def blocks(size):
    count = size // TILE
    return [(i, j) for i in range(count) for j in range(i, count)]


def density_kernel(b_ref, r_ref, over_ref, codes, counts, dens_in, mt_ref, keep_ref, send_ref, m_ref):
    vir = b_ref.shape[0]
    half = vir // 2
    me = lax.axis_index("mem")
    own, far = weights(codes, counts, first_round(me))
    for at in (slice(0, half), slice(half, vir)):
        mt = amp_part(at, b_ref, r_ref.at[at, :], over_ref)
        mt_ref[:, at] = mt
        m_ref[at, :] = mt.T
    high, low = slice(0, half), slice(half, vir)

    def sums(rows, columns):
        one = nn(mt_ref[rows, :], m_ref[:, columns])
        two = nn(m_ref[rows, :], mt_ref[:, columns])
        return dens_in[rows, columns] + own * one + far * two

    top, rest = sums(high, slice(0, vir)), sums(low, low)
    pieces = []
    for i, j in blocks(vir):
        if i * TILE < half:
            pieces.append(top[i * TILE : (i + 1) * TILE, j * TILE : (j + 1) * TILE])
        else:
            a, b = i * TILE - half, j * TILE - half
            pieces.append(rest[a : a + TILE, b : b + TILE])
    lead = leads(me)
    count = len(pieces) // 2
    for n in range(count):
        at = pl.ds(n * TILE, TILE)
        keep_ref[at, :] = jnp.where(lead, pieces[n], pieces[n + count])
        send_ref[at, :] = jnp.where(lead, pieces[n + count], pieces[n]).astype(BF16)


def first_gamma_kernel(codes, counts, gamma_in, mt_ref, r_ref, gamma_ref):
    own, far = weights(codes, counts, first_round(lax.axis_index("mem")))
    aux = gamma_ref.shape[1]
    for p in range(STRIPS):
        at = pl.ds(p * (aux // STRIPS), aux // STRIPS)
        gamma_ref[:, at] = gamma_in[:, at] + (own + far) * nn(mt_ref[...], r_ref[:, at])


def strips_out(out_ref, held, sems, strips, compute):
    step = held.shape[1] // strips
    copies = []
    for p in range(strips):
        at = pl.ds(p * step, step)
        held[:, at] = compute(at).astype(held.dtype)
        copies.append(pltpu.make_async_copy(held.at[:, at], out_ref.at[:, at], sems.at[p]))
        copies[-1].start()
    for copy in copies:
        copy.wait()


def joined(parts, held):
    start = 0
    for part in parts:
        held[start : start + part.shape[0], :] = part[...]
        start += part.shape[0]


def flat_amp(at, b_ref, r_ref, over_ref, m_ref):
    m_ref[...] = (nt(r_ref[...], b_ref[...]) * over_ref[at, :]).astype(BF16)
    return m_ref[...].T


def second_gamma_kernel(codes, counts, b_ref, over_ref, gamma_in, r_ref, gamma_ref, mt_ref, m_ref):
    own, far = weights(codes, counts, 3 - first_round(lax.axis_index("mem")))
    mt_ref[...] = flat_amp(slice(0, r_ref.shape[0]), b_ref, r_ref, over_ref, m_ref)
    aux = gamma_ref.shape[1]
    for p in range(STRIPS):
        at = pl.ds(p * (aux // STRIPS), aux // STRIPS)
        gamma_ref[:, at] = gamma_in[:, at] + (own + far) * nn(mt_ref[...], r_ref[:, at])


def amp_kernel(b_ref, over_ref, *refs):
    parts, (mt_ref, r_ref, m_ref) = refs[:-3], refs[-3:]
    joined(parts, r_ref)
    vir = b_ref.shape[0]
    mt_ref[...] = flat_amp(slice(vir - r_ref.shape[0], vir), b_ref, r_ref, over_ref, m_ref)


def last_gamma_kernel(codes, counts, gamma_in, mt_ref, r_ref, out_ref, held, sems):
    own, far = weights(codes, counts, 3 - first_round(lax.axis_index("mem")))
    strips_out(
        out_ref, held, sems, STRIPS, lambda at: gamma_in[:, at] + (own + far) * nn(mt_ref[...], r_ref[:, at])
    )


def apply_kernel(mine_ref, other_ref, b_ref, out_ref, tile, held, sems):
    lead = leads(lax.axis_index("mem"))
    names = blocks(tile.shape[0])
    half = len(names) // 2
    for n, (i, j) in enumerate(names):
        at = pl.ds((n % half) * TILE, TILE)
        low, high = (mine_ref, other_ref) if n < half else (other_ref, mine_ref)
        block = jnp.where(lead, low[at, :].astype(F32), high[at, :].astype(F32)).astype(BF16)
        tile[pl.ds(i * TILE, TILE), pl.ds(j * TILE, TILE)] = block
        if i != j:
            tile[pl.ds(j * TILE, TILE), pl.ds(i * TILE, TILE)] = block.T
    strips_out(out_ref, held, sems, STRIPS, lambda at: nn(tile[...], b_ref[:, at]))


def call(kernel, outs, scratch=(), smem=(), count=0, flops=0, out_spec=VMEM):
    return lambda *args: kernel_call(kernel, outs, scratch, smem, count, flops, out_spec)(*args)


def kernel_call(kernel, outs, scratch, smem, count, flops, out_spec):
    return pl.pallas_call(
        kernel,
        out_shape=outs,
        in_specs=[SMEM if i in smem else VMEM for i in range(count)],
        out_specs=jax.tree.map(lambda _: out_spec, outs),
        scratch_shapes=scratch,
        compiler_params=pltpu.CompilerParams(vmem_limit_bytes=12 << 20),
        cost_estimate=pl.CostEstimate(flops=flops, bytes_accessed=1 << 20, transcendentals=0),
    )


def per_device(factors, occ_energy, vir_energy, pair_code, pair_count):
    return body(factors[0], occ_energy, vir_energy, pair_code, pair_count)


def body(block, occ_energy, vir_energy, pair_code, pair_count):
    vir, aux = block.shape
    members, groups = lax.axis_size("mem"), lax.axis_size("grp")
    shape = jax.ShapeDtypeStruct
    square = shape((vir, vir), F32)
    wide = shape((vir, aux), F32)
    dot = 2 * vir * vir * aux
    out_scratch = [pltpu.VMEM((vir, aux), BF16), pltpu.SemaphoreType.DMA((STRIPS,))]
    any_space = pl.BlockSpec(memory_space=pl.ANY)

    first_energy = turn(occ_energy, False).astype(F32)
    first = turn(block, False)
    second_energy = turn(occ_energy, True).astype(F32)

    pair_code = jnp.transpose(pair_code, (2, 0, 1))
    energy = occ_energy.astype(F32)
    row = vir_energy.astype(F32).reshape(1, vir)
    half = len(blocks(vir)) * TILE // 2
    along = [(0, 3)] + [(0, (1 << k) | 3) for k in range(2, members.bit_length() - 1)]
    across = [(1 << k, 0) for k in range(groups.bit_length() - 1)]
    splits = list(zip(across, across[1:] + across[:1]))
    splits, later = splits[:2], splits[2:]
    over_first, over_second, dens, gamma, *uppers = call(
        functools.partial(early_kernel, splits),
        (square, square, square, wide, shape((half // 2, TILE), F32), shape((half // 4, TILE), F32)),
        [pltpu.VMEM((vir, vir), BF16)],
        (2, 3, 4, 5, 6), 7, 2 * dot,
    )(block, row, energy, first_energy, second_energy, pair_code, pair_count)

    mt, keep, send = call(
        density_kernel,
        (shape((vir, vir), BF16), shape((half, TILE), F32), shape((half, TILE), BF16)),
        [pltpu.VMEM((vir, vir), BF16)], (3, 4), 6, dot,
    )(block, first, over_first, pair_code, pair_count, dens)

    total = keep + swap(send, [(0, 1), (0, 1)]).astype(F32)
    uppers = [upper > 0.5 for upper in uppers]
    for k, (split, upper) in enumerate(zip(splits, uppers)):
        below, above = total[: half // 2 >> k], total[half // 2 >> k :]
        got = swap(jnp.where(upper, below, above).astype(BF16), split)
        total = jnp.where(upper, above, below) + got.astype(F32)
    for masks in later:
        total = total + swap(total.astype(BF16), masks).astype(F32)
    out = total.astype(BF16)
    near = [m for _, m in along[:2]]
    masks = (near + [near[0] ^ near[1]])[::-1] if len(near) > 1 else near
    masks = sorted(masks, key=lambda m: -(m >> 1))
    for got in [swap(out, [(0, m), (0, m)]) for m in masks]:
        total = total + got.astype(F32)
    for mask in along[2:]:
        total = total + swap(total.astype(BF16), [mask, mask]).astype(F32)
    mine = (total * (1.0 / (8.0 * groups * members))).astype(BF16)
    for k, (split, upper) in reversed(list(enumerate(zip(splits, uppers)))):
        got = swap(mine, split)
        mine = jnp.concatenate([jnp.where(upper, got, mine), jnp.where(upper, mine, got)])
    other = swap(mine, [(0, 1), (0, 1)])

    unit = vir // 16
    cuts = (0, 8 * unit, 11 * unit, vir)
    parts = [block[a:b] for a, b in zip(cuts, cuts[1:])]
    second = [turn(part, True) for part in parts]
    gamma = call(first_gamma_kernel, wide, (), (0, 1), 5, dot)(
        pair_code, pair_count, gamma, mt, first
    )
    bounce = [pltpu.VMEM((vir, vir // 2), BF16), pltpu.VMEM((vir // 2, vir), BF16)]
    gamma = call(second_gamma_kernel, wide, bounce, (0, 1), 6, dot)(
        pair_code, pair_count, block, over_second, gamma, second[0]
    )
    rest, rows = call(
        amp_kernel, (shape((vir, vir // 2), BF16), shape((vir // 2, aux), BF16)), bounce[1:], (), 4, dot // 2
    )(block, over_second, *second[1:])
    result = call(last_gamma_kernel, shape((vir, aux), BF16), out_scratch, (0, 1), 5, dot // 2, any_space)(
        pair_code, pair_count, gamma, rest, rows
    )
    lagrangian = call(
        apply_kernel, shape((vir, aux), BF16), [pltpu.VMEM((vir, vir), BF16), *out_scratch], (), 3, dot,
        any_space,
    )(mine, other, block)
    return (result[None], lagrangian[None])


def solution(mesh):
    in_specs = (
        P(("grp", "mem"), None, None),
        P(("grp", "mem")),
        P(),
        P("grp", None, None),
        P("grp", None),
    )
    out_specs = (P(("grp", "mem"), None, None), P(("grp", "mem"), None, None))
    return jax.shard_map(
        per_device, mesh=mesh, in_specs=in_specs, out_specs=out_specs, check_vma=False
    )
```

```python
import functools

import jax
import jax.numpy as jnp
from jax import lax
from jax.experimental import pallas as pl
from jax.experimental.pallas import tpu as pltpu
from jax.sharding import PartitionSpec as P


STRIPS = 4
TILE = 128
F32 = jnp.float32
BF16 = jnp.bfloat16

VMEM = pl.BlockSpec(memory_space=pltpu.VMEM)
SMEM = pl.BlockSpec(memory_space=pltpu.SMEM)


def leads(member):
    return (member & 1) == ((member >> 1) & 1)


def first_round(member):
    return jnp.where(leads(member), 2, 1)


def turn(value, back):
    pairs = []
    for member in range(lax.axis_size("mem")):
        target = member ^ (1 if leads(member) else 2)
        pairs.append((target, member) if back else (member, target))
    return lax.ppermute(value, "mem", pairs)


def swap(value, masks):
    groups, members = lax.axis_size("grp"), lax.axis_size("mem")
    pairs = []
    for g in range(groups):
        for m in range(members):
            grp_mask, mem_mask = masks[0] if leads(m) else masks[1]
            pairs.append((g * members + m, (g ^ grp_mask) * members + (m ^ mem_mask)))
    return lax.ppermute(value, ("grp", "mem"), pairs)


def live(codes, counts, member, round_no):
    total = jnp.int32(0)
    for slot in range(codes.shape[0]):
        hit = (slot < counts[0, member]) & (codes[slot, 0, member] == round_no)
        total = total + hit.astype(jnp.int32)
    return total


def weights(codes, counts, round_no):
    me = lax.axis_index("mem")
    other = jnp.where(round_no == 0, me, me ^ round_no)
    own = live(codes, counts, me, round_no)
    far = live(codes, counts, other, round_no)
    return own.astype(F32), far.astype(F32)


def nt(a, b):
    return lax.dot_general(a, b, (((1,), (1,)), ((), ())), preferred_element_type=F32)


def nn(a, b):
    return jnp.dot(a, b, preferred_element_type=F32)


def early_kernel(
    splits, b_ref, row_ref, e_ref, first_ref, second_ref, codes, counts,
    one_ref, two_ref, dens_ref, gamma_ref, upper_ref, upper2_ref, amp
):
    vir, aux = b_ref.shape
    for split, ref in zip(splits, (upper_ref, upper2_ref)):
        mask = jnp.where(leads(lax.axis_index("mem")), split[0][0], split[1][0])
        ref[...] = jnp.full(ref.shape, ((lax.axis_index("grp") & mask) != 0).astype(F32))
    row = row_ref[...]
    sums = jnp.broadcast_to(row, (vir, vir)).T + row - e_ref[0]
    one_ref[...] = 1.0 / (sums - first_ref[0])
    two_ref[...] = 1.0 / (sums - second_ref[0])
    own, _ = weights(codes, counts, 0)
    half = vir // 2
    for at in (slice(0, half), slice(half, vir)):
        k = nt(b_ref[...], b_ref[at, :])
        amp[:, at] = (k / (sums[:, at] - e_ref[0])).astype(BF16)
    a = amp[...]
    dens_ref[...] = own * nn(a, a)
    for p in range(STRIPS):
        at = pl.ds(p * (aux // STRIPS), aux // STRIPS)
        gamma_ref[:, at] = (2.0 * own) * nn(a, b_ref[:, at])


def amp_part(at, b_ref, r_ref, over_ref):
    return (nt(b_ref[...], r_ref[...]) * over_ref[:, at]).astype(BF16)


def blocks(size):
    count = size // TILE
    return [(i, j) for i in range(count) for j in range(i, count)]


def density_kernel(b_ref, r_ref, over_ref, codes, counts, dens_in, mt_ref, keep_ref, send_ref, m_ref):
    vir = b_ref.shape[0]
    half = vir // 2
    me = lax.axis_index("mem")
    own, far = weights(codes, counts, first_round(me))
    for at in (slice(0, half), slice(half, vir)):
        mt = amp_part(at, b_ref, r_ref.at[at, :], over_ref)
        mt_ref[:, at] = mt
        m_ref[at, :] = mt.T
    high, low = slice(0, half), slice(half, vir)

    def sums(rows, columns):
        one = nn(mt_ref[rows, :], m_ref[:, columns])
        two = nn(m_ref[rows, :], mt_ref[:, columns])
        return dens_in[rows, columns] + own * one + far * two

    top, rest = sums(high, slice(0, vir)), sums(low, low)
    pieces = []
    for i, j in blocks(vir):
        if i * TILE < half:
            pieces.append(top[i * TILE : (i + 1) * TILE, j * TILE : (j + 1) * TILE])
        else:
            a, b = i * TILE - half, j * TILE - half
            pieces.append(rest[a : a + TILE, b : b + TILE])
    lead = leads(me)
    count = len(pieces) // 2
    for n in range(count):
        at = pl.ds(n * TILE, TILE)
        keep_ref[at, :] = jnp.where(lead, pieces[n], pieces[n + count])
        send_ref[at, :] = jnp.where(lead, pieces[n + count], pieces[n]).astype(BF16)


def first_gamma_kernel(codes, counts, gamma_in, mt_ref, r_ref, gamma_ref):
    own, far = weights(codes, counts, first_round(lax.axis_index("mem")))
    aux = gamma_ref.shape[1]
    for p in range(STRIPS):
        at = pl.ds(p * (aux // STRIPS), aux // STRIPS)
        gamma_ref[:, at] = gamma_in[:, at] + (own + far) * nn(mt_ref[...], r_ref[:, at])


def strips_out(out_ref, held, sems, strips, compute):
    step = held.shape[1] // strips
    copies = []
    for p in range(strips):
        at = pl.ds(p * step, step)
        held[:, at] = compute(at).astype(held.dtype)
        copies.append(pltpu.make_async_copy(held.at[:, at], out_ref.at[:, at], sems.at[p]))
        copies[-1].start()
    for copy in copies:
        copy.wait()


def flat_amp(at, b_ref, r_ref, over_ref, m_ref):
    m_ref[...] = (nt(r_ref[...], b_ref[...]) * over_ref[at, :]).astype(BF16)
    return m_ref[...].T


def second_gamma_kernel(codes, counts, b_ref, over_ref, gamma_in, r_ref, gamma_ref, mt_ref, m_ref):
    own, far = weights(codes, counts, 3 - first_round(lax.axis_index("mem")))
    rows = slice(0, m_ref.shape[0])
    mt_ref[...] = flat_amp(rows, b_ref, r_ref.at[rows, :], over_ref, m_ref)
    aux = gamma_ref.shape[1]
    for p in range(STRIPS):
        at = pl.ds(p * (aux // STRIPS), aux // STRIPS)
        gamma_ref[:, at] = gamma_in[:, at] + (own + far) * nn(mt_ref[...], r_ref[rows, at])


def amp_kernel(b_ref, over_ref, first_ref, last_ref, mt_ref, r_ref, m_ref):
    vir, rows = b_ref.shape[0], r_ref.shape[0]
    left = first_ref.shape[0] - (vir - rows)
    r_ref[:left, :] = first_ref[vir - rows :, :]
    r_ref[left:, :] = last_ref[...]
    mt_ref[...] = flat_amp(slice(vir - rows, vir), b_ref, r_ref, over_ref, m_ref)


def last_gamma_kernel(codes, counts, gamma_in, mt_ref, r_ref, out_ref, held, sems):
    own, far = weights(codes, counts, 3 - first_round(lax.axis_index("mem")))
    strips_out(
        out_ref, held, sems, STRIPS, lambda at: gamma_in[:, at] + (own + far) * nn(mt_ref[...], r_ref[:, at])
    )


def apply_kernel(mine_ref, other_ref, b_ref, out_ref, tile, held, sems):
    lead = leads(lax.axis_index("mem"))
    names = blocks(tile.shape[0])
    half = len(names) // 2
    for n, (i, j) in enumerate(names):
        at = pl.ds((n % half) * TILE, TILE)
        low, high = (mine_ref, other_ref) if n < half else (other_ref, mine_ref)
        block = jnp.where(lead, low[at, :].astype(F32), high[at, :].astype(F32)).astype(BF16)
        tile[pl.ds(i * TILE, TILE), pl.ds(j * TILE, TILE)] = block
        if i != j:
            tile[pl.ds(j * TILE, TILE), pl.ds(i * TILE, TILE)] = block.T
    strips_out(out_ref, held, sems, STRIPS, lambda at: nn(tile[...], b_ref[:, at]))


def call(kernel, outs, scratch=(), smem=(), count=0, flops=0, out_spec=VMEM):
    return lambda *args: kernel_call(kernel, outs, scratch, smem, count, flops, out_spec)(*args)


def kernel_call(kernel, outs, scratch, smem, count, flops, out_spec):
    return pl.pallas_call(
        kernel,
        out_shape=outs,
        in_specs=[SMEM if i in smem else VMEM for i in range(count)],
        out_specs=jax.tree.map(lambda _: out_spec, outs),
        scratch_shapes=scratch,
        compiler_params=pltpu.CompilerParams(vmem_limit_bytes=12 << 20),
        cost_estimate=pl.CostEstimate(flops=flops, bytes_accessed=1 << 20, transcendentals=0),
    )


def per_device(factors, occ_energy, vir_energy, pair_code, pair_count):
    return body(factors[0], occ_energy, vir_energy, pair_code, pair_count)


def body(block, occ_energy, vir_energy, pair_code, pair_count):
    vir, aux = block.shape
    members, groups = lax.axis_size("mem"), lax.axis_size("grp")
    shape = jax.ShapeDtypeStruct
    square = shape((vir, vir), F32)
    wide = shape((vir, aux), F32)
    dot = 2 * vir * vir * aux
    out_scratch = [pltpu.VMEM((vir, aux), BF16), pltpu.SemaphoreType.DMA((STRIPS,))]
    any_space = pl.BlockSpec(memory_space=pl.ANY)

    first_energy = turn(occ_energy, False).astype(F32)
    first = turn(block, False)
    second_energy = turn(occ_energy, True).astype(F32)

    pair_code = jnp.transpose(pair_code, (2, 0, 1))
    energy = occ_energy.astype(F32)
    row = vir_energy.astype(F32).reshape(1, vir)
    half = len(blocks(vir)) * TILE // 2
    along = [(0, 3)] + [(0, (1 << k) | 3) for k in range(2, members.bit_length() - 1)]
    across = [(1 << k, 0) for k in range(groups.bit_length() - 1)]
    splits = list(zip(across, across[1:] + across[:1]))
    splits, later = splits[:2], splits[2:]
    over_first, over_second, dens, gamma, *uppers = call(
        functools.partial(early_kernel, splits),
        (square, square, square, wide, shape((half // 2, TILE), F32), shape((half // 4, TILE), F32)),
        [pltpu.VMEM((vir, vir), BF16)],
        (2, 3, 4, 5, 6), 7, 2 * dot,
    )(block, row, energy, first_energy, second_energy, pair_code, pair_count)

    mt, keep, send = call(
        density_kernel,
        (shape((vir, vir), BF16), shape((half, TILE), F32), shape((half, TILE), BF16)),
        [pltpu.VMEM((vir, vir), BF16)], (3, 4), 6, dot,
    )(block, first, over_first, pair_code, pair_count, dens)

    total = keep + swap(send, [(0, 1), (0, 1)]).astype(F32)
    uppers = [upper > 0.5 for upper in uppers]
    for k, (split, upper) in enumerate(zip(splits, uppers)):
        below, above = total[: half // 2 >> k], total[half // 2 >> k :]
        got = swap(jnp.where(upper, below, above).astype(BF16), split)
        total = jnp.where(upper, above, below) + got.astype(F32)
    for masks in later:
        total = total + swap(total.astype(BF16), masks).astype(F32)
    out = total.astype(BF16)
    near = [m for _, m in along[:2]]
    masks = (near + [near[0] ^ near[1]])[::-1] if len(near) > 1 else near
    masks = sorted(masks, key=lambda m: -(m >> 1))
    for got in [swap(out, [(0, m), (0, m)]) for m in masks]:
        total = total + got.astype(F32)
    for mask in along[2:]:
        total = total + swap(total.astype(BF16), [mask, mask]).astype(F32)
    mine = (total * (1.0 / (8.0 * groups * members))).astype(BF16)
    for k, (split, upper) in reversed(list(enumerate(zip(splits, uppers)))):
        got = swap(mine, split)
        mine = jnp.concatenate([jnp.where(upper, got, mine), jnp.where(upper, mine, got)])
    other = swap(mine, [(0, 1), (0, 1)])

    unit = vir // 16
    cuts = (0, 10 * unit, vir)
    parts = [block[a:b] for a, b in zip(cuts, cuts[1:])]
    second = [turn(part, True) for part in parts]
    gamma = call(first_gamma_kernel, wide, (), (0, 1), 5, dot)(
        pair_code, pair_count, gamma, mt, first
    )
    bounce = [pltpu.VMEM((vir, vir // 2), BF16), pltpu.VMEM((vir // 2, vir), BF16)]
    gamma = call(second_gamma_kernel, wide, bounce, (0, 1), 6, dot)(
        pair_code, pair_count, block, over_second, gamma, second[0]
    )
    rest, rows = call(
        amp_kernel, (shape((vir, vir // 2), BF16), shape((vir // 2, aux), BF16)), bounce[1:], (), 4, dot // 2
    )(block, over_second, *second)
    result = call(last_gamma_kernel, shape((vir, aux), BF16), out_scratch, (0, 1), 5, dot // 2, any_space)(
        pair_code, pair_count, gamma, rest, rows
    )
    lagrangian = call(
        apply_kernel, shape((vir, aux), BF16), [pltpu.VMEM((vir, vir), BF16), *out_scratch], (), 3, dot,
        any_space,
    )(mine, other, block)
    return (result[None], lagrangian[None])


def solution(mesh):
    in_specs = (
        P(("grp", "mem"), None, None),
        P(("grp", "mem")),
        P(),
        P("grp", None, None),
        P("grp", None),
    )
    out_specs = (P(("grp", "mem"), None, None), P(("grp", "mem"), None, None))
    return jax.shard_map(
        per_device, mesh=mesh, in_specs=in_specs, out_specs=out_specs, check_vma=False
    )
```

```python
import functools

import jax
import jax.numpy as jnp
from jax import lax
from jax.experimental import pallas as pl
from jax.experimental.pallas import tpu as pltpu
from jax.sharding import PartitionSpec as P


STRIPS = 4
TILE = 128
F32 = jnp.float32
BF16 = jnp.bfloat16

VMEM = pl.BlockSpec(memory_space=pltpu.VMEM)
SMEM = pl.BlockSpec(memory_space=pltpu.SMEM)


def leads(member):
    return (member & 1) == ((member >> 1) & 1)


def first_round(member):
    return jnp.where(leads(member), 2, 1)


def turn(value, back):
    pairs = []
    for member in range(lax.axis_size("mem")):
        target = member ^ (1 if leads(member) else 2)
        pairs.append((target, member) if back else (member, target))
    return lax.ppermute(value, "mem", pairs)


def swap(value, masks):
    groups, members = lax.axis_size("grp"), lax.axis_size("mem")
    pairs = []
    for g in range(groups):
        for m in range(members):
            grp_mask, mem_mask = masks[0] if leads(m) else masks[1]
            pairs.append((g * members + m, (g ^ grp_mask) * members + (m ^ mem_mask)))
    return lax.ppermute(value, ("grp", "mem"), pairs)


def live(codes, counts, member, round_no):
    total = jnp.int32(0)
    for slot in range(codes.shape[0]):
        hit = (slot < counts[0, member]) & (codes[slot, 0, member] == round_no)
        total = total + hit.astype(jnp.int32)
    return total


def weights(codes, counts, round_no):
    me = lax.axis_index("mem")
    other = jnp.where(round_no == 0, me, me ^ round_no)
    own = live(codes, counts, me, round_no)
    far = live(codes, counts, other, round_no)
    return own.astype(F32), far.astype(F32)


def nt(a, b):
    return lax.dot_general(a, b, (((1,), (1,)), ((), ())), preferred_element_type=F32)


def nn(a, b):
    return jnp.dot(a, b, preferred_element_type=F32)


def early_kernel(
    splits, b_ref, row_ref, e_ref, first_ref, second_ref, codes, counts,
    one_ref, two_ref, dens_ref, gamma_ref, upper_ref, upper2_ref, amp
):
    vir, aux = b_ref.shape
    for split, ref in zip(splits, (upper_ref, upper2_ref)):
        mask = jnp.where(leads(lax.axis_index("mem")), split[0][0], split[1][0])
        ref[...] = jnp.full(ref.shape, ((lax.axis_index("grp") & mask) != 0).astype(F32))
    row = row_ref[...]
    sums = jnp.broadcast_to(row, (vir, vir)).T + row - e_ref[0]
    one_ref[...] = 1.0 / (sums - first_ref[0])
    two_ref[...] = 1.0 / (sums - second_ref[0])
    own, _ = weights(codes, counts, 0)
    half = vir // 2
    for at in (slice(0, half), slice(half, vir)):
        k = nt(b_ref[...], b_ref[at, :])
        amp[:, at] = (k / (sums[:, at] - e_ref[0])).astype(BF16)
    a = amp[...]
    dens_ref[...] = own * nn(a, a)
    for p in range(STRIPS):
        at = pl.ds(p * (aux // STRIPS), aux // STRIPS)
        gamma_ref[:, at] = (2.0 * own) * nn(a, b_ref[:, at])


def amp_part(at, b_ref, r_ref, over_ref):
    return (nt(b_ref[...], r_ref[...]) * over_ref[:, at]).astype(BF16)


def blocks(size):
    count = size // TILE
    return [(i, j) for i in range(count) for j in range(i, count)]


def density_kernel(b_ref, r_ref, over_ref, codes, counts, dens_in, mt_ref, keep_ref, send_ref, m_ref):
    vir = b_ref.shape[0]
    half = vir // 2
    me = lax.axis_index("mem")
    own, far = weights(codes, counts, first_round(me))
    for at in (slice(0, half), slice(half, vir)):
        mt = amp_part(at, b_ref, r_ref.at[at, :], over_ref)
        mt_ref[:, at] = mt
        m_ref[at, :] = mt.T
    high, low = slice(0, half), slice(half, vir)

    def sums(rows, columns):
        one = nn(mt_ref[rows, :], m_ref[:, columns])
        two = nn(m_ref[rows, :], mt_ref[:, columns])
        return dens_in[rows, columns] + own * one + far * two

    top, rest = sums(high, slice(0, vir)), sums(low, low)
    pieces = []
    for i, j in blocks(vir):
        if i * TILE < half:
            pieces.append(top[i * TILE : (i + 1) * TILE, j * TILE : (j + 1) * TILE])
        else:
            a, b = i * TILE - half, j * TILE - half
            pieces.append(rest[a : a + TILE, b : b + TILE])
    lead = leads(me)
    count = len(pieces) // 2
    for n in range(count):
        at = pl.ds(n * TILE, TILE)
        keep_ref[at, :] = jnp.where(lead, pieces[n], pieces[n + count])
        send_ref[at, :] = jnp.where(lead, pieces[n + count], pieces[n]).astype(BF16)


def first_gamma_kernel(codes, counts, gamma_in, mt_ref, r_ref, gamma_ref):
    own, far = weights(codes, counts, first_round(lax.axis_index("mem")))
    aux = gamma_ref.shape[1]
    for p in range(STRIPS):
        at = pl.ds(p * (aux // STRIPS), aux // STRIPS)
        gamma_ref[:, at] = gamma_in[:, at] + (own + far) * nn(mt_ref[...], r_ref[:, at])


def strips_out(out_ref, held, sems, strips, compute):
    step = held.shape[1] // strips
    copies = []
    for p in range(strips):
        at = pl.ds(p * step, step)
        held[:, at] = compute(at).astype(held.dtype)
        copies.append(pltpu.make_async_copy(held.at[:, at], out_ref.at[:, at], sems.at[p]))
        copies[-1].start()
    for copy in copies:
        copy.wait()


def flat_amp(at, b_ref, r_ref, over_ref, m_ref):
    m_ref[...] = (nt(r_ref[...], b_ref[...]) * over_ref[at, :]).astype(BF16)
    return m_ref[...].T


def second_gamma_kernel(codes, counts, b_ref, over_ref, gamma_in, r_ref, gamma_ref, mt_ref, m_ref):
    own, far = weights(codes, counts, 3 - first_round(lax.axis_index("mem")))
    rows = slice(0, m_ref.shape[0])
    mt_ref[...] = flat_amp(rows, b_ref, r_ref.at[rows, :], over_ref, m_ref)
    aux = gamma_ref.shape[1]
    for p in range(STRIPS):
        at = pl.ds(p * (aux // STRIPS), aux // STRIPS)
        gamma_ref[:, at] = gamma_in[:, at] + (own + far) * nn(mt_ref[...], r_ref[rows, at])


def amp_kernel(b_ref, over_ref, first_ref, last_ref, mt_ref, r_ref, m_ref):
    vir, rows = b_ref.shape[0], r_ref.shape[0]
    left = first_ref.shape[0] - (vir - rows)
    r_ref[:left, :] = first_ref[vir - rows :, :]
    r_ref[left:, :] = last_ref[...]
    mt_ref[...] = flat_amp(slice(vir - rows, vir), b_ref, r_ref, over_ref, m_ref)


def half_gamma_kernel(start, codes, counts, gamma_in, mt_ref, r_ref, *refs):
    out_ref, held, sems = refs[-3:]
    own, far = weights(codes, counts, 3 - first_round(lax.axis_index("mem")))
    strips = sems.shape[0]
    width = held.shape[1] // strips
    copies = []
    for p in range(strips):
        here, at = pl.ds(p * width, width), pl.ds(start + p * width, width)
        total = gamma_in[:, at] + (own + far) * nn(mt_ref[...], r_ref[:, at])
        held[:, here] = total.astype(held.dtype)
        copies.append(pltpu.make_async_copy(held.at[:, here], out_ref.at[:, at], sems.at[p]))
        copies[-1].start()
    for copy in copies:
        copy.wait()


def apply_kernel(mine_ref, other_ref, b_ref, out_ref, tile, held, sems):
    lead = leads(lax.axis_index("mem"))
    names = blocks(tile.shape[0])
    half = len(names) // 2
    for n, (i, j) in enumerate(names):
        at = pl.ds((n % half) * TILE, TILE)
        low, high = (mine_ref, other_ref) if n < half else (other_ref, mine_ref)
        block = jnp.where(lead, low[at, :].astype(F32), high[at, :].astype(F32)).astype(BF16)
        tile[pl.ds(i * TILE, TILE), pl.ds(j * TILE, TILE)] = block
        if i != j:
            tile[pl.ds(j * TILE, TILE), pl.ds(i * TILE, TILE)] = block.T
    strips_out(out_ref, held, sems, STRIPS, lambda at: nn(tile[...], b_ref[:, at]))


def call(kernel, outs, scratch=(), smem=(), count=0, flops=0, out_spec=VMEM):
    return lambda *args: kernel_call(kernel, outs, scratch, smem, count, flops, out_spec)(*args)


def kernel_call(kernel, outs, scratch, smem, count, flops, out_spec):
    return pl.pallas_call(
        kernel,
        out_shape=outs,
        in_specs=[SMEM if i in smem else VMEM for i in range(count)],
        out_specs=jax.tree.map(lambda _: out_spec, outs),
        scratch_shapes=scratch,
        compiler_params=pltpu.CompilerParams(vmem_limit_bytes=12 << 20),
        cost_estimate=pl.CostEstimate(flops=flops, bytes_accessed=1 << 20, transcendentals=0),
    )


def per_device(factors, occ_energy, vir_energy, pair_code, pair_count):
    return body(factors[0], occ_energy, vir_energy, pair_code, pair_count)


def body(block, occ_energy, vir_energy, pair_code, pair_count):
    vir, aux = block.shape
    members, groups = lax.axis_size("mem"), lax.axis_size("grp")
    shape = jax.ShapeDtypeStruct
    square = shape((vir, vir), F32)
    wide = shape((vir, aux), F32)
    dot = 2 * vir * vir * aux
    out_scratch = [pltpu.VMEM((vir, aux), BF16), pltpu.SemaphoreType.DMA((STRIPS,))]
    any_space = pl.BlockSpec(memory_space=pl.ANY)

    first_energy = turn(occ_energy, False).astype(F32)
    first = turn(block, False)
    second_energy = turn(occ_energy, True).astype(F32)

    pair_code = jnp.transpose(pair_code, (2, 0, 1))
    energy = occ_energy.astype(F32)
    row = vir_energy.astype(F32).reshape(1, vir)
    half = len(blocks(vir)) * TILE // 2
    along = [(0, 3)] + [(0, (1 << k) | 3) for k in range(2, members.bit_length() - 1)]
    across = [(1 << k, 0) for k in range(groups.bit_length() - 1)]
    splits = list(zip(across, across[1:] + across[:1]))
    splits, later = splits[:2], splits[2:]
    over_first, over_second, dens, gamma, *uppers = call(
        functools.partial(early_kernel, splits),
        (square, square, square, wide, shape((half // 2, TILE), F32), shape((half // 4, TILE), F32)),
        [pltpu.VMEM((vir, vir), BF16)],
        (2, 3, 4, 5, 6), 7, 2 * dot,
    )(block, row, energy, first_energy, second_energy, pair_code, pair_count)

    mt, keep, send = call(
        density_kernel,
        (shape((vir, vir), BF16), shape((half, TILE), F32), shape((half, TILE), BF16)),
        [pltpu.VMEM((vir, vir), BF16)], (3, 4), 6, dot,
    )(block, first, over_first, pair_code, pair_count, dens)

    total = keep + swap(send, [(0, 1), (0, 1)]).astype(F32)
    uppers = [upper > 0.5 for upper in uppers]
    for k, (split, upper) in enumerate(zip(splits, uppers)):
        below, above = total[: half // 2 >> k], total[half // 2 >> k :]
        got = swap(jnp.where(upper, below, above).astype(BF16), split)
        total = jnp.where(upper, above, below) + got.astype(F32)
    for masks in later:
        total = total + swap(total.astype(BF16), masks).astype(F32)
    out = total.astype(BF16)
    near = [m for _, m in along[:2]]
    masks = (near + [near[0] ^ near[1]])[::-1] if len(near) > 1 else near
    masks = sorted(masks, key=lambda m: -(m >> 1))
    for got in [swap(out, [(0, m), (0, m)]) for m in masks]:
        total = total + got.astype(F32)
    for mask in along[2:]:
        total = total + swap(total.astype(BF16), [mask, mask]).astype(F32)
    mine = (total * (1.0 / (8.0 * groups * members))).astype(BF16)
    for k, (split, upper) in reversed(list(enumerate(zip(splits, uppers)))):
        got = swap(mine, split)
        mine = jnp.concatenate([jnp.where(upper, got, mine), jnp.where(upper, mine, got)])
    other = swap(mine, [(0, 1), (0, 1)])

    unit = vir // 16
    cuts = (0, 11 * unit, vir)
    parts = [block[a:b] for a, b in zip(cuts, cuts[1:])]
    second = [turn(part, True) for part in parts]
    gamma = call(first_gamma_kernel, wide, (), (0, 1), 5, dot)(
        pair_code, pair_count, gamma, mt, first
    )
    bounce = [pltpu.VMEM((vir, vir // 2), BF16), pltpu.VMEM((vir // 2, vir), BF16)]
    gamma = call(second_gamma_kernel, wide, bounce, (0, 1), 6, dot)(
        pair_code, pair_count, block, over_second, gamma, second[0]
    )
    rest, rows = call(
        amp_kernel, (shape((vir, vir // 2), BF16), shape((vir // 2, aux), BF16)), bounce[1:], (), 4, dot // 2
    )(block, over_second, *second)
    result = ()
    for part in range(2):
        result = (
            pl.pallas_call(
                functools.partial(half_gamma_kernel, part * (aux // 2)),
                out_shape=shape((vir, aux), BF16),
                in_specs=[SMEM, SMEM, VMEM, VMEM, VMEM] + [any_space] * part,
                out_specs=any_space,
                scratch_shapes=[pltpu.VMEM((vir, aux // 2), BF16), pltpu.SemaphoreType.DMA((2,))],
                input_output_aliases={5: 0} if part else {},
                compiler_params=pltpu.CompilerParams(vmem_limit_bytes=12 << 20),
                cost_estimate=pl.CostEstimate(flops=dot // 4, bytes_accessed=1 << 20, transcendentals=0),
            )(pair_code, pair_count, gamma, rest, rows, *result),
        )
    result = result[0]
    lagrangian = call(
        apply_kernel, shape((vir, aux), BF16), [pltpu.VMEM((vir, vir), BF16), *out_scratch], (), 3, dot,
        any_space,
    )(mine, other, block)
    return (result[None], lagrangian[None])


def solution(mesh):
    in_specs = (
        P(("grp", "mem"), None, None),
        P(("grp", "mem")),
        P(),
        P("grp", None, None),
        P("grp", None),
    )
    out_specs = (P(("grp", "mem"), None, None), P(("grp", "mem"), None, None))
    return jax.shard_map(
        per_device, mesh=mesh, in_specs=in_specs, out_specs=out_specs, check_vma=False
    )
```

```python
import functools

import jax
import jax.numpy as jnp
from jax import lax
from jax.experimental import pallas as pl
from jax.experimental.pallas import tpu as pltpu
from jax.sharding import PartitionSpec as P


STRIPS = 4
TILE = 128
F32 = jnp.float32
BF16 = jnp.bfloat16

VMEM = pl.BlockSpec(memory_space=pltpu.VMEM)
SMEM = pl.BlockSpec(memory_space=pltpu.SMEM)


def leads(member):
    return (member & 1) == ((member >> 1) & 1)


def first_round(member):
    return jnp.where(leads(member), 2, 1)


def turn(value, back):
    pairs = []
    for member in range(lax.axis_size("mem")):
        target = member ^ (1 if leads(member) else 2)
        pairs.append((target, member) if back else (member, target))
    return lax.ppermute(value, "mem", pairs)


def swap(value, masks):
    groups, members = lax.axis_size("grp"), lax.axis_size("mem")
    pairs = []
    for g in range(groups):
        for m in range(members):
            grp_mask, mem_mask = masks[0] if leads(m) else masks[1]
            pairs.append((g * members + m, (g ^ grp_mask) * members + (m ^ mem_mask)))
    return lax.ppermute(value, ("grp", "mem"), pairs)


def live(codes, counts, member, round_no):
    total = jnp.int32(0)
    for slot in range(codes.shape[0]):
        hit = (slot < counts[0, member]) & (codes[slot, 0, member] == round_no)
        total = total + hit.astype(jnp.int32)
    return total


def weights(codes, counts, round_no):
    me = lax.axis_index("mem")
    other = jnp.where(round_no == 0, me, me ^ round_no)
    own = live(codes, counts, me, round_no)
    far = live(codes, counts, other, round_no)
    return own.astype(F32), far.astype(F32)


def nt(a, b):
    return lax.dot_general(a, b, (((1,), (1,)), ((), ())), preferred_element_type=F32)


def nn(a, b):
    return jnp.dot(a, b, preferred_element_type=F32)


def early_kernel(
    splits, b_ref, row_ref, e_ref, first_ref, second_ref, codes, counts,
    one_ref, two_ref, dens_ref, gamma_ref, upper_ref, upper2_ref, amp
):
    vir, aux = b_ref.shape
    for split, ref in zip(splits, (upper_ref, upper2_ref)):
        mask = jnp.where(leads(lax.axis_index("mem")), split[0][0], split[1][0])
        ref[...] = jnp.full(ref.shape, ((lax.axis_index("grp") & mask) != 0).astype(F32))
    row = row_ref[...]
    sums = jnp.broadcast_to(row, (vir, vir)).T + row - e_ref[0]
    one_ref[...] = 1.0 / (sums - first_ref[0])
    two_ref[...] = 1.0 / (sums - second_ref[0])
    own, _ = weights(codes, counts, 0)
    half = vir // 2
    for at in (slice(0, half), slice(half, vir)):
        k = nt(b_ref[...], b_ref[at, :])
        amp[:, at] = (k / (sums[:, at] - e_ref[0])).astype(BF16)
    a = amp[...]
    dens_ref[...] = own * nn(a, a)
    for p in range(STRIPS):
        at = pl.ds(p * (aux // STRIPS), aux // STRIPS)
        gamma_ref[:, at] = (2.0 * own) * nn(a, b_ref[:, at])


def amp_part(at, b_ref, r_ref, over_ref):
    return (nt(b_ref[...], r_ref[...]) * over_ref[:, at]).astype(BF16)


def blocks(size):
    count = size // TILE
    return [(i, j) for i in range(count) for j in range(i, count)]


def density_kernel(b_ref, r_ref, over_ref, codes, counts, dens_in, mt_ref, keep_ref, send_ref, m_ref):
    vir = b_ref.shape[0]
    half = vir // 2
    me = lax.axis_index("mem")
    own, far = weights(codes, counts, first_round(me))
    for at in (slice(0, half), slice(half, vir)):
        mt = amp_part(at, b_ref, r_ref.at[at, :], over_ref)
        mt_ref[:, at] = mt
        m_ref[at, :] = mt.T
    high, low = slice(0, half), slice(half, vir)

    def sums(rows, columns):
        one = nn(mt_ref[rows, :], m_ref[:, columns])
        two = nn(m_ref[rows, :], mt_ref[:, columns])
        return dens_in[rows, columns] + own * one + far * two

    top, rest = sums(high, slice(0, vir)), sums(low, low)
    pieces = []
    for i, j in blocks(vir):
        if i * TILE < half:
            pieces.append(top[i * TILE : (i + 1) * TILE, j * TILE : (j + 1) * TILE])
        else:
            a, b = i * TILE - half, j * TILE - half
            pieces.append(rest[a : a + TILE, b : b + TILE])
    lead = leads(me)
    count = len(pieces) // 2
    for n in range(count):
        at = pl.ds(n * TILE, TILE)
        keep_ref[at, :] = jnp.where(lead, pieces[n], pieces[n + count])
        send_ref[at, :] = jnp.where(lead, pieces[n + count], pieces[n]).astype(BF16)


def first_gamma_kernel(codes, counts, gamma_in, mt_ref, r_ref, gamma_ref):
    own, far = weights(codes, counts, first_round(lax.axis_index("mem")))
    aux = gamma_ref.shape[1]
    for p in range(STRIPS):
        at = pl.ds(p * (aux // STRIPS), aux // STRIPS)
        gamma_ref[:, at] = gamma_in[:, at] + (own + far) * nn(mt_ref[...], r_ref[:, at])


def strips_out(out_ref, held, sems, strips, compute):
    step = held.shape[1] // strips
    copies = []
    for p in range(strips):
        at = pl.ds(p * step, step)
        held[:, at] = compute(at).astype(held.dtype)
        copies.append(pltpu.make_async_copy(held.at[:, at], out_ref.at[:, at], sems.at[p]))
        copies[-1].start()
    for copy in copies:
        copy.wait()


def flat_amp(at, b_ref, r_ref, over_ref, m_ref):
    m_ref[...] = (nt(r_ref[...], b_ref[...]) * over_ref[at, :]).astype(BF16)
    return m_ref[...].T


def second_gamma_kernel(codes, counts, b_ref, over_ref, gamma_in, r_ref, gamma_ref, mt_ref, m_ref):
    own, far = weights(codes, counts, 3 - first_round(lax.axis_index("mem")))
    rows = slice(0, m_ref.shape[0])
    mt_ref[...] = flat_amp(rows, b_ref, r_ref.at[rows, :], over_ref, m_ref)
    aux = gamma_ref.shape[1]
    for p in range(STRIPS):
        at = pl.ds(p * (aux // STRIPS), aux // STRIPS)
        gamma_ref[:, at] = gamma_in[:, at] + (own + far) * nn(mt_ref[...], r_ref[rows, at])


def amp_kernel(b_ref, over_ref, first_ref, last_ref, mt_ref, r_ref, m_ref):
    vir, rows = b_ref.shape[0], r_ref.shape[0]
    left = first_ref.shape[0] - (vir - rows)
    r_ref[:left, :] = first_ref[vir - rows :, :]
    r_ref[left:, :] = last_ref[...]
    mt_ref[...] = flat_amp(slice(vir - rows, vir), b_ref, r_ref, over_ref, m_ref)


def half_gamma_kernel(start, codes, counts, gamma_in, mt_ref, r_ref, *refs):
    out_ref, held, sems = refs[-3:]
    own, far = weights(codes, counts, 3 - first_round(lax.axis_index("mem")))
    strips = sems.shape[0]
    width = held.shape[1] // strips
    copies = []
    for p in range(strips):
        here, at = pl.ds(p * width, width), pl.ds(start + p * width, width)
        total = gamma_in[:, at] + (own + far) * nn(mt_ref[...], r_ref[:, at])
        held[:, here] = total.astype(held.dtype)
        copies.append(pltpu.make_async_copy(held.at[:, here], out_ref.at[:, at], sems.at[p]))
        copies[-1].start()
    for copy in copies:
        copy.wait()


def apply_kernel(mine_ref, other_ref, b_ref, out_ref, tile, held, sems):
    lead = leads(lax.axis_index("mem"))
    names = blocks(tile.shape[0])
    half = len(names) // 2
    for n, (i, j) in enumerate(names):
        at = pl.ds((n % half) * TILE, TILE)
        low, high = (mine_ref, other_ref) if n < half else (other_ref, mine_ref)
        block = jnp.where(lead, low[at, :].astype(F32), high[at, :].astype(F32)).astype(BF16)
        tile[pl.ds(i * TILE, TILE), pl.ds(j * TILE, TILE)] = block
        if i != j:
            tile[pl.ds(j * TILE, TILE), pl.ds(i * TILE, TILE)] = block.T
    strips_out(out_ref, held, sems, STRIPS, lambda at: nn(tile[...], b_ref[:, at]))


def call(kernel, outs, scratch=(), smem=(), count=0, flops=0, out_spec=VMEM):
    return lambda *args: kernel_call(kernel, outs, scratch, smem, count, flops, out_spec)(*args)


def kernel_call(kernel, outs, scratch, smem, count, flops, out_spec):
    return pl.pallas_call(
        kernel,
        out_shape=outs,
        in_specs=[SMEM if i in smem else VMEM for i in range(count)],
        out_specs=jax.tree.map(lambda _: out_spec, outs),
        scratch_shapes=scratch,
        compiler_params=pltpu.CompilerParams(vmem_limit_bytes=12 << 20),
        cost_estimate=pl.CostEstimate(flops=flops, bytes_accessed=1 << 20, transcendentals=0),
    )


def per_device(factors, occ_energy, vir_energy, pair_code, pair_count):
    return body(factors[0], occ_energy, vir_energy, pair_code, pair_count)


def body(block, occ_energy, vir_energy, pair_code, pair_count):
    vir, aux = block.shape
    members, groups = lax.axis_size("mem"), lax.axis_size("grp")
    shape = jax.ShapeDtypeStruct
    square = shape((vir, vir), F32)
    wide = shape((vir, aux), F32)
    dot = 2 * vir * vir * aux
    out_scratch = [pltpu.VMEM((vir, aux), BF16), pltpu.SemaphoreType.DMA((STRIPS,))]
    any_space = pl.BlockSpec(memory_space=pl.ANY)

    first_energy = turn(occ_energy, False).astype(F32)
    first = turn(block, False)
    second_energy = turn(occ_energy, True).astype(F32)

    pair_code = jnp.transpose(pair_code, (2, 0, 1))
    energy = occ_energy.astype(F32)
    row = vir_energy.astype(F32).reshape(1, vir)
    half = len(blocks(vir)) * TILE // 2
    along = [(0, 3)] + [(0, (1 << k) | 3) for k in range(2, members.bit_length() - 1)]
    across = [(1 << k, 0) for k in range(groups.bit_length() - 1)]
    splits = list(zip(across, across[1:] + across[:1]))
    splits, later = splits[:2], splits[2:]
    over_first, over_second, dens, gamma, *uppers = call(
        functools.partial(early_kernel, splits),
        (square, square, square, wide, shape((half // 2, TILE), F32), shape((half // 4, TILE), F32)),
        [pltpu.VMEM((vir, vir), BF16)],
        (2, 3, 4, 5, 6), 7, 2 * dot,
    )(block, row, energy, first_energy, second_energy, pair_code, pair_count)

    mt, keep, send = call(
        density_kernel,
        (shape((vir, vir), BF16), shape((half, TILE), F32), shape((half, TILE), BF16)),
        [pltpu.VMEM((vir, vir), BF16)], (3, 4), 6, dot,
    )(block, first, over_first, pair_code, pair_count, dens)

    total = keep + swap(send, [(0, 1), (0, 1)]).astype(F32)
    uppers = [upper > 0.5 for upper in uppers]
    for k, (split, upper) in enumerate(zip(splits, uppers)):
        below, above = total[: half // 2 >> k], total[half // 2 >> k :]
        got = swap(jnp.where(upper, below, above).astype(BF16), split)
        total = jnp.where(upper, above, below) + got.astype(F32)
    for masks in later:
        total = total + swap(total.astype(BF16), masks).astype(F32)
    out = total.astype(BF16)
    near = [m for _, m in along[:2]]
    masks = (near + [near[0] ^ near[1]])[::-1] if len(near) > 1 else near
    masks = sorted(masks, key=lambda m: -(m >> 1))
    for got in [swap(out, [(0, m), (0, m)]) for m in masks]:
        total = total + got.astype(F32)
    for mask in along[2:]:
        total = total + swap(total.astype(BF16), [mask, mask]).astype(F32)
    mine = (total * (1.0 / (8.0 * groups * members))).astype(BF16)
    for k, (split, upper) in reversed(list(enumerate(zip(splits, uppers)))):
        got = swap(mine, split)
        mine = jnp.concatenate([jnp.where(upper, got, mine), jnp.where(upper, mine, got)])
    other = swap(mine, [(0, 1), (0, 1)])

    unit = vir // 16
    cuts = (0, 11 * unit, vir)
    parts = [block[a:b] for a, b in zip(cuts, cuts[1:])]
    second = [turn(part, True) for part in parts]
    gamma = call(first_gamma_kernel, wide, (), (0, 1), 5, dot)(
        pair_code, pair_count, gamma, mt, first
    )
    bounce = [pltpu.VMEM((vir, vir // 2), BF16), pltpu.VMEM((vir // 2, vir), BF16)]
    gamma = call(second_gamma_kernel, wide, bounce, (0, 1), 6, dot)(
        pair_code, pair_count, block, over_second, gamma, second[0]
    )
    rest, rows = call(
        amp_kernel, (shape((vir, vir // 2), BF16), shape((vir // 2, aux), BF16)), bounce[1:], (), 4, dot // 2
    )(block, over_second, *second)
    result = ()
    quarter = aux // STRIPS
    for part, strips in enumerate((1, STRIPS - 1)):
        result = (
            pl.pallas_call(
                functools.partial(half_gamma_kernel, part * quarter),
                out_shape=shape((vir, aux), BF16),
                in_specs=[SMEM, SMEM, VMEM, VMEM, VMEM] + [any_space] * part,
                out_specs=any_space,
                scratch_shapes=[pltpu.VMEM((vir, strips * quarter), BF16), pltpu.SemaphoreType.DMA((strips,))],
                input_output_aliases={5: 0} if part else {},
                compiler_params=pltpu.CompilerParams(vmem_limit_bytes=12 << 20),
                cost_estimate=pl.CostEstimate(flops=dot // 4, bytes_accessed=1 << 20, transcendentals=0),
            )(pair_code, pair_count, gamma, rest, rows, *result),
        )
    result = result[0]
    lagrangian = call(
        apply_kernel, shape((vir, aux), BF16), [pltpu.VMEM((vir, vir), BF16), *out_scratch], (), 3, dot,
        any_space,
    )(mine, other, block)
    return (result[None], lagrangian[None])


def solution(mesh):
    in_specs = (
        P(("grp", "mem"), None, None),
        P(("grp", "mem")),
        P(),
        P("grp", None, None),
        P("grp", None),
    )
    out_specs = (P(("grp", "mem"), None, None), P(("grp", "mem"), None, None))
    return jax.shard_map(
        per_device, mesh=mesh, in_specs=in_specs, out_specs=out_specs, check_vma=False
    )
```
